32 devices in a mesh: dp: 4 (over y, core), ctx: 8 (over z, x).
Axes of the slice: x: 2, y: 2, z: 4, core: 2. Of those that a mesh axis runs over, the one named last changes fastest.
Arguments:
- layer_input: bfloat16 [8192, 1024], P(('dp', 'ctx')), may hold values from -6 to 6
- query_weight: bfloat16 [1024, 1024], P('dp'), may hold values from -0.75 to 0.75
- key_weight: bfloat16 [1024, 512], P('dp'), may hold values from -0.75 to 0.75
- value_weight: bfloat16 [1024, 512], P('dp'), may hold values from -0.1875 to 0.1875
- out_weight: bfloat16 [1024, 1024], P('dp'), may hold values from -1.5 to 1.5
- attn_gain: bfloat16 [1024], P('dp'), may hold values from 0.5 to 1.5
- router_weight: bfloat16 [1024, 32], P('dp'), may hold values from -0.08984375 to 0.08984375
- moe_gain: bfloat16 [1024], P('dp'), may hold values from 0.5 to 1.5
- gate_weight: bfloat16 [32, 1024, 512], P('dp'), may hold values from -0.1875 to 0.1875
- up_weight: bfloat16 [32, 1024, 512], P('dp'), may hold values from -0.1875 to 0.1875
- down_weight: bfloat16 [32, 512, 1024], P('dp'), may hold values from -0.75 to 0.75
- expert_ids: int32 [8192, 8], P(('dp', 'ctx')), may hold values from 0 to 31, all different within a row
- fill_order: int32 [32, 256], P(('dp', 'ctx')), may hold values from 0 to 255, each once within a row
- block_deal: int32 [4, 16], P('dp'), may hold values from 0 to 15, each once within a row
- seq_lengths: int32 [4, 4], P('dp'), may hold values from 1 to 1024, 2048 in all within a row
- out_grad: float32 [8192, 1024], P(('dp', 'ctx')), may hold values from -6 to 6
Outputs:
- layer_output: float32 [8192, 1024], P(('dp', 'ctx'))
- input_grad: float32 [8192, 1024], P(('dp', 'ctx'))
- query_grad: float32 [1024, 1024], P('dp')
- key_grad: float32 [1024, 512], P('dp')
- value_grad: float32 [1024, 512], P('dp')
- outproj_grad: float32 [1024, 1024], P('dp')
- attn_gain_grad: float32 [1024], P('dp')
- router_grad: float32 [1024, 32], P('dp')
- moe_gain_grad: float32 [1024], P('dp')
- gate_grad: float32 [32, 1024, 512], P('dp')
- up_grad: float32 [32, 1024, 512], P('dp')
- down_grad: float32 [32, 512, 1024], P('dp')
The draws below stay inside these ranges and needn't reach their ends.
Inputs may be any that keep to these rules, and one draw needn't show every extreme that they name: `expert_ids`: each row names 8 different experts, and every expert is named. `fill_order`: each row is a permutation. `block_deal`: each row is a permutation. `seq_lengths`: each row sums to 2048, and its largest length is 1024.
All inputs are finite; a program needn't handle non-finite values.
Results may differ from the reference program's by a relative error of at most 0.023.
Values may be sent and summed in bfloat16 or wider, within the bound.
No kernel may reach another device: no remote copies, remote signals or barrier semaphores. Data moves between devices by JAX's collectives and lax.ppermute only.
A program may use at most 192 MiB of HBM per device.

```python
import math
import jax
import jax.numpy as jnp
import numpy as np
from jax import lax

D = 1024
QUERY_HEADS = 16
KEY_VALUE_HEADS = 8
HEAD_SIZE = 64
EXPERTS = 32
FFE = 512
TOP = 8
TOK_DEV = 256
BLOCK = 128
NSEQ = 4
GROUP_TOKENS = 2048
TOKENS_TOTAL = 8192
NDEV = 32
SEQ_MAX = 1024
NBLK = 16
CAP = 64
QD = 1024
KVD = 512
N_DP = 4


def level_of(own_key, extent, pieces, low, top_value):
    def one(position, shards_of):
        steps = jax.random.uniform(jax.random.fold_in(jax.random.fold_in(own_key, 6), position), (shards_of,), jnp.float32, low / len(pieces), top_value / len(pieces))
        return jnp.repeat(jnp.exp(steps), extent[position] // shards_of).reshape((-1,) + (1,) * (len(extent) - position - 1))

    level = one(*pieces[0])
    for cut in pieces[1:]:
        level = level * one(*cut)
    return level


def distinct(own_key, rows, count, top, lift):
    sequence = jax.random.permutation(jax.random.fold_in(own_key, 1), count)
    favour = sequence
    for power in range(3):
        favour = favour * favour // count
    favour = favour * lift // count
    tickets = jax.random.randint(jax.random.fold_in(own_key, 2), (rows, count), 0, 4096) + favour
    fixed_rows = jax.random.permutation(jax.random.fold_in(own_key, 3), rows)[jnp.arange(count) % rows]
    tickets = jnp.where(jnp.arange(rows)[:, None] == fixed_rows[None, :], 1 << 14, tickets)
    priority = tickets * count + jnp.arange(count)
    return lax.top_k(priority.astype(jnp.int32), top)[1].astype(jnp.int32)


def split_up(amount, total, most, skew):
    weights = [(1 << 20) // math.isqrt(rank ** skew) + 1 for rank in range(2, amount + 1)]
    surplus, counts = total - most - (amount - 1), [1] * (amount - 1)
    while surplus > 0:
        movable = [i for i in range(amount - 1) if counts[i] < most]
        whole, remaining = sum([weights[i] for i in movable]), surplus
        for i in movable:
            more = min(most - counts[i], max(1, remaining * weights[i] // whole), surplus)
            counts[i] = counts[i] + more
            surplus = surplus - more
    return np.array([most] + counts)


def ragged(key, number_of, total, most, lean):
    if number_of == 2:
        one = jax.random.randint(key, (), max(1, total - most), min(most, total - 1) + 1)
        return jnp.stack([one, total - one])
    tallies = jnp.asarray(split_up(number_of, total, most, lean), jnp.int32)
    twos = (number_of - 1) // 2
    source_of, sink = tallies[1:1 + 2 * twos:2], tallies[2:2 + 2 * twos:2]
    margin = jnp.minimum(source_of - 1, most - sink)
    shifted = jax.random.randint(jax.random.fold_in(key, 1), (twos,), 0, 1 << 20) % (margin + 1)
    tallies = tallies.at[1:1 + 2 * twos:2].set(source_of - shifted).at[2:2 + 2 * twos:2].set(sink + shifted)
    return tallies[jax.random.permutation(jax.random.fold_in(key, 2), number_of)]


def normal_values(own_key, dims, spread, most, shards=(), kind=jnp.bfloat16):
    factor_of = level_of(own_key, dims, shards, -0.22, 0.18) if shards else 1.0
    values = jax.random.normal(own_key, dims, jnp.float32) * spread * factor_of
    return jnp.minimum(jnp.maximum(values, -most), most).astype(kind)


def setup_inputs(seed: int = 0) -> dict:
    streams_of = jax.random.split(jax.random.key(seed), 17)
    layer_input = normal_values(streams_of[0], (TOKENS_TOTAL, D), 1.0, 6.0, ((0, 32),))
    query_weight = normal_values(streams_of[1], (D, QD), (D // 16) ** -0.5, 0.75, ((0, 4),))
    key_weight = normal_values(streams_of[2], (D, KVD), (D // 16) ** -0.5, 0.75, ((0, 4),))
    value_weight = normal_values(streams_of[3], (D, KVD), D ** -0.5, 0.1875, ((0, 4),))
    out_weight = normal_values(streams_of[4], (QD, D), (QD // 64) ** -0.5, 1.5, ((0, 4),))
    attn_gain = jnp.clip(1.0 + 0.1 * jax.random.normal(streams_of[5], (D,), jnp.float32), 0.5, 1.5).astype(jnp.bfloat16)
    router_weight = normal_values(streams_of[6], (D, EXPERTS), 0.015625, 0.08984375, ((0, 4),))
    moe_gain = jnp.clip(1.0 + 0.1 * jax.random.normal(streams_of[7], (D,), jnp.float32), 0.5, 1.5).astype(jnp.bfloat16)
    gate_weight = normal_values(streams_of[8], (EXPERTS, D, FFE), D ** -0.5, 0.1875, ((0, 4),))
    up_weight = normal_values(streams_of[9], (EXPERTS, D, FFE), D ** -0.5, 0.1875, ((0, 4),))
    down_weight = normal_values(streams_of[10], (EXPERTS, FFE, D), (FFE // 8) ** -0.5, 0.75, ((0, 4),))
    expert_ids = distinct(streams_of[11], TOKENS_TOTAL, EXPERTS, TOP, 2048)
    fill_order = jax.vmap(lambda own: jax.random.permutation(own, TOK_DEV))(jax.random.split(streams_of[12], NDEV)).reshape((NDEV, TOK_DEV)).astype(jnp.int32)
    block_deal = jax.vmap(lambda own: jax.random.permutation(own, NBLK))(jax.random.split(streams_of[13], N_DP)).reshape((N_DP, NBLK)).astype(jnp.int32)
    seq_lengths = jax.vmap(lambda own: ragged(own, NSEQ, GROUP_TOKENS, SEQ_MAX, 2))(jax.random.split(streams_of[14], N_DP)).reshape((N_DP, NSEQ)).astype(jnp.int32)
    out_grad = normal_values(streams_of[15], (TOKENS_TOTAL, D), 1.0, 6.0, ((0, 32),), jnp.float32)
    return {"layer_input": layer_input, "query_weight": query_weight, "key_weight": key_weight, "value_weight": value_weight, "out_weight": out_weight, "attn_gain": attn_gain, "router_weight": router_weight, "moe_gain": moe_gain, "gate_weight": gate_weight, "up_weight": up_weight, "down_weight": down_weight, "expert_ids": expert_ids, "fill_order": fill_order, "block_deal": block_deal, "seq_lengths": seq_lengths, "out_grad": out_grad}


EPS = 1e-06
NEGATIVE_FILL = -1e+30
HIGH_PRECISION = lax.Precision.HIGHEST

@jax.custom_vjp
def low(v):
    return lax.optimization_barrier(v.astype(jnp.bfloat16)).astype(jnp.float32)

@jax.custom_vjp
def lowered_backward(v):
    return v

def low_keep(v):
    return (low(v), None)

def low_pass(kept, grad):
    return (grad,)

def back_keep(v):
    return (v, None)

def back_low(kept, grad):
    return (low(grad),)
low.defvjp(low_keep, low_pass)
lowered_backward.defvjp(back_keep, back_low)

def group_positions(block_order, seq_lens):
    token_places = (block_order[:, None] * BLOCK + jnp.arange(BLOCK, dtype=jnp.int32)[None, :]).reshape(-1)
    seq_ends = jnp.cumsum(seq_lens, dtype=jnp.int32)
    passed = (token_places[:, None] >= seq_ends[None, :]).astype(jnp.int32)
    sequence_starts = lax.optimization_barrier(jnp.sum(seq_lens[None, :] * passed, axis=1, dtype=jnp.int32))
    return (token_places, sequence_starts)

def rope_tables(relative):
    half_width = HEAD_SIZE // 2
    inverse = 10000.0 ** (-jnp.arange(half_width, dtype=jnp.float32) * (2.0 / HEAD_SIZE))
    angles = relative[:, None] * inverse[None, :]
    return (jnp.cos(angles)[:, None, :], jnp.sin(angles)[:, None, :])

def rotary_turn(values, cosine_table, sine_table):
    half_width = values.shape[-1] // 2
    first_half = values[..., :half_width]
    second_half = values[..., half_width:]
    return jnp.concatenate([first_half * cosine_table - second_half * sine_table, second_half * cosine_table + first_half * sine_table], axis=-1)

def slot_tables(chosen, order_rank):
    tok_count = chosen.shape[0]
    picks = chosen.shape[1]
    choice_hits = (chosen[:, :, None] == jnp.arange(EXPERTS, dtype=jnp.int32)[None, None, :]).astype(jnp.int32)
    per_token = lax.optimization_barrier(jnp.sum(choice_hits, axis=1, dtype=jnp.int32))
    inverse_order = jnp.zeros((tok_count,), jnp.int32).at[order_rank].set(jnp.arange(tok_count, dtype=jnp.int32))
    ordered = per_token[inverse_order]
    before = (jnp.cumsum(ordered, axis=0, dtype=jnp.int32) - ordered).astype(jnp.int32)
    prior = before[order_rank]
    slot_index = lax.optimization_barrier(jnp.sum(choice_hits * prior[:, None, :], axis=2, dtype=jnp.int32))
    kept_pairs = slot_index < CAP
    flat_pair = chosen * CAP + jnp.minimum(slot_index, CAP - 1)
    target = jnp.where(kept_pairs, chosen * CAP + slot_index, EXPERTS * CAP).reshape(-1)
    token_ids = jnp.broadcast_to(jnp.arange(tok_count, dtype=jnp.int32)[:, None], (tok_count, picks)).reshape(-1)
    pick_ids = jnp.broadcast_to(jnp.arange(picks, dtype=jnp.int32)[None, :], (tok_count, picks)).reshape(-1)
    slot_token = jnp.zeros((EXPERTS * CAP + 1,), jnp.int32).at[target].set(token_ids)[:EXPERTS * CAP]
    slot_pick = jnp.zeros((EXPERTS * CAP + 1,), jnp.int32).at[target].set(pick_ids)[:EXPERTS * CAP]
    slot_live = jnp.zeros((EXPERTS * CAP + 1,), jnp.int32).at[target].set(jnp.ones_like(token_ids))[:EXPERTS * CAP]
    return (choice_hits, kept_pairs, flat_pair, slot_token, slot_pick, slot_live)

def grouped_attention(query_entries, key_entries, values, token_places, sequence_starts):
    group_rows = query_entries.shape[0]
    block_rows = min(512, group_rows)
    block_count = group_rows // block_rows

    def one_block(split_parts):
        query_block, query_places, query_starts = split_parts
        raw_scores = jnp.einsum('qgrd,kgd->grqk', query_block, key_entries, precision=HIGH_PRECISION) * (1.0 / HEAD_SIZE)
        scores = lowered_backward(raw_scores)
        allowed = (token_places[None, :] <= query_places[:, None]) & (token_places[None, :] >= query_starts[:, None])
        scores = jnp.where(allowed[None, None], scores, NEGATIVE_FILL)
        weights = low(jax.nn.softmax(scores, axis=-1))
        return jnp.einsum('grqk,kgd->qgrd', weights, values, precision=HIGH_PRECISION)
    result = lax.map(jax.checkpoint(one_block), (query_entries.reshape((block_count, block_rows) + query_entries.shape[1:]), token_places.reshape(block_count, block_rows), sequence_starts.reshape(block_count, block_rows)))
    return result.reshape(group_rows, QD)

def reference(layer_input, query_weight, key_weight, value_weight, out_weight, attn_gain, router_weight, moe_gain, gate_weight, up_weight, down_weight, expert_ids, fill_order, block_deal, seq_lengths, out_grad):
    token_places, sequence_starts = jax.vmap(group_positions)(block_deal, seq_lengths)
    places_flat = token_places.reshape(TOKENS_TOTAL)
    starts_flat = sequence_starts.reshape(TOKENS_TOTAL)
    cosine_table, sine_table = rope_tables((places_flat - starts_flat).astype(jnp.float32))
    tables = jax.vmap(slot_tables)(expert_ids.reshape(NDEV, TOK_DEV, TOP), fill_order)
    kept_pairs, flat_pair, slot_token, slot_live = (tables[1], tables[2], tables[3], tables[5])
    kept_float = kept_pairs.astype(jnp.float32)
    rotation_ratio = QUERY_HEADS // KEY_VALUE_HEADS

    def forward(input_rows, query_mat, key_matrix, value_mat, out_mat, gain_attn, router_mat, gain_moe, gate_mat, up_mat, down_mat):
        scale_one = lax.rsqrt(lax.optimization_barrier(jnp.mean(input_rows * input_rows, axis=-1, keepdims=True)) + EPS)
        first_normed = low(input_rows * scale_one * gain_attn)
        queries_raw = lowered_backward(jnp.dot(first_normed, query_mat, precision=HIGH_PRECISION)).reshape(TOKENS_TOTAL, QUERY_HEADS, HEAD_SIZE)
        unrotated_keys = lowered_backward(jnp.dot(first_normed, key_matrix, precision=HIGH_PRECISION)).reshape(TOKENS_TOTAL, KEY_VALUE_HEADS, HEAD_SIZE)
        every_value = low(lowered_backward(jnp.dot(first_normed, value_mat, precision=HIGH_PRECISION)))
        query_entries = low(rotary_turn(queries_raw, cosine_table, sine_table))
        key_entries = low(rotary_turn(unrotated_keys, cosine_table, sine_table))
        attended_rows = lax.map(lambda split_parts: grouped_attention(*split_parts), (query_entries.reshape(N_DP, GROUP_TOKENS, KEY_VALUE_HEADS, rotation_ratio, HEAD_SIZE), key_entries.reshape(N_DP, GROUP_TOKENS, KEY_VALUE_HEADS, HEAD_SIZE), every_value.reshape(N_DP, GROUP_TOKENS, KEY_VALUE_HEADS, HEAD_SIZE), token_places, sequence_starts))
        attended_rows = lowered_backward(low(attended_rows.reshape(TOKENS_TOTAL, QD)))
        mixed = input_rows + lowered_backward(jnp.dot(attended_rows, out_mat, precision=HIGH_PRECISION))
        scale_two = lax.rsqrt(lax.optimization_barrier(jnp.mean(mixed * mixed, axis=-1, keepdims=True)) + EPS)
        normed_two = low(mixed * scale_two * gain_moe)
        logits = lowered_backward(jnp.dot(normed_two, router_mat, precision=HIGH_PRECISION))
        chosen = jnp.take_along_axis(logits, expert_ids, axis=1)
        gates = jax.nn.softmax(chosen, axis=-1)

        def device_moe(split_parts):
            row_data, gate_rows, token_index, live_index, pair_index, kept_rows = split_parts
            sent = lowered_backward(jnp.where(live_index[:, None] > 0, row_data[token_index], 0.0)).reshape(EXPERTS, CAP, D)
            gate_part = lowered_backward(jnp.einsum('erd,edf->erf', sent, gate_mat, precision=HIGH_PRECISION))
            up_part = lowered_backward(jnp.einsum('erd,edf->erf', sent, up_mat, precision=HIGH_PRECISION))
            hidden = low(jax.nn.silu(gate_part) * up_part)
            expert_out = lowered_backward(low(jnp.einsum('erf,efd->erd', hidden, down_mat, precision=HIGH_PRECISION))).reshape(EXPERTS * CAP, D)
            pairs = expert_out[pair_index]
            return jnp.einsum('tk,tkd->td', gate_rows * kept_rows, pairs, precision=HIGH_PRECISION)
        moe_out = lax.map(jax.checkpoint(device_moe), (normed_two.reshape(NDEV, TOK_DEV, D), gates.reshape(NDEV, TOK_DEV, TOP), slot_token, slot_live, flat_pair, kept_float))
        return mixed + moe_out.reshape(TOKENS_TOTAL, D)
    floats = (layer_input.astype(jnp.float32), query_weight.astype(jnp.float32), key_weight.astype(jnp.float32), value_weight.astype(jnp.float32), out_weight.astype(jnp.float32), attn_gain.astype(jnp.float32), router_weight.astype(jnp.float32), moe_gain.astype(jnp.float32), gate_weight.astype(jnp.float32), up_weight.astype(jnp.float32), down_weight.astype(jnp.float32))
    layer_output, pull_back = jax.vjp(forward, *floats)
    grads = pull_back(out_grad)
    return (layer_output, grads[0], grads[1], grads[2], grads[3], grads[4], grads[5], grads[6], grads[7], grads[8], grads[9], grads[10])
```

```python
import jax
import jax.numpy as jnp
from jax import lax
from jax.experimental import pallas as pl
from jax.experimental.pallas import tpu as pltpu
from jax.sharding import PartitionSpec as P

EXPERTS = 32
BLOCK = 128
CAP = 64
HEAD = 64
KVD = 512
PAIRS = 4
EPS = 1e-06
NEG = -1e30
F32 = jnp.float32
BF16 = jnp.bfloat16


def dot_nn(a, b):
    return lax.dot_general(a, b, (((1,), (0,)), ((), ())), preferred_element_type=F32)


def dot_nt(a, b):
    return lax.dot_general(a, b, (((1,), (1,)), ((), ())), preferred_element_type=F32)


def dot_tn(a, b):
    return lax.dot_general(a, b, (((0,), (0,)), ((), ())), preferred_element_type=F32)


def vmem():
    return pl.BlockSpec(memory_space=pltpu.VMEM)


def smem():
    return pl.BlockSpec(memory_space=pltpu.SMEM)


def call(body, scalars, arrays, outs, scratch=(), mib=48):
    return pl.pallas_call(
        body,
        in_specs=[smem() for _ in scalars] + [vmem() for _ in arrays],
        out_specs=[vmem() for _ in outs],
        out_shape=[jax.ShapeDtypeStruct(s, d) for s, d in outs],
        scratch_shapes=list(scratch),
        compiler_params=pltpu.CompilerParams(vmem_limit_bytes=mib << 20),
    )(*scalars, *arrays)


def xor_pairs(count, step):
    return [(i, i ^ step) for i in range(count)]


def dp_gather(block, count):
    pieces = {0: block}
    for step in range(2, count, 2):
        pieces[step] = lax.ppermute(block, "dp", xor_pairs(count, step))
    for step in range(0, count, 2):
        pieces[step + 1] = lax.ppermute(pieces[step], "dp", xor_pairs(count, 1))
    return [pieces[s] for s in range(count)]


def dp_reduce(pieces, count):
    kept = {}
    for step in range(0, count, 2):
        other = lax.ppermute(pieces[step + 1], "dp", xor_pairs(count, 1))
        kept[step] = pieces[step].astype(F32) + other.astype(F32)
    total = kept[0]
    for step in range(2, count, 2):
        other = lax.ppermute(kept[step].astype(BF16), "dp", xor_pairs(count, step))
        total = total + other.astype(F32)
    return total


def in_order(pieces, index):
    stacked = jnp.stack(pieces)
    count = len(pieces)
    bit = 1
    while bit < count:
        swapped = jnp.stack([stacked[j ^ bit] for j in range(count)])
        stacked = jnp.where((index & bit) > 0, swapped, stacked)
        bit *= 2
    return stacked


def ring_order(count):
    return [list(range(0, count, 2)) + list(range(count - 1, 0, -2))]


def ring_gather(block, count):
    return lax.all_gather(block, "ctx", axis=0, tiled=True, axis_index_groups=ring_order(count))


def ring_scatter(block, count):
    return lax.psum_scatter(
        block, "ctx", scatter_dimension=0, tiled=True, axis_index_groups=ring_order(count)
    )


def half_swap(tile, first):
    return jnp.where(first, pltpu.roll(tile, 96, 1), pltpu.roll(tile, 32, 1))


def turn(tile, cosine, sine, first):
    return tile * cosine + half_swap(tile, first) * sine


def turn_back(tile, cosine, sine, first):
    return tile * cosine - half_swap(tile, first) * sine


def lanes_of(rows):
    return lax.broadcasted_iota(jnp.int32, (rows, 128), 1)


def spread_heads(tile_a, tile_b):
    low = lanes_of(tile_a.shape[0]) < HEAD
    return jnp.concatenate(
        [
            jnp.where(low, tile_a, 0.0),
            jnp.where(low, pltpu.roll(tile_a, HEAD, 1), 0.0),
            jnp.where(low, 0.0, pltpu.roll(tile_b, HEAD, 1)),
            jnp.where(low, 0.0, tile_b),
        ],
        axis=0,
    )


def join_heads(stacked):
    rows = stacked.shape[0] // 4
    low = lanes_of(rows) < HEAD
    part = [stacked[h * rows : (h + 1) * rows] for h in range(4)]
    return (
        jnp.where(low, part[0], pltpu.roll(part[1], HEAD, 1)),
        jnp.where(low, pltpu.roll(part[2], HEAD, 1), part[3]),
    )


def norm_back(grad, normed, inverse, gain):
    scaled = grad * gain
    return inverse * (scaled - normed * jnp.mean(scaled * normed, axis=-1, keepdims=True))


def kv_body(count):
    def body(me_ref, x_ref, gain_ref, cos_ref, sin_ref, *rest):
        weights, (kv_ref, act_ref) = rest[:count], rest[count:]
        x = x_ref[...].astype(F32)
        inverse = lax.rsqrt(jnp.mean(x * x, axis=-1, keepdims=True) + EPS)
        act = (x * inverse * gain_ref[...]).astype(BF16)
        width = x.shape[1] // count
        for b in range(count):
            act_ref[b] = act[:, b * width : (b + 1) * width]
        me = me_ref[0]
        total = dot_nn(act_ref[me], weights[0][...])
        for s in range(1, count):
            total = total + dot_nn(act_ref[me ^ s], weights[s][...])
        first = (lanes_of(x.shape[0]) & 63) < 32
        cosine, sine = cos_ref[...], sin_ref[...]
        for j in range(KVD // 128):
            tile = total[:, j * 128 : (j + 1) * 128]
            kv_ref[:, j * 128 : (j + 1) * 128] = turn(tile, cosine, sine, first).astype(BF16)
        kv_ref[:, KVD:] = total[:, KVD:].astype(BF16)

    return body


def query_body(count):
    def body(me_ref, act_ref, cos_ref, sin_ref, *rest):
        weights, q_ref = rest[:count], rest[count]
        me = me_ref[0]
        total = dot_nn(act_ref[me], weights[0][...])
        for s in range(1, count):
            total = total + dot_nn(act_ref[me ^ s], weights[s][...])
        first = (lanes_of(total.shape[0]) & 63) < 32
        cosine, sine = cos_ref[...], sin_ref[...]
        for j in range(total.shape[1] // 128):
            tile = total[:, j * 128 : (j + 1) * 128]
            turned = turn(tile, cosine, sine, first).astype(BF16)
            q_ref[:, j * 128 : (j + 1) * 128] = turned * (1.0 / HEAD)

    return body


def visible(place_block, key_block, starts):
    rows = lax.broadcasted_iota(jnp.int32, (BLOCK, BLOCK), 0) + place_block * BLOCK
    keys = lax.broadcasted_iota(jnp.int32, (BLOCK, BLOCK), 1) + key_block * BLOCK
    return (keys <= rows) & (keys >= starts)


def attend_body(low_ref, high_ref, where_ref, q_ref, kv_ref, starts_ref, o_ref, ext_ref, qs, ms, ls, accs):
    low_half = lanes_of(BLOCK) < HEAD
    for qb in range(q_ref.shape[0] // BLOCK):
        rows = slice(qb * BLOCK, (qb + 1) * BLOCK)
        for j in range(PAIRS):
            qs[j] = spread_heads(
                q_ref[rows, 256 * j : 256 * j + 128].astype(F32),
                q_ref[rows, 256 * j + 128 : 256 * j + 256].astype(F32),
            ).astype(BF16)
        ms[...] = jnp.full(ms.shape, NEG, F32)
        ls[...] = jnp.zeros(ls.shape, F32)
        accs[...] = jnp.zeros(accs.shape, F32)
        high = high_ref[qb]

        def step(b, carry):
            at = pl.multiple_of(where_ref[b] * BLOCK, BLOCK)
            seen = visible(high, b, starts_ref[rows, :])[None]
            for j in range(PAIRS):
                key = kv_ref[pl.ds(at, BLOCK), 128 * j : 128 * j + 128]
                value = kv_ref[pl.ds(at, BLOCK), KVD + 128 * j : KVD + 128 * j + 128]
                scores = dot_nt(qs[j], key).reshape(4, BLOCK, BLOCK)
                scores = jnp.where(seen, scores, NEG).reshape(4 * BLOCK, BLOCK)
                old = ms[j]
                new = jnp.maximum(old, jnp.max(scores, axis=-1, keepdims=True))
                weights = jnp.exp(scores - new)
                shrink = jnp.exp(old - new)
                ls[j] = ls[j] * shrink + jnp.sum(weights, axis=-1, keepdims=True)
                accs[j] = accs[j] * shrink + dot_nn(weights.astype(BF16), value)
                ms[j] = new
            return carry

        lax.fori_loop(low_ref[qb], high + 1, step, 0)
        for j in range(PAIRS):
            attended = accs[j] / ls[j]
            total = ms[j] + jnp.log(ls[j])
            left, right = join_heads(attended)
            o_ref[rows, 256 * j : 256 * j + 128] = left.astype(BF16)
            o_ref[rows, 256 * j + 128 : 256 * j + 256] = right.astype(BF16)
            for h in range(4):
                part = slice(h * BLOCK, (h + 1) * BLOCK)
                keep = low_half if h < 2 else jnp.logical_not(low_half)
                ext_ref[j, h, rows, :] = jnp.where(keep, attended[part], total[part])


def attend_back_body(
    low_ref, high_ref, where_ref, q_ref, kv_ref, starts_ref, go_ref, ext_ref, cos_ref, sin_ref,
    gq_ref, dkv_ref, qs, gs, ds, lse, dqs, sums,
):
    first = (lanes_of(BLOCK) & 63) < 32
    sums[...] = jnp.zeros(sums.shape, F32)
    for qb in range(q_ref.shape[0] // BLOCK):
        rows = slice(qb * BLOCK, (qb + 1) * BLOCK)
        for j in range(PAIRS):
            cols = slice(256 * j, 256 * j + 128), slice(256 * j + 128, 256 * j + 256)
            qs[j] = spread_heads(
                q_ref[rows, cols[0]].astype(F32), q_ref[rows, cols[1]].astype(F32)
            ).astype(BF16)
            grad = spread_heads(
                go_ref[rows, cols[0]].astype(F32), go_ref[rows, cols[1]].astype(F32)
            )
            gs[j] = grad.astype(BF16)
            for h in range(4):
                part = slice(h * BLOCK, (h + 1) * BLOCK)
                ext = ext_ref[j, h, rows, :]
                ds[j, part, :] = jnp.sum(grad[part] * ext, axis=-1, keepdims=True)
                lse[j, part, :] = ext[:, 127:128] if h < 2 else ext[:, 0:1]
        dqs[...] = jnp.zeros(dqs.shape, F32)
        high = high_ref[qb]

        def step(b, carry):
            at = pl.multiple_of(where_ref[b] * BLOCK, BLOCK)
            seen = visible(high, b, starts_ref[rows, :])[None]
            for j in range(PAIRS):
                kcols = slice(128 * j, 128 * j + 128)
                vcols = slice(KVD + 128 * j, KVD + 128 * j + 128)
                key = kv_ref[pl.ds(at, BLOCK), kcols]
                value = kv_ref[pl.ds(at, BLOCK), vcols]
                scores = dot_nt(qs[j], key).reshape(4, BLOCK, BLOCK)
                scores = jnp.where(seen, scores, NEG).reshape(4 * BLOCK, BLOCK)
                weights = jnp.exp(scores - lse[j])
                grad = dot_nt(gs[j], value)
                score_grad = (weights * (grad - ds[j])).astype(BF16)
                dqs[j] += dot_nn(score_grad, key)
                sums[pl.ds(at, BLOCK), kcols] += dot_tn(score_grad, qs[j])
                sums[pl.ds(at, BLOCK), vcols] += dot_tn(weights.astype(BF16), gs[j])
            return carry

        lax.fori_loop(low_ref[qb], high + 1, step, 0)
        cosine, sine = cos_ref[rows, :], sin_ref[rows, :]
        for j in range(PAIRS):
            left, right = join_heads(dqs[j] * (1.0 / HEAD))
            gq_ref[rows, 256 * j : 256 * j + 128] = turn_back(left, cosine, sine, first).astype(BF16)
            gq_ref[rows, 256 * j + 128 : 256 * j + 256] = turn_back(right, cosine, sine, first).astype(
                BF16
            )
    dkv_ref[...] = sums[...].astype(BF16)


def mix_body(count):
    def body(me_ref, x_ref, o_ref, gain_ref, *rest):
        weights, (mixed_ref, act_ref, parts) = rest[:count], rest[count:]
        width = o_ref.shape[1] // count
        for b in range(count):
            parts[b] = o_ref[:, b * width : (b + 1) * width]
        me = me_ref[0]
        total = x_ref[...].astype(F32)
        for s in range(count):
            total = total + dot_nn(parts[me ^ s], weights[s][...])
        mixed_ref[...] = total
        inverse = lax.rsqrt(jnp.mean(total * total, axis=-1, keepdims=True) + EPS)
        act_ref[...] = (total * inverse * gain_ref[...]).astype(BF16)

    return body


def expert_body(count, local, rows):
    slots = local * CAP

    def body(me_ref, *refs):
        acts, grads = refs[:count], refs[count : 2 * count]
        slot_ref, hit_ref, router_ref, wg_ref, wu_ref, wd_ref = refs[2 * count : 2 * count + 6]
        (gg_ref, ug_ref, dg_ref, gate_out, dgate_ref) = refs[2 * count + 6 : 2 * count + 11]
        youts = refs[2 * count + 11 : 3 * count + 11]
        gouts = refs[3 * count + 11 : 4 * count + 11]
        gate_all, xe, gyx, dye, picks, ys, dxs = refs[4 * count + 11 :]
        e = pl.program_id(0)

        @pl.when(e == 0)
        def _():
            for s in range(count):
                part = slice(s * rows, (s + 1) * rows)
                logits = dot_nt(router_ref[...], acts[s][...])
                hit = hit_ref[:, part] > 0
                logits = jnp.where(hit, logits, NEG)
                top = jnp.max(logits, axis=0, keepdims=True)
                raised = jnp.where(hit, jnp.exp(logits - top), 0.0)
                gates = raised / jnp.sum(raised, axis=0, keepdims=True)
                gate_all[:, part] = gates
                if s == 0:
                    gate_out[...] = gates

        slot_row = slot_ref[0]
        gate_row = gate_all[pl.ds(me_ref[0] * local + e, 1), :]
        slot_id = lax.broadcasted_iota(jnp.int32, (CAP, rows), 0)
        at = pl.multiple_of(e * CAP, CAP)
        slot_gates = []
        for s in range(count):
            part = slice(s * rows, (s + 1) * rows)
            put = slice(s * CAP, (s + 1) * CAP)
            hits = slot_id == slot_row[:, part]
            pick = jnp.where(hits, 1.0, 0.0).astype(BF16)
            picks[s, pl.ds(at, CAP), :] = pick
            gate = jnp.sum(jnp.where(hits, gate_row[:, part], 0.0), axis=1, keepdims=True)
            slot_gates.append(gate)
            xe[put, :] = dot_nn(pick, acts[s][...]).astype(BF16)
            picked = dot_nn(pick, grads[s][...])
            gyx[put, :] = picked.astype(BF16)
            dye[put, :] = (gate * picked).astype(BF16)
        gate_part = dot_nn(xe[...], wg_ref[0])
        up_part = dot_nn(xe[...], wu_ref[0])
        sig = jax.nn.sigmoid(gate_part)
        act = gate_part * sig
        hidden = (act * up_part).astype(BF16)
        out = dot_nn(hidden, wd_ref[0]).astype(BF16).astype(F32)
        slot_dot = jnp.sum(gyx[...].astype(F32) * out, axis=1, keepdims=True)
        for s in range(count):
            part = slice(s * rows, (s + 1) * rows)
            put = slice(s * CAP, (s + 1) * CAP)
            hits = slot_id == slot_row[:, part]
            dgate_ref[0, :, part] = jnp.sum(jnp.where(hits, slot_dot[put], 0.0), axis=0, keepdims=True)
            ys[s, pl.ds(at, CAP), :] = (slot_gates[s] * out[put]).astype(BF16)
        dg_ref[0] = dot_tn(hidden, dye[...]).astype(BF16)
        grad_hidden = dot_nt(dye[...], wd_ref[0])
        grad_gate = (grad_hidden * up_part * sig * (1.0 + gate_part * (1.0 - sig))).astype(BF16)
        grad_up = (grad_hidden * act).astype(BF16)
        gg_ref[0] = dot_tn(xe[...], grad_gate).astype(BF16)
        ug_ref[0] = dot_tn(xe[...], grad_up).astype(BF16)
        grad_in = (dot_nt(grad_gate, wg_ref[0]) + dot_nt(grad_up, wu_ref[0])).astype(BF16)
        for s in range(count):
            dxs[s, pl.ds(at, CAP), :] = grad_in[s * CAP : (s + 1) * CAP]

        @pl.when(e == local - 1)
        def _():
            for s in range(count):
                youts[s][...] = dot_tn(picks[s], ys[s]).astype(BF16)
                gouts[s][...] = dot_tn(picks[s], dxs[s]).astype(BF16)

    def run(me, acts, grads, slots_t, hits, router_t, wg, wu, wd):
        wide = acts[0].shape[1]
        inner = wg.shape[2]
        whole = lambda shape: pl.BlockSpec(shape, lambda e: tuple(0 for _ in shape))
        each = lambda shape: pl.BlockSpec(
            (1,) + shape, lambda e: (e,) + tuple(0 for _ in shape)
        )
        tokens = count * rows
        shape = jax.ShapeDtypeStruct
        res = pl.pallas_call(
            body,
            grid=(local,),
            in_specs=[smem()]
            + [whole((rows, wide)) for _ in range(2 * count)]
            + [
                each((1, tokens)),
                whole((EXPERTS, tokens)),
                whole((EXPERTS, wide)),
                each((wide, inner)),
                each((wide, inner)),
                each((inner, wide)),
            ],
            out_specs=[
                each((wide, inner)),
                each((wide, inner)),
                each((inner, wide)),
                whole((EXPERTS, rows)),
                each((1, tokens)),
            ]
            + [whole((rows, wide)) for _ in range(2 * count)],
            out_shape=[
                shape((local, wide, inner), BF16),
                shape((local, wide, inner), BF16),
                shape((local, inner, wide), BF16),
                shape((EXPERTS, rows), F32),
                shape((local, 1, tokens), F32),
            ]
            + [shape((rows, wide), BF16) for _ in range(2 * count)],
            scratch_shapes=[
                pltpu.VMEM((EXPERTS, tokens), F32),
                pltpu.VMEM((count * CAP, wide), BF16),
                pltpu.VMEM((count * CAP, wide), BF16),
                pltpu.VMEM((count * CAP, wide), BF16),
                pltpu.VMEM((count, slots, rows), BF16),
                pltpu.VMEM((count, slots, wide), BF16),
                pltpu.VMEM((count, slots, wide), BF16),
            ],
            compiler_params=pltpu.CompilerParams(
                vmem_limit_bytes=56 << 20, dimension_semantics=("arbitrary",)
            ),
        )(me, *acts, *grads, slots_t, hits, router_t, wg, wu, wd)
        return (
            res[:3],
            res[3],
            res[4],
            res[5 : 5 + count],
            res[5 + count :],
        )

    return run


def after_body(count):
    def body(
        me_ref, mixed_ref, ga_ref, gy_ref, gain_ref, gates_ref, dgate_ref, router_ref, act_ref, o_ref,
        *rest,
    ):
        weights = rest[:count]
        gy1_ref, go_ref, rgrad_ref, ggrad_ref = rest[count : count + 4]
        wgrads = rest[count + 4 : 2 * count + 4]
        parts, gparts = rest[2 * count + 4 :]
        gates, dgate = gates_ref[...], dgate_ref[...]
        dlogits = gates * (dgate - jnp.sum(gates * dgate, axis=0, keepdims=True))
        dlogits = dlogits.astype(BF16)
        grad = ga_ref[...] + dot_tn(dlogits, router_ref[...])
        rgrad_ref[...] = dot_nn(dlogits, act_ref[...])
        mixed = mixed_ref[...]
        inverse = lax.rsqrt(jnp.mean(mixed * mixed, axis=-1, keepdims=True) + EPS)
        normed = mixed * inverse
        ggrad_ref[...] = jnp.sum(grad * normed, axis=0, keepdims=True)
        gy1 = gy_ref[...] + norm_back(grad, normed, inverse, gain_ref[...])
        gy1_ref[...] = gy1
        low = gy1.astype(BF16)
        me = me_ref[0]
        width = o_ref.shape[1] // count
        for b in range(count):
            parts[b] = o_ref[:, b * width : (b + 1) * width]
        for s in range(count):
            gparts[me ^ s] = dot_nt(low, weights[s][...]).astype(BF16)
            wgrads[s][...] = dot_tn(parts[me ^ s], low).astype(BF16)
        for b in range(count):
            go_ref[:, b * width : (b + 1) * width] = gparts[b]

    return body


def first_body(count):
    def body(me_ref, x_ref, gain_ref, cos_ref, sin_ref, act_ref, gq_ref, dkv_ref, gy1_ref, *rest):
        wq, wkv = rest[:count], rest[count : 2 * count]
        in_ref, ggrad_ref = rest[2 * count : 2 * count + 2]
        qgrads = rest[2 * count + 2 : 3 * count + 2]
        kgrads = rest[3 * count + 2 : 4 * count + 2]
        gkv, gparts = rest[4 * count + 2 :]
        rows = x_ref.shape[0]
        first = (lanes_of(rows) & 63) < 32
        cosine, sine = cos_ref[...], sin_ref[...]
        for j in range(KVD // 128):
            tile = dkv_ref[:, j * 128 : (j + 1) * 128].astype(F32)
            gkv[:, j * 128 : (j + 1) * 128] = turn_back(tile, cosine, sine, first).astype(BF16)
        gkv[:, KVD:] = dkv_ref[:, KVD:].astype(BF16)
        me = me_ref[0]
        gq = gq_ref[...]
        for s in range(count):
            gparts[me ^ s] = dot_nt(gq, wq[s][...]) + dot_nt(gkv[...], wkv[s][...])
            qgrads[s][...] = dot_tn(act_ref[me ^ s], gq).astype(BF16)
            kgrads[s][...] = dot_tn(act_ref[me ^ s], gkv[...]).astype(BF16)
        grad = jnp.concatenate([gparts[b] for b in range(count)], axis=1)
        x = x_ref[...].astype(F32)
        inverse = lax.rsqrt(jnp.mean(x * x, axis=-1, keepdims=True) + EPS)
        normed = x * inverse
        ggrad_ref[...] = jnp.sum(grad * normed, axis=0, keepdims=True)
        in_ref[...] = gy1_ref[...] + norm_back(grad, normed, inverse, gain_ref[...])

    return body


def make(n_dp, n_ctx):
    def on_device(
        layer_input, query_weight, key_weight, value_weight, out_weight, attn_gain, router_weight,
        moe_gain, gate_weight, up_weight, down_weight, expert_ids, fill_order, block_deal,
        seq_lengths, out_grad,
    ):
        rows, wide = layer_input.shape
        local = gate_weight.shape[0]
        width = wide // n_dp
        me_dp = lax.axis_index("dp").astype(jnp.int32)
        me_ctx = lax.axis_index("ctx").astype(jnp.int32)
        me = me_dp.reshape(1)
        near = rows // BLOCK

        wkv = dp_gather(jnp.concatenate([key_weight, value_weight], axis=1), n_dp)
        small = jnp.concatenate(
            [
                router_weight.T,
                attn_gain[None, :],
                moe_gain[None, :],
                jnp.zeros((14, width), BF16),
            ],
            axis=0,
        )
        small = in_order(dp_gather(small, n_dp), me_dp)
        small = small.transpose(1, 0, 2).reshape(EXPERTS + 16, wide)
        router_t = small[:EXPERTS]
        gain_one = small[EXPERTS : EXPERTS + 1].astype(F32)
        gain_two = small[EXPERTS + 1 : EXPERTS + 2].astype(F32)
        wq = dp_gather(query_weight, n_dp)

        deal, lengths = block_deal[0], seq_lengths[0]
        blocks = deal.shape[0]
        ends = jnp.cumsum(lengths, dtype=jnp.int32)
        mine = lax.dynamic_slice_in_dim(deal, me_ctx * near, near)
        places = (mine[:, None] * BLOCK + jnp.arange(BLOCK, dtype=jnp.int32)[None, :]).reshape(rows, 1)
        starts = jnp.sum(
            jnp.where(places >= ends[None, :], lengths[None, :], 0), axis=1, keepdims=True, dtype=jnp.int32
        )
        relative = (places - starts).astype(F32)
        lane = jnp.arange(128, dtype=jnp.int32)
        inverse = 10000.0 ** (-(lane % 32).astype(F32) * (2.0 / HEAD))
        angles = relative * inverse[None, :]
        cosine = jnp.cos(angles)
        sine = jnp.sin(angles) * jnp.where(lane % 64 < 32, -1.0, 1.0)[None, :]
        block_starts = jnp.sum(
            jnp.where((mine * BLOCK)[:, None] >= ends[None, :], lengths[None, :], 0), axis=1, dtype=jnp.int32
        )
        low_blocks = block_starts // BLOCK
        ring = jnp.array(ring_order(n_ctx)[0], jnp.int32)
        ring_deal = deal.reshape(n_ctx, near)[ring].reshape(blocks)
        held = jnp.arange(blocks, dtype=jnp.int32)
        where_block = jnp.sum(
            jnp.where(ring_deal[None, :] == held[:, None], held[None, :], 0), axis=1, dtype=jnp.int32
        )

        kv_mine, act_one = call(
            kv_body(n_dp),
            [me],
            [layer_input, gain_one, cosine, sine] + wkv,
            [((rows, 2 * KVD), BF16), ((n_dp, rows, width), BF16)],
        )
        every_kv = ring_gather(kv_mine, n_ctx)
        (query,) = call(query_body(n_dp), [me], [act_one, cosine, sine] + wq, [((rows, wide), BF16)])
        wo = dp_gather(out_weight, n_dp)

        ids = jnp.stack(dp_gather(expert_ids.T, n_dp))
        fill = jnp.stack(dp_gather(fill_order, n_dp))
        names = jnp.arange(EXPERTS, dtype=jnp.int32)
        hits = jnp.sum((ids[:, :, None, :] == names[None, None, :, None]).astype(F32), axis=1)
        earlier = (fill[:, 0, :, None] < fill[:, 0, None, :]).astype(BF16)
        prior = jnp.einsum(
            "set,stu->seu", hits.astype(BF16), earlier, preferred_element_type=F32
        )
        slot = jnp.where((hits > 0) & (prior < CAP), prior, -1.0).astype(jnp.int32)
        slot = lax.dynamic_slice_in_dim(slot, me_dp * local, local, axis=1)
        slots_t = slot.transpose(1, 0, 2).reshape(local, 1, n_dp * rows)
        hits_t = hits.transpose(1, 0, 2).reshape(EXPERTS, n_dp * rows)
        grads_all = dp_gather(out_grad.astype(BF16), n_dp)

        attended, extended = call(
            attend_body,
            [low_blocks, mine, where_block],
            [query, every_kv, starts],
            [((rows, wide), BF16), ((PAIRS, 4, rows, 128), F32)],
            [
                pltpu.VMEM((PAIRS, 4 * BLOCK, 128), BF16),
                pltpu.VMEM((PAIRS, 4 * BLOCK, 1), F32),
                pltpu.VMEM((PAIRS, 4 * BLOCK, 1), F32),
                pltpu.VMEM((PAIRS, 4 * BLOCK, 128), F32),
            ],
        )
        mixed, act_two = call(
            mix_body(n_dp),
            [me],
            [layer_input, attended, gain_two] + wo,
            [((rows, wide), F32), ((rows, wide), BF16)],
            [pltpu.VMEM((n_dp, rows, width), BF16)],
        )

        acts_all = dp_gather(act_two, n_dp)
        weight_grads, gates, dgates, y_parts, g_parts = expert_body(n_dp, local, rows)(
            me, acts_all, grads_all, slots_t, hits_t, router_t, gate_weight, up_weight, down_weight
        )

        expert_sums = []
        scattered = [
            ring_scatter(g.reshape(-1, g.shape[2]), n_ctx) for g in weight_grads
        ]
        for g, part in zip(weight_grads, scattered):
            expert_sums.append(ring_gather(part, n_ctx).reshape(g.shape).astype(F32))

        back = [dgates[:, 0, s * rows : (s + 1) * rows] for s in range(n_dp)]
        back = [back[0]] + [lax.ppermute(back[s], "dp", xor_pairs(n_dp, s)) for s in range(1, n_dp)]
        dgate_t = in_order(back, me_dp).reshape(EXPERTS, rows)
        grad_act_two = dp_reduce(g_parts, n_dp)
        layer_output = mixed + dp_reduce(y_parts, n_dp)
        res = call(
            after_body(n_dp),
            [me],
            [mixed, grad_act_two, out_grad, gain_two, gates, dgate_t, router_t, act_two, attended] + wo,
            [((rows, wide), F32), ((rows, wide), BF16), ((EXPERTS, wide), F32), ((1, wide), F32)]
            + [((width, wide), BF16)] * n_dp,
            [pltpu.VMEM((n_dp, rows, width), BF16), pltpu.VMEM((n_dp, rows, width), BF16)],
        )
        grad_mixed, grad_heads, router_part, gain_two_part = res[:4]
        out_parts = res[4:]
        grad_query, kv_grads = call(
            attend_back_body,
            [low_blocks, mine, where_block],
            [query, every_kv, starts, grad_heads, extended, cosine, sine],
            [((rows, wide), BF16), ((blocks * BLOCK, 2 * KVD), BF16)],
            [
                pltpu.VMEM((PAIRS, 4 * BLOCK, 128), BF16),
                pltpu.VMEM((PAIRS, 4 * BLOCK, 128), BF16),
                pltpu.VMEM((PAIRS, 4 * BLOCK, 1), F32),
                pltpu.VMEM((PAIRS, 4 * BLOCK, 1), F32),
                pltpu.VMEM((PAIRS, 4 * BLOCK, 128), F32),
                pltpu.VMEM((blocks * BLOCK, 2 * KVD), F32),
            ],
        )
        kv_grad = ring_scatter(kv_grads, n_ctx)
        res = call(
            first_body(n_dp),
            [me],
            [layer_input, gain_one, cosine, sine, act_one, grad_query, kv_grad, grad_mixed] + wq + wkv,
            [((rows, wide), F32), ((1, wide), F32)]
            + [((width, wide), BF16)] * n_dp
            + [((width, 2 * KVD), BF16)] * n_dp,
            [pltpu.VMEM((rows, 2 * KVD), BF16), pltpu.VMEM((n_dp, rows, width), F32)],
        )
        input_grad, gain_one_part = res[:2]
        q_parts, kv_parts = res[2 : 2 + n_dp], res[2 + n_dp :]

        dense = jnp.concatenate(
            [dp_reduce(part, n_dp).astype(BF16) for part in (out_parts, q_parts, kv_parts)], axis=0
        )
        dense = ring_gather(ring_scatter(dense, n_ctx), n_ctx).astype(F32)
        tiny = jnp.concatenate([router_part, gain_one_part, gain_two_part], axis=0)
        for step in [1 << b for b in range(n_ctx.bit_length() - 1)]:
            tiny = tiny + lax.ppermute(tiny, "ctx", xor_pairs(n_ctx, step))
        for step in [1 << b for b in range(n_dp.bit_length() - 1)]:
            tiny = tiny + lax.ppermute(tiny, "dp", xor_pairs(n_dp, step))
        tiny = lax.dynamic_slice_in_dim(tiny, me_dp * width, width, axis=1)
        return (
            layer_output,
            input_grad,
            dense[width : 2 * width],
            dense[2 * width :, :KVD],
            dense[2 * width :, KVD:],
            dense[:width],
            tiny[EXPERTS],
            tiny[:EXPERTS].T,
            tiny[EXPERTS + 1],
            expert_sums[0],
            expert_sums[1],
            expert_sums[2],
        )

    return on_device


def solution(mesh):
    rows2 = P(("dp", "ctx"), None)
    mat = P("dp", None)
    cube = P("dp", None, None)
    in_specs = (
        rows2, mat, mat, mat, mat, P("dp"), mat, P("dp"), cube, cube, cube, rows2, rows2, mat, mat, rows2,
    )
    out_specs = (rows2, rows2, mat, mat, mat, mat, P("dp"), mat, P("dp"), cube, cube, cube)
    return jax.shard_map(
        make(mesh.shape["dp"], mesh.shape["ctx"]),
        mesh=mesh,
        in_specs=in_specs,
        out_specs=out_specs,
        check_vma=False,
    )
```

```python
import math

import jax
import jax.numpy as jnp
from jax import lax
from jax.experimental import pallas as pl
from jax.experimental.pallas import tpu as pltpu
from jax.sharding import PartitionSpec as P

EXPERTS = 32
BLOCK = 128
CAP = 64
HEAD = 64
KVD = 512
PAIRS = 4
EPS = 1e-06
NEG = -1e30
F32 = jnp.float32
BF16 = jnp.bfloat16


def dot_nn(a, b):
    return lax.dot_general(a, b, (((1,), (0,)), ((), ())), preferred_element_type=F32)


def dot_nt(a, b):
    return lax.dot_general(a, b, (((1,), (1,)), ((), ())), preferred_element_type=F32)


def dot_tn(a, b):
    return lax.dot_general(a, b, (((0,), (0,)), ((), ())), preferred_element_type=F32)


def vmem():
    return pl.BlockSpec(memory_space=pltpu.VMEM)


def smem():
    return pl.BlockSpec(memory_space=pltpu.SMEM)


def cost(flops, arrays, outs):
    moved = sum(a.size * a.dtype.itemsize for a in arrays)
    moved += sum(math.prod(s) * jnp.dtype(d).itemsize for s, d in outs)
    return pl.CostEstimate(flops=flops, transcendentals=0, bytes_accessed=moved)


def call(body, scalars, arrays, outs, scratch=(), mib=48, flops=0):
    return pl.pallas_call(
        body,
        cost_estimate=cost(flops, arrays, outs),
        in_specs=[smem() for _ in scalars] + [vmem() for _ in arrays],
        out_specs=[vmem() for _ in outs],
        out_shape=[jax.ShapeDtypeStruct(s, d) for s, d in outs],
        scratch_shapes=list(scratch),
        compiler_params=pltpu.CompilerParams(vmem_limit_bytes=mib << 20),
    )(*scalars, *arrays)


def xor_pairs(count, step):
    return [(i, i ^ step) for i in range(count)]


def dp_gather(block, count):
    pieces = {0: block}
    for step in range(2, count, 2):
        pieces[step] = lax.ppermute(block, "dp", xor_pairs(count, step))
    for step in range(0, count, 2):
        pieces[step + 1] = lax.ppermute(pieces[step], "dp", xor_pairs(count, 1))
    return [pieces[s] for s in range(count)]


def dp_cores(pieces, count):
    kept = []
    for step in range(0, count, 2):
        other = lax.ppermute(pieces[step + 1], "dp", xor_pairs(count, 1))
        kept.append((pieces[step].astype(F32) + other.astype(F32)).astype(BF16))
    return kept


def dp_rest(kept, count):
    total = kept[0].astype(F32)
    for i in range(1, len(kept)):
        other = lax.ppermute(kept[i], "dp", xor_pairs(count, 2 * i))
        total = total + other.astype(F32)
    return total


def dp_reduce(pieces, count):
    return dp_rest(dp_cores(pieces, count), count)


def in_order(pieces, index):
    stacked = jnp.stack(pieces)
    count = len(pieces)
    bit = 1
    while bit < count:
        swapped = jnp.stack([stacked[j ^ bit] for j in range(count)])
        stacked = jnp.where((index & bit) > 0, swapped, stacked)
        bit *= 2
    return stacked


def ring_order(count):
    return [list(range(0, count, 2)) + list(range(count - 1, 0, -2))]


def ring_gather(block, count):
    return lax.all_gather(block, "ctx", axis=0, tiled=True, axis_index_groups=ring_order(count))


def ring_scatter(block, count):
    return lax.psum_scatter(
        block, "ctx", scatter_dimension=0, tiled=True, axis_index_groups=ring_order(count)
    )


def half_swap(tile, first):
    return jnp.where(first, pltpu.roll(tile, 96, 1), pltpu.roll(tile, 32, 1))


def turn(tile, cosine, sine, first):
    return tile * cosine + half_swap(tile, first) * sine


def turn_back(tile, cosine, sine, first):
    return tile * cosine - half_swap(tile, first) * sine


def lanes_of(rows):
    return lax.broadcasted_iota(jnp.int32, (rows, 128), 1)


def spread_heads(tile_a, tile_b):
    low = lanes_of(tile_a.shape[0]) < HEAD
    return jnp.concatenate(
        [
            jnp.where(low, tile_a, 0.0),
            jnp.where(low, pltpu.roll(tile_a, HEAD, 1), 0.0),
            jnp.where(low, 0.0, pltpu.roll(tile_b, HEAD, 1)),
            jnp.where(low, 0.0, tile_b),
        ],
        axis=0,
    )


def join_heads(stacked):
    rows = stacked.shape[0] // 4
    low = lanes_of(rows) < HEAD
    part = [stacked[h * rows : (h + 1) * rows] for h in range(4)]
    return (
        jnp.where(low, part[0], pltpu.roll(part[1], HEAD, 1)),
        jnp.where(low, pltpu.roll(part[2], HEAD, 1), part[3]),
    )


def norm_back(grad, normed, inverse, gain):
    scaled = grad * gain
    return inverse * (scaled - normed * jnp.mean(scaled * normed, axis=-1, keepdims=True))


def kv_body(count):
    def body(me_ref, x_ref, gain_ref, cos_ref, sin_ref, *rest):
        weights, (kv_ref, act_ref) = rest[:count], rest[count:]
        x = x_ref[...].astype(F32)
        inverse = lax.rsqrt(jnp.mean(x * x, axis=-1, keepdims=True) + EPS)
        act = (x * inverse * gain_ref[...]).astype(BF16)
        width = x.shape[1] // count
        for b in range(count):
            act_ref[b] = act[:, b * width : (b + 1) * width]
        me = me_ref[0]
        total = dot_nn(act_ref[me], weights[0][...])
        for s in range(1, count):
            total = total + dot_nn(act_ref[me ^ s], weights[s][...])
        first = (lanes_of(x.shape[0]) & 63) < 32
        cosine, sine = cos_ref[...], sin_ref[...]
        for j in range(KVD // 128):
            tile = total[:, j * 128 : (j + 1) * 128]
            kv_ref[:, j * 128 : (j + 1) * 128] = turn(tile, cosine, sine, first).astype(BF16)
        kv_ref[:, KVD:] = total[:, KVD:].astype(BF16)

    return body


def query_body(count):
    def body(me_ref, act_ref, cos_ref, sin_ref, *rest):
        weights, q_ref = rest[:count], rest[count]
        me = me_ref[0]
        total = dot_nn(act_ref[me], weights[0][...])
        for s in range(1, count):
            total = total + dot_nn(act_ref[me ^ s], weights[s][...])
        first = (lanes_of(total.shape[0]) & 63) < 32
        cosine, sine = cos_ref[...], sin_ref[...]
        for j in range(total.shape[1] // 128):
            tile = total[:, j * 128 : (j + 1) * 128]
            turned = turn(tile, cosine, sine, first).astype(BF16)
            q_ref[:, j * 128 : (j + 1) * 128] = turned * (1.0 / HEAD)

    return body


def visible(place_block, key_block, starts):
    rows = lax.broadcasted_iota(jnp.int32, (BLOCK, BLOCK), 0) + place_block * BLOCK
    keys = lax.broadcasted_iota(jnp.int32, (BLOCK, BLOCK), 1) + key_block * BLOCK
    return (keys <= rows) & (keys >= starts)


def attend_body(low_ref, high_ref, where_ref, q_ref, kv_ref, starts_ref, o_ref, ext_ref, qs, ms, ls, accs):
    low_half = lanes_of(BLOCK) < HEAD
    for qb in range(q_ref.shape[0] // BLOCK):
        rows = slice(qb * BLOCK, (qb + 1) * BLOCK)
        for j in range(PAIRS):
            qs[j] = spread_heads(
                q_ref[rows, 256 * j : 256 * j + 128].astype(F32),
                q_ref[rows, 256 * j + 128 : 256 * j + 256].astype(F32),
            ).astype(BF16)
        ms[...] = jnp.full(ms.shape, NEG, F32)
        ls[...] = jnp.zeros(ls.shape, F32)
        accs[...] = jnp.zeros(accs.shape, F32)
        high = high_ref[qb]

        def step(b, carry):
            at = pl.multiple_of(where_ref[b] * BLOCK, BLOCK)
            seen = visible(high, b, starts_ref[rows, :])[None]
            for j in range(PAIRS):
                key = kv_ref[pl.ds(at, BLOCK), 128 * j : 128 * j + 128]
                value = kv_ref[pl.ds(at, BLOCK), KVD + 128 * j : KVD + 128 * j + 128]
                scores = dot_nt(qs[j], key).reshape(4, BLOCK, BLOCK)
                scores = jnp.where(seen, scores, NEG).reshape(4 * BLOCK, BLOCK)
                old = ms[j]
                new = jnp.maximum(old, jnp.max(scores, axis=-1, keepdims=True))
                weights = jnp.exp(scores - new)
                shrink = jnp.exp(old - new)
                ls[j] = ls[j] * shrink + jnp.sum(weights, axis=-1, keepdims=True)
                accs[j] = accs[j] * shrink + dot_nn(weights.astype(BF16), value)
                ms[j] = new
            return carry

        lax.fori_loop(low_ref[qb], high + 1, step, 0)
        for j in range(PAIRS):
            attended = accs[j] / ls[j]
            total = ms[j] + jnp.log(ls[j])
            left, right = join_heads(attended)
            o_ref[rows, 256 * j : 256 * j + 128] = left.astype(BF16)
            o_ref[rows, 256 * j + 128 : 256 * j + 256] = right.astype(BF16)
            for h in range(4):
                part = slice(h * BLOCK, (h + 1) * BLOCK)
                keep = low_half if h < 2 else jnp.logical_not(low_half)
                ext_ref[j, h, rows, :] = jnp.where(keep, attended[part], total[part])


def attend_back_body(
    low_ref, high_ref, where_ref, q_ref, kv_ref, starts_ref, go_ref, ext_ref, cos_ref, sin_ref,
    gq_ref, dkv_ref, qs, gs, ds, lse, dqs, sums,
):
    first = (lanes_of(BLOCK) & 63) < 32
    sums[...] = jnp.zeros(sums.shape, F32)
    for qb in range(q_ref.shape[0] // BLOCK):
        rows = slice(qb * BLOCK, (qb + 1) * BLOCK)
        for j in range(PAIRS):
            cols = slice(256 * j, 256 * j + 128), slice(256 * j + 128, 256 * j + 256)
            qs[j] = spread_heads(
                q_ref[rows, cols[0]].astype(F32), q_ref[rows, cols[1]].astype(F32)
            ).astype(BF16)
            grad = spread_heads(
                go_ref[rows, cols[0]].astype(F32), go_ref[rows, cols[1]].astype(F32)
            )
            gs[j] = grad.astype(BF16)
            for h in range(4):
                part = slice(h * BLOCK, (h + 1) * BLOCK)
                ext = ext_ref[j, h, rows, :]
                ds[j, part, :] = jnp.sum(grad[part] * ext, axis=-1, keepdims=True)
                lse[j, part, :] = ext[:, 127:128] if h < 2 else ext[:, 0:1]
        dqs[...] = jnp.zeros(dqs.shape, F32)
        high = high_ref[qb]

        def step(b, carry):
            at = pl.multiple_of(where_ref[b] * BLOCK, BLOCK)
            seen = visible(high, b, starts_ref[rows, :])[None]
            for j in range(PAIRS):
                kcols = slice(128 * j, 128 * j + 128)
                vcols = slice(KVD + 128 * j, KVD + 128 * j + 128)
                key = kv_ref[pl.ds(at, BLOCK), kcols]
                value = kv_ref[pl.ds(at, BLOCK), vcols]
                scores = dot_nt(qs[j], key).reshape(4, BLOCK, BLOCK)
                scores = jnp.where(seen, scores, NEG).reshape(4 * BLOCK, BLOCK)
                weights = jnp.exp(scores - lse[j])
                grad = dot_nt(gs[j], value)
                score_grad = (weights * (grad - ds[j])).astype(BF16)
                dqs[j] += dot_nn(score_grad, key)
                sums[pl.ds(at, BLOCK), kcols] += dot_tn(score_grad, qs[j])
                sums[pl.ds(at, BLOCK), vcols] += dot_tn(weights.astype(BF16), gs[j])
            return carry

        lax.fori_loop(low_ref[qb], high + 1, step, 0)
        cosine, sine = cos_ref[rows, :], sin_ref[rows, :]
        for j in range(PAIRS):
            left, right = join_heads(dqs[j] * (1.0 / HEAD))
            gq_ref[rows, 256 * j : 256 * j + 128] = turn_back(left, cosine, sine, first).astype(BF16)
            gq_ref[rows, 256 * j + 128 : 256 * j + 256] = turn_back(right, cosine, sine, first).astype(
                BF16
            )
    dkv_ref[...] = sums[...].astype(BF16)


def mix_body(count):
    def body(me_ref, x_ref, o_ref, gain_ref, *rest):
        weights, (mixed_ref, act_ref, parts) = rest[:count], rest[count:]
        width = o_ref.shape[1] // count
        for b in range(count):
            parts[b] = o_ref[:, b * width : (b + 1) * width]
        me = me_ref[0]
        total = x_ref[...].astype(F32)
        for s in range(count):
            total = total + dot_nn(parts[me ^ s], weights[s][...])
        mixed_ref[...] = total
        inverse = lax.rsqrt(jnp.mean(total * total, axis=-1, keepdims=True) + EPS)
        act_ref[...] = (total * inverse * gain_ref[...]).astype(BF16)

    return body


def expert_call(blocks, rows, local, served, first, number, last_dims):
    wide, inner = last_dims
    tokens = blocks * rows

    def body(at_ref, *refs):
        acts, grads = refs[:blocks], refs[blocks : 2 * blocks]
        slot_ref, hit_ref, router_ref, wg_ref, wu_ref, wd_ref = refs[2 * blocks : 2 * blocks + 6]
        gg_ref, ug_ref, dg_ref, gate_out, dgate_ref, y_ref, dx_ref = refs[2 * blocks + 6 : 2 * blocks + 13]
        gate_all, xe, gyx, dye = refs[2 * blocks + 13 :]
        e = pl.program_id(0)

        @pl.when(e == 0)
        def _():
            for s in range(blocks):
                part = slice(s * rows, (s + 1) * rows)
                logits = dot_nt(router_ref[...], acts[s][...])
                hit = hit_ref[:, part] > 0
                logits = jnp.where(hit, logits, NEG)
                top = jnp.max(logits, axis=0, keepdims=True)
                raised = jnp.where(hit, jnp.exp(logits - top), 0.0)
                gates = raised / jnp.sum(raised, axis=0, keepdims=True)
                gate_all[:, part] = gates
                if s == 0:
                    gate_out[...] = gates

        slot_row = slot_ref[0]
        gate_row = gate_all[pl.ds(at_ref[1] + e, 1), :]
        slot_id = lax.broadcasted_iota(jnp.int32, (CAP, rows), 0)
        slot_gates = []
        for s in range(blocks):
            part = slice(s * rows, (s + 1) * rows)
            put = slice(s * CAP, (s + 1) * CAP)
            hits = slot_id == slot_row[:, part]
            pick = jnp.where(hits, 1.0, 0.0).astype(BF16)
            gate = jnp.sum(jnp.where(hits, gate_row[:, part], 0.0), axis=1, keepdims=True)
            slot_gates.append(gate)
            xe[put, :] = dot_nn(pick, acts[s][...]).astype(BF16)
            picked = dot_nn(pick, grads[s][...])
            gyx[put, :] = picked.astype(BF16)
            dye[put, :] = (gate * picked).astype(BF16)
        gate_part = dot_nn(xe[...], wg_ref[0])
        up_part = dot_nn(xe[...], wu_ref[0])
        sig = jax.nn.sigmoid(gate_part)
        act = gate_part * sig
        hidden = (act * up_part).astype(BF16)
        out = dot_nn(hidden, wd_ref[0]).astype(BF16).astype(F32)
        slot_dot = jnp.sum(gyx[...].astype(F32) * out, axis=1, keepdims=True)
        for s in range(blocks):
            part = slice(s * rows, (s + 1) * rows)
            put = slice(s * CAP, (s + 1) * CAP)
            hits = slot_id == slot_row[:, part]
            dgate_ref[0, :, part] = jnp.sum(jnp.where(hits, slot_dot[put], 0.0), axis=0, keepdims=True)
            y_ref[0, put, :] = (slot_gates[s] * out[put]).astype(BF16)
        dg_ref[0] = dot_tn(hidden, dye[...]).astype(BF16)
        grad_hidden = dot_nt(dye[...], wd_ref[0])
        grad_gate = (grad_hidden * up_part * sig * (1.0 + gate_part * (1.0 - sig))).astype(BF16)
        grad_up = (grad_hidden * act).astype(BF16)
        gg_ref[0] = dot_tn(xe[...], grad_gate).astype(BF16)
        ug_ref[0] = dot_tn(xe[...], grad_up).astype(BF16)
        dx_ref[0] = (dot_nt(grad_gate, wg_ref[0]) + dot_nt(grad_up, wu_ref[0])).astype(BF16)

    def whole(*shape):
        return pl.BlockSpec(
            shape, lambda e, at: tuple(0 for _ in shape), pipeline_mode=pl.Buffered(1)
        )

    def each(*shape):
        return pl.BlockSpec((1,) + shape, lambda e, at: (e,) + tuple(0 for _ in shape))

    def weight(*shape):
        return pl.BlockSpec((1,) + shape, lambda e, at: (at[0] + e,) + tuple(0 for _ in shape))

    shape = jax.ShapeDtypeStruct
    return pl.pallas_call(
        body,
        cost_estimate=pl.CostEstimate(
            flops=number * blocks * CAP * wide * (18 * inner + 4 * rows),
            transcendentals=0,
            bytes_accessed=number * 12 * wide * inner + 4 * blocks * rows * wide,
        ),
        grid_spec=pltpu.PrefetchScalarGridSpec(
            num_scalar_prefetch=1,
            grid=(number,),
            in_specs=[whole(rows, wide) for _ in range(2 * blocks)]
            + [
                pl.BlockSpec((1, 1, tokens), lambda e, at: (first + e, 0, 0)),
                whole(EXPERTS, tokens),
                whole(EXPERTS, wide),
                weight(wide, inner),
                weight(wide, inner),
                weight(inner, wide),
            ],
            out_specs=[
                each(wide, inner),
                each(wide, inner),
                each(inner, wide),
                pl.BlockSpec((EXPERTS, rows), lambda e, at: (0, 0)),
                each(1, tokens),
                each(blocks * CAP, wide),
                each(blocks * CAP, wide),
            ],
            scratch_shapes=[
                pltpu.VMEM((EXPERTS, tokens), F32),
                pltpu.VMEM((blocks * CAP, wide), BF16),
                pltpu.VMEM((blocks * CAP, wide), BF16),
                pltpu.VMEM((blocks * CAP, wide), BF16),
            ],
        ),
        out_shape=[
            shape((number, wide, inner), BF16),
            shape((number, wide, inner), BF16),
            shape((number, inner, wide), BF16),
            shape((EXPERTS, rows), F32),
            shape((number, 1, tokens), F32),
            shape((number, blocks * CAP, wide), BF16),
            shape((number, blocks * CAP, wide), BF16),
        ],
        compiler_params=pltpu.CompilerParams(
            vmem_limit_bytes=56 << 20, dimension_semantics=("arbitrary",)
        ),
    )


def combine_body(blocks, rows, groups):
    def body(slot_ref, *refs):
        parts, outs = refs[: len(groups)], refs[len(groups) :]
        slot_id = lax.broadcasted_iota(jnp.int32, (CAP, rows), 0)
        for s in range(blocks):
            picks, slots = [], []
            for g, (first, number) in enumerate(groups):
                for e in range(number):
                    hits = slot_id == slot_ref[first + e, :, s * rows : (s + 1) * rows]
                    picks.append(jnp.where(hits, 1.0, 0.0).astype(BF16))
                    slots.append(parts[g][e, s * CAP : (s + 1) * CAP, :])
            outs[s][...] = dot_tn(
                jnp.concatenate(picks, axis=0), jnp.concatenate(slots, axis=0)
            ).astype(BF16)

    return body


def store_pair(held, here, there, places, total):
    rows, cols = here.shape

    def body(at_ref, here_ref, there_ref, *rest):
        out_ref = rest[-1]

        @pl.when(pl.program_id(0) == 0)
        def _():
            out_ref[0] = here_ref[...].astype(F32)

        @pl.when(pl.program_id(0) == 1)
        def _():
            out_ref[0] = there_ref[...].astype(F32)

    more = [] if held is None else [held]
    return pl.pallas_call(
        body,
        grid_spec=pltpu.PrefetchScalarGridSpec(
            num_scalar_prefetch=1,
            grid=(2,),
            in_specs=[pl.BlockSpec((rows, cols), lambda i, at: (0, 0))] * 2
            + [pl.BlockSpec(memory_space=pl.ANY)] * len(more),
            out_specs=pl.BlockSpec((1, rows, cols), lambda i, at: (at[i], 0, 0)),
        ),
        out_shape=jax.ShapeDtypeStruct((total, rows, cols), F32),
        input_output_aliases={3: 0} if more else {},
        compiler_params=pltpu.CompilerParams(
            vmem_limit_bytes=24 << 20, dimension_semantics=("arbitrary",)
        ),
    )(places, here, there, *more)


TO_INNER = [(0, 2), (1, 3), (6, 4), (7, 5)]
ACROSS = [(2, 4), (3, 5), (4, 2), (5, 3)]
TO_OUTER = [(2, 0), (3, 1), (4, 6), (5, 7)]


def tie(value, marks):
    return lax.optimization_barrier((value, marks))[0] if marks else value


def line_step(outer, came, block, part, across, following, sent):
    want_part, want_sent, want_done = block is not None, part is not None, sent is not None
    given = [came] + [a for a in (block, part, across, following, sent) if a is not None]
    outs = want_part + want_sent + want_done

    def body(outer_ref, *refs):
        ins, out = list(refs[: len(given)]), list(refs[len(given) :])
        came_ref = ins.pop(0)
        block_ref = ins.pop(0) if want_part else None
        part_ref, across_ref = (ins.pop(0), ins.pop(0)) if want_sent else (None, None)
        following_ref = ins.pop(0) if following is not None else None
        sent_ref = ins.pop(0) if want_done else None
        part_out = out.pop(0) if want_part else None
        sent_out = out.pop(0) if want_sent else None
        done_out = out.pop(0) if want_done else None

        @pl.when(outer_ref[0] == 0)
        def _():
            if want_part:
                part_out[...] = block_ref[...] + came_ref[...]
            if want_sent:
                sent_out[...] = part_ref[...] + across_ref[...]
            if want_done:
                done_out[...] = sent_ref[...]

        @pl.when(outer_ref[0] == 1)
        def _():
            if following is not None:
                sent_out[...] = following_ref[...]
            if want_done:
                done_out[...] = came_ref[...]

    res = call(body, [outer], given, [(came.shape, BF16)] * outs, mib=24)
    res = list(res)
    return [res.pop(0) if w else None for w in (want_part, want_sent, want_done)]


class LineSums:
    LAG = 3

    def __init__(self, me, beside, base, base_there, total):
        self.outer = ((me < 2) | (me >= 6)).astype(jnp.int32).reshape(1)
        self.beside, self.base, self.base_there, self.total = beside, base, base_there, total
        self.blocks, self.held = [], [None, None, None]
        self.sent, self.parts, self.across = {}, [], []
        self.swaps, self.marks, self.done = [], [], 0

    def feed(self, results):
        for e in range(results[0].shape[0]):
            self.blocks += [results[m][e] for m in range(3)]

    def store(self):
        if self.done < len(self.swaps):
            here, there = self.swaps[self.done]
            e, m = divmod(self.done, 3)
            places = jnp.stack([self.base + e, self.base_there + e])
            self.held[m] = store_pair(self.held[m], here, there, places, self.total)
            self.done += 1

    def step(self, after=()):
        t, count = len(self.marks), len(self.blocks)
        new, old = t < count, t >= self.LAG
        sent = self.sent[t] if old else self.blocks[t]
        kept = [h for h in self.held if h is not None]
        sent, kept, _ = lax.optimization_barrier((sent, kept, list(after)))
        self.held[: len(kept)] = kept
        came = lax.ppermute(sent, "ctx", (TO_INNER if new else []) + (TO_OUTER if old else []))
        self.marks.append(came)
        turn_back = 0 < t <= count
        shape = self.blocks[t % 3].shape
        more = turn_back and t + 2 < count
        part, _, finished = line_step(
            self.outer, came, self.blocks[t] if new else None, None, None, None, sent if old else None
        ) if new or old else (None, None, None)
        if turn_back:
            _, self.sent[t + 2], _ = line_step(
                self.outer, self.across[t - 1], None, self.parts[t - 1], self.across[t - 1],
                self.blocks[t + 2] if more else None, None,
            )
        if new:
            self.parts.append(part)
            self.across.append(lax.ppermute(part, "ctx", ACROSS))
        if len(self.swaps) > 1:
            self.store()
        if old:
            self.swaps.append((finished, lax.ppermute(finished, "ctx", self.beside)))

    def hold(self, value):
        return tie(value, self.marks[-2:-1])

    def finish(self):
        while self.done < len(self.swaps):
            self.store()
        return self.held


def after_body(count):
    def body(
        me_ref, mixed_ref, ga_ref, gy_ref, gain_ref, gates_ref, dgate_ref, router_ref, act_ref, o_ref,
        *rest,
    ):
        weights = rest[:count]
        gy1_ref, go_ref, rgrad_ref, ggrad_ref = rest[count : count + 4]
        wgrads = rest[count + 4 : 2 * count + 4]
        parts, gparts = rest[2 * count + 4 :]
        gates, dgate = gates_ref[...], dgate_ref[...]
        dlogits = gates * (dgate - jnp.sum(gates * dgate, axis=0, keepdims=True))
        dlogits = dlogits.astype(BF16)
        grad = ga_ref[...] + dot_tn(dlogits, router_ref[...])
        rgrad_ref[...] = dot_nn(dlogits, act_ref[...])
        mixed = mixed_ref[...]
        inverse = lax.rsqrt(jnp.mean(mixed * mixed, axis=-1, keepdims=True) + EPS)
        normed = mixed * inverse
        ggrad_ref[...] = jnp.sum(grad * normed, axis=0, keepdims=True)
        gy1 = gy_ref[...] + norm_back(grad, normed, inverse, gain_ref[...])
        gy1_ref[...] = gy1
        low = gy1.astype(BF16)
        me = me_ref[0]
        width = o_ref.shape[1] // count
        for b in range(count):
            parts[b] = o_ref[:, b * width : (b + 1) * width]
        for s in range(count):
            gparts[me ^ s] = dot_nt(low, weights[s][...]).astype(BF16)
            wgrads[s][...] = dot_tn(parts[me ^ s], low).astype(BF16)
        for b in range(count):
            go_ref[:, b * width : (b + 1) * width] = gparts[b]

    return body


def first_body(count):
    def body(me_ref, x_ref, gain_ref, cos_ref, sin_ref, act_ref, gq_ref, dkv_ref, gy1_ref, *rest):
        wq, wkv = rest[:count], rest[count : 2 * count]
        in_ref, ggrad_ref = rest[2 * count : 2 * count + 2]
        qgrads = rest[2 * count + 2 : 3 * count + 2]
        kgrads = rest[3 * count + 2 : 4 * count + 2]
        gkv, gparts = rest[4 * count + 2 :]
        rows = x_ref.shape[0]
        first = (lanes_of(rows) & 63) < 32
        cosine, sine = cos_ref[...], sin_ref[...]
        for j in range(KVD // 128):
            tile = dkv_ref[:, j * 128 : (j + 1) * 128].astype(F32)
            gkv[:, j * 128 : (j + 1) * 128] = turn_back(tile, cosine, sine, first).astype(BF16)
        gkv[:, KVD:] = dkv_ref[:, KVD:].astype(BF16)
        me = me_ref[0]
        gq = gq_ref[...]
        for s in range(count):
            gparts[me ^ s] = dot_nt(gq, wq[s][...]) + dot_nt(gkv[...], wkv[s][...])
            qgrads[s][...] = dot_tn(act_ref[me ^ s], gq).astype(BF16)
            kgrads[s][...] = dot_tn(act_ref[me ^ s], gkv[...]).astype(BF16)
        grad = jnp.concatenate([gparts[b] for b in range(count)], axis=1)
        x = x_ref[...].astype(F32)
        inverse = lax.rsqrt(jnp.mean(x * x, axis=-1, keepdims=True) + EPS)
        normed = x * inverse
        ggrad_ref[...] = jnp.sum(grad * normed, axis=0, keepdims=True)
        in_ref[...] = gy1_ref[...] + norm_back(grad, normed, inverse, gain_ref[...])

    return body


def make(n_dp, n_ctx):
    def on_device(
        layer_input, query_weight, key_weight, value_weight, out_weight, attn_gain, router_weight,
        moe_gain, gate_weight, up_weight, down_weight, expert_ids, fill_order, block_deal,
        seq_lengths, out_grad,
    ):
        rows, wide = layer_input.shape
        local = gate_weight.shape[0]
        width = wide // n_dp
        me_dp = lax.axis_index("dp").astype(jnp.int32)
        me_ctx = lax.axis_index("ctx").astype(jnp.int32)
        me = me_dp.reshape(1)
        near = rows // BLOCK

        pairs = n_ctx == 8 and local % 2 == 0
        served = local // 2 if pairs else local
        beside = xor_pairs(n_ctx, 1)
        column = me_ctx & 1 if pairs else jnp.zeros((), jnp.int32)
        grad_low = out_grad.astype(BF16)
        grad_beside = lax.ppermute(grad_low, "ctx", beside) if pairs else None
        wkv = dp_gather(jnp.concatenate([key_weight, value_weight], axis=1), n_dp)
        small = jnp.concatenate(
            [
                router_weight.T,
                attn_gain[None, :],
                moe_gain[None, :],
                jnp.zeros((14, width), BF16),
            ],
            axis=0,
        )
        small = in_order(dp_gather(small, n_dp), me_dp)
        small = small.transpose(1, 0, 2).reshape(EXPERTS + 16, wide)
        router_t = small[:EXPERTS]
        gain_one = small[EXPERTS : EXPERTS + 1].astype(F32)
        gain_two = small[EXPERTS + 1 : EXPERTS + 2].astype(F32)
        wq = dp_gather(query_weight, n_dp)

        deal, lengths = block_deal[0], seq_lengths[0]
        blocks = deal.shape[0]
        ends = jnp.cumsum(lengths, dtype=jnp.int32)
        mine = lax.dynamic_slice_in_dim(deal, me_ctx * near, near)
        places = (mine[:, None] * BLOCK + jnp.arange(BLOCK, dtype=jnp.int32)[None, :]).reshape(rows, 1)
        starts = jnp.sum(
            jnp.where(places >= ends[None, :], lengths[None, :], 0), axis=1, keepdims=True, dtype=jnp.int32
        )
        relative = (places - starts).astype(F32)
        lane = jnp.arange(128, dtype=jnp.int32)
        inverse = 10000.0 ** (-(lane % 32).astype(F32) * (2.0 / HEAD))
        angles = relative * inverse[None, :]
        cosine = jnp.cos(angles)
        sine = jnp.sin(angles) * jnp.where(lane % 64 < 32, -1.0, 1.0)[None, :]
        block_starts = jnp.sum(
            jnp.where((mine * BLOCK)[:, None] >= ends[None, :], lengths[None, :], 0), axis=1, dtype=jnp.int32
        )
        low_blocks = block_starts // BLOCK
        ring = jnp.array(ring_order(n_ctx)[0], jnp.int32)
        ring_deal = deal.reshape(n_ctx, near)[ring].reshape(blocks)
        held = jnp.arange(blocks, dtype=jnp.int32)
        where_block = jnp.sum(
            jnp.where(ring_deal[None, :] == held[:, None], held[None, :], 0), axis=1, dtype=jnp.int32
        )

        kv_mine, act_one = call(
            kv_body(n_dp),
            [me],
            [tie(layer_input, [grad_beside] if pairs else []), gain_one, cosine, sine] + wkv,
            [((rows, 2 * KVD), BF16), ((n_dp, rows, width), BF16)],
        )
        every_kv = ring_gather(kv_mine, n_ctx)
        (query,) = call(query_body(n_dp), [me], [act_one, cosine, sine] + wq, [((rows, wide), BF16)])
        wo = dp_gather(out_weight, n_dp)

        def reach(block):
            pieces = dp_gather(block, n_dp)
            if pairs:
                pieces = pieces + dp_gather(lax.ppermute(block, "ctx", beside), n_dp)
            return pieces

        table = jnp.concatenate([expert_ids.T, fill_order], axis=0)
        table = jnp.stack(reach(table))
        ids, fill = table[:, :-1], table[:, -1]
        held_blocks = table.shape[0]
        names = jnp.arange(EXPERTS, dtype=jnp.int32)
        hits = jnp.sum((ids[:, :, None, :] == names[None, None, :, None]).astype(F32), axis=1)
        earlier = (fill[:, :, None] < fill[:, None, :]).astype(BF16)
        prior = jnp.einsum(
            "set,stu->seu", hits.astype(BF16), earlier, preferred_element_type=F32
        )
        slot = jnp.where((hits > 0) & (prior < CAP), prior, -1.0).astype(jnp.int32)
        base = column * served
        slot = lax.dynamic_slice_in_dim(slot, me_dp * local + base, served, axis=1)
        slots_t = slot.transpose(1, 0, 2).reshape(served, 1, held_blocks * rows)
        hits_t = hits.transpose(1, 0, 2).reshape(EXPERTS, held_blocks * rows)
        grads_all = dp_gather(grad_low, n_dp)
        if pairs:
            grads_all = grads_all + dp_gather(grad_beside, n_dp)
        query, grads_all, wo = lax.optimization_barrier((query, grads_all, wo))

        attended, extended = call(
            attend_body,
            [low_blocks, mine, where_block],
            [query, every_kv, starts],
            [((rows, wide), BF16), ((PAIRS, 4, rows, 128), F32)],
            [
                pltpu.VMEM((PAIRS, 4 * BLOCK, 128), BF16),
                pltpu.VMEM((PAIRS, 4 * BLOCK, 1), F32),
                pltpu.VMEM((PAIRS, 4 * BLOCK, 1), F32),
                pltpu.VMEM((PAIRS, 4 * BLOCK, 128), F32),
            ],
            flops=rows * blocks * BLOCK * wide * 4,
        )
        mixed, act_two = call(
            mix_body(n_dp),
            [me],
            [layer_input, attended, gain_two] + wo,
            [((rows, wide), F32), ((rows, wide), BF16)],
            [pltpu.VMEM((n_dp, rows, width), BF16)],
        )

        acts_all = reach(act_two)
        groups = [(0, 1), (1, served - 1)] if pairs else [(0, served)]
        results = []
        line = LineSums(me_ctx, beside, base, (1 - column) * served, local) if pairs else None

        def step(*after):
            if pairs:
                line.step(after)

        def hold(value):
            return value

        for first, number in groups:
            at = jnp.stack([base + first, me_dp * local + base + first])
            results.append(
                expert_call(
                    held_blocks, rows, local, served, first, number, gate_weight.shape[1:]
                )(
                    at, *acts_all, *grads_all, slots_t, hits_t, router_t, gate_weight, up_weight,
                    down_weight,
                )
            )
            if pairs:
                line.feed(results[-1])
            step(*[res[4] for res in results[1:]])
        gates = results[0][3]

        def combine(index, after):
            return call(
                combine_body(held_blocks, rows, groups),
                [],
                [hold(tie(slots_t, after))] + [res[index] for res in results],
                [((rows, wide), BF16)] * held_blocks,
            )

        def settle(parts, between):
            kept = [dp_cores(parts[s : s + n_dp], n_dp) for s in range(0, held_blocks, n_dp)]
            between(kept)
            totals = [dp_rest(hold(k), n_dp) for k in kept]
            between(totals)
            totals = hold(totals)
            if pairs:
                totals[0] = totals[0] + lax.ppermute(
                    totals[1].astype(BF16), "ctx", beside
                ).astype(F32)
            return totals[0]

        dgates = jnp.concatenate([res[4] for res in results], axis=0)[:, 0]
        back = [dgates[:, s * rows : (s + 1) * rows] for s in range(held_blocks)]
        if pairs:
            other = lax.ppermute(jnp.stack(back[n_dp:]), "ctx", beside)
            own = jnp.stack(back[:n_dp])
            back = jnp.where(
                column == 0,
                jnp.concatenate([own, other], axis=1),
                jnp.concatenate([other, own], axis=1),
            )
        back = [back[0]] + [lax.ppermute(back[s], "dp", xor_pairs(n_dp, s)) for s in range(1, n_dp)]
        dgate_t = in_order(back, me_dp).reshape(EXPERTS, rows)
        g_parts = combine(6, [])
        grad_act_two = settle(g_parts, lambda values: None)
        step(grad_act_two)
        res = call(
            after_body(n_dp),
            [me],
            [mixed, hold(grad_act_two), out_grad, gain_two, gates, dgate_t, router_t, act_two, attended] + wo,
            [((rows, wide), F32), ((rows, wide), BF16), ((EXPERTS, wide), F32), ((1, wide), F32)]
            + [((width, wide), BF16)] * n_dp,
            [pltpu.VMEM((n_dp, rows, width), BF16), pltpu.VMEM((n_dp, rows, width), BF16)],
        )
        grad_mixed, grad_heads, router_part, gain_two_part = res[:4]
        out_parts = res[4:]
        grad_query, kv_grads = call(
            attend_back_body,
            [low_blocks, mine, where_block],
            [query, every_kv, starts, hold(grad_heads), extended, cosine, sine],
            [((rows, wide), BF16), ((blocks * BLOCK, 2 * KVD), BF16)],
            [
                pltpu.VMEM((PAIRS, 4 * BLOCK, 128), BF16),
                pltpu.VMEM((PAIRS, 4 * BLOCK, 128), BF16),
                pltpu.VMEM((PAIRS, 4 * BLOCK, 1), F32),
                pltpu.VMEM((PAIRS, 4 * BLOCK, 1), F32),
                pltpu.VMEM((PAIRS, 4 * BLOCK, 128), F32),
                pltpu.VMEM((blocks * BLOCK, 2 * KVD), F32),
            ],
            flops=rows * blocks * BLOCK * wide * 10,
        )
        step(grad_query)
        kv_grad = ring_scatter(kv_grads, n_ctx)
        y_parts = combine(5, [grad_query])
        y_total = settle(y_parts, lambda values: None)
        layer_output = mixed + y_total
        dense_out = dp_reduce(hold(out_parts), n_dp).astype(BF16)
        step(layer_output)
        res = call(
            first_body(n_dp),
            [me],
            [layer_input, gain_one, cosine, sine, act_one, grad_query, hold(kv_grad), grad_mixed] + wq + wkv,
            [((rows, wide), F32), ((1, wide), F32)]
            + [((width, wide), BF16)] * n_dp
            + [((width, 2 * KVD), BF16)] * n_dp,
            [pltpu.VMEM((rows, 2 * KVD), BF16), pltpu.VMEM((n_dp, rows, width), F32)],
        )
        input_grad, gain_one_part = res[:2]
        q_parts, kv_parts = res[2 : 2 + n_dp], res[2 + n_dp :]
        step(gain_one_part)

        dense_q = dp_reduce(hold(q_parts), n_dp).astype(BF16)
        dense_kv = dp_reduce(kv_parts, n_dp).astype(BF16)
        dense = jnp.concatenate([dense_out, dense_q, dense_kv], axis=0)
        dense = ring_gather(ring_scatter(dense, n_ctx), n_ctx).astype(F32)
        tiny = jnp.concatenate([router_part, gain_one_part, gain_two_part], axis=0)
        for bit in [1 << b for b in range(n_ctx.bit_length() - 1)]:
            tiny = tiny + lax.ppermute(tiny, "ctx", xor_pairs(n_ctx, bit))
        for bit in [1 << b for b in range(n_dp.bit_length() - 1)]:
            tiny = tiny + lax.ppermute(tiny, "dp", xor_pairs(n_dp, bit))
        tiny = lax.dynamic_slice_in_dim(tiny, me_dp * width, width, axis=1)
        if pairs:
            while len(line.marks) < len(line.blocks) + line.LAG:
                line.step()
            expert_sums = line.finish()
        else:
            expert_sums = [
                ring_gather(ring_scatter(g.reshape(-1, g.shape[2]), n_ctx), n_ctx)
                .reshape(g.shape)
                .astype(F32)
                for g in results[0][:3]
            ]
        return (
            layer_output,
            input_grad,
            dense[width : 2 * width],
            dense[2 * width :, :KVD],
            dense[2 * width :, KVD:],
            dense[:width],
            tiny[EXPERTS],
            tiny[:EXPERTS].T,
            tiny[EXPERTS + 1],
            expert_sums[0],
            expert_sums[1],
            expert_sums[2],
        )

    return on_device


def solution(mesh):
    rows2 = P(("dp", "ctx"), None)
    mat = P("dp", None)
    cube = P("dp", None, None)
    in_specs = (
        rows2, mat, mat, mat, mat, P("dp"), mat, P("dp"), cube, cube, cube, rows2, rows2, mat, mat, rows2,
    )
    out_specs = (rows2, rows2, mat, mat, mat, mat, P("dp"), mat, P("dp"), cube, cube, cube)
    return jax.shard_map(
        make(mesh.shape["dp"], mesh.shape["ctx"]),
        mesh=mesh,
        in_specs=in_specs,
        out_specs=out_specs,
        check_vma=False,
    )
```

```python
import math

import jax
import jax.numpy as jnp
from jax import lax
from jax.experimental import pallas as pl
from jax.experimental.pallas import tpu as pltpu
from jax.sharding import PartitionSpec as P

EXPERTS = 32
BLOCK = 128
CAP = 64
HEAD = 64
KVD = 512
PAIRS = 4
EPS = 1e-06
NEG = -1e30
F32 = jnp.float32
BF16 = jnp.bfloat16


def dot_nn(a, b):
    return lax.dot_general(a, b, (((1,), (0,)), ((), ())), preferred_element_type=F32)


def dot_nt(a, b):
    return lax.dot_general(a, b, (((1,), (1,)), ((), ())), preferred_element_type=F32)


def dot_tn(a, b):
    return lax.dot_general(a, b, (((0,), (0,)), ((), ())), preferred_element_type=F32)


def vmem():
    return pl.BlockSpec(memory_space=pltpu.VMEM)


def smem():
    return pl.BlockSpec(memory_space=pltpu.SMEM)


def cost(flops, arrays, outs):
    moved = sum(a.size * a.dtype.itemsize for a in arrays)
    moved += sum(math.prod(s) * jnp.dtype(d).itemsize for s, d in outs)
    return pl.CostEstimate(flops=flops, transcendentals=0, bytes_accessed=moved)


def call(body, scalars, arrays, outs, scratch=(), mib=48, flops=0):
    return pl.pallas_call(
        body,
        cost_estimate=cost(flops, arrays, outs),
        in_specs=[smem() for _ in scalars] + [vmem() for _ in arrays],
        out_specs=[vmem() for _ in outs],
        out_shape=[jax.ShapeDtypeStruct(s, d) for s, d in outs],
        scratch_shapes=list(scratch),
        compiler_params=pltpu.CompilerParams(vmem_limit_bytes=mib << 20),
    )(*scalars, *arrays)


def xor_pairs(count, step):
    return [(i, i ^ step) for i in range(count)]


def dp_gather(block, count):
    pieces = {0: block}
    for step in range(2, count, 2):
        pieces[step] = lax.ppermute(block, "dp", xor_pairs(count, step))
    for step in range(0, count, 2):
        pieces[step + 1] = lax.ppermute(pieces[step], "dp", xor_pairs(count, 1))
    return [pieces[s] for s in range(count)]


def dp_cores(pieces, count):
    kept = []
    for step in range(0, count, 2):
        other = lax.ppermute(pieces[step + 1], "dp", xor_pairs(count, 1))
        kept.append((pieces[step].astype(F32) + other.astype(F32)).astype(BF16))
    return kept


def dp_rest(kept, count):
    total = kept[0].astype(F32)
    for i in range(1, len(kept)):
        other = lax.ppermute(kept[i], "dp", xor_pairs(count, 2 * i))
        total = total + other.astype(F32)
    return total


def dp_reduce(pieces, count):
    return dp_rest(dp_cores(pieces, count), count)


def in_order(pieces, index):
    stacked = jnp.stack(pieces)
    count = len(pieces)
    bit = 1
    while bit < count:
        swapped = jnp.stack([stacked[j ^ bit] for j in range(count)])
        stacked = jnp.where((index & bit) > 0, swapped, stacked)
        bit *= 2
    return stacked


def ring_order(count):
    return [list(range(0, count, 2)) + list(range(count - 1, 0, -2))]


def ring_gather(block, count):
    return lax.all_gather(block, "ctx", axis=0, tiled=True, axis_index_groups=ring_order(count))


def ring_scatter(block, count):
    return lax.psum_scatter(
        block, "ctx", scatter_dimension=0, tiled=True, axis_index_groups=ring_order(count)
    )


def half_swap(tile, first):
    return jnp.where(first, pltpu.roll(tile, 96, 1), pltpu.roll(tile, 32, 1))


def turn(tile, cosine, sine, first):
    return tile * cosine + half_swap(tile, first) * sine


def turn_back(tile, cosine, sine, first):
    return tile * cosine - half_swap(tile, first) * sine


def lanes_of(rows):
    return lax.broadcasted_iota(jnp.int32, (rows, 128), 1)


def spread_heads(tile_a, tile_b):
    low = lanes_of(tile_a.shape[0]) < HEAD
    return jnp.concatenate(
        [
            jnp.where(low, tile_a, 0.0),
            jnp.where(low, pltpu.roll(tile_a, HEAD, 1), 0.0),
            jnp.where(low, 0.0, pltpu.roll(tile_b, HEAD, 1)),
            jnp.where(low, 0.0, tile_b),
        ],
        axis=0,
    )


def join_heads(stacked):
    rows = stacked.shape[0] // 4
    low = lanes_of(rows) < HEAD
    part = [stacked[h * rows : (h + 1) * rows] for h in range(4)]
    return (
        jnp.where(low, part[0], pltpu.roll(part[1], HEAD, 1)),
        jnp.where(low, pltpu.roll(part[2], HEAD, 1), part[3]),
    )


def norm_back(grad, normed, inverse, gain):
    scaled = grad * gain
    return inverse * (scaled - normed * jnp.mean(scaled * normed, axis=-1, keepdims=True))


def kv_body(count):
    def body(me_ref, x_ref, gain_ref, cos_ref, sin_ref, *rest):
        weights, (kv_ref, act_ref) = rest[:count], rest[count:]
        x = x_ref[...].astype(F32)
        inverse = lax.rsqrt(jnp.mean(x * x, axis=-1, keepdims=True) + EPS)
        act = (x * inverse * gain_ref[...]).astype(BF16)
        width = x.shape[1] // count
        for b in range(count):
            act_ref[b] = act[:, b * width : (b + 1) * width]
        me = me_ref[0]
        total = dot_nn(act_ref[me], weights[0][...])
        for s in range(1, count):
            total = total + dot_nn(act_ref[me ^ s], weights[s][...])
        first = (lanes_of(x.shape[0]) & 63) < 32
        cosine, sine = cos_ref[...], sin_ref[...]
        for j in range(KVD // 128):
            tile = total[:, j * 128 : (j + 1) * 128]
            kv_ref[:, j * 128 : (j + 1) * 128] = turn(tile, cosine, sine, first).astype(BF16)
        kv_ref[:, KVD:] = total[:, KVD:].astype(BF16)

    return body


def query_body(count):
    def body(me_ref, act_ref, cos_ref, sin_ref, *rest):
        weights, q_ref = rest[:count], rest[count]
        me = me_ref[0]
        total = dot_nn(act_ref[me], weights[0][...])
        for s in range(1, count):
            total = total + dot_nn(act_ref[me ^ s], weights[s][...])
        first = (lanes_of(total.shape[0]) & 63) < 32
        cosine, sine = cos_ref[...], sin_ref[...]
        for j in range(total.shape[1] // 128):
            tile = total[:, j * 128 : (j + 1) * 128]
            turned = turn(tile, cosine, sine, first).astype(BF16)
            q_ref[:, j * 128 : (j + 1) * 128] = turned * (1.0 / HEAD)

    return body


def visible(place_block, key_block, starts):
    rows = lax.broadcasted_iota(jnp.int32, (BLOCK, BLOCK), 0) + place_block * BLOCK
    keys = lax.broadcasted_iota(jnp.int32, (BLOCK, BLOCK), 1) + key_block * BLOCK
    return (keys <= rows) & (keys >= starts)


def attend_body(low_ref, high_ref, where_ref, q_ref, kv_ref, starts_ref, o_ref, ext_ref, qs, tops, sums, accs):
    low_half = lanes_of(BLOCK) < HEAD
    for qb in range(q_ref.shape[0] // BLOCK):
        rows = slice(qb * BLOCK, (qb + 1) * BLOCK)
        for j in range(PAIRS):
            qs[j] = spread_heads(
                q_ref[rows, 256 * j : 256 * j + 128].astype(F32),
                q_ref[rows, 256 * j + 128 : 256 * j + 256].astype(F32),
            ).astype(BF16)
        tops[...] = jnp.full(tops.shape, NEG, F32)
        sums[...] = jnp.zeros(sums.shape, F32)
        accs[...] = jnp.zeros(accs.shape, F32)
        low, high = low_ref[qb], high_ref[qb]

        def scores_of(b, at, seen, j):
            key = kv_ref[pl.ds(at, BLOCK), 128 * j : 128 * j + 128]
            scores = dot_nt(qs[j], key).reshape(4, BLOCK, BLOCK)
            return jnp.where(seen, scores, NEG).reshape(4 * BLOCK, BLOCK)

        def find_top(b, carry):
            at = pl.multiple_of(where_ref[b] * BLOCK, BLOCK)
            seen = visible(high, b, starts_ref[rows, :])[None]
            for j in range(PAIRS):
                tops[j] = jnp.maximum(tops[j], scores_of(b, at, seen, j))
            return carry

        lax.fori_loop(low, high + 1, find_top, 0)
        for j in range(PAIRS):
            top = jnp.max(tops[j], axis=-1, keepdims=True)
            tops[j] = jnp.broadcast_to(top, tops.shape[1:])

        def gather_values(b, carry):
            at = pl.multiple_of(where_ref[b] * BLOCK, BLOCK)
            seen = visible(high, b, starts_ref[rows, :])[None]
            for j in range(PAIRS):
                value = kv_ref[pl.ds(at, BLOCK), KVD + 128 * j : KVD + 128 * j + 128]
                weights = jnp.exp(scores_of(b, at, seen, j) - tops[j])
                sums[j] += weights
                accs[j] += dot_nn(weights.astype(BF16), value)
            return carry

        lax.fori_loop(low, high + 1, gather_values, 0)
        for j in range(PAIRS):
            weight = jnp.sum(sums[j], axis=-1, keepdims=True)
            attended = accs[j] / weight
            total = tops[j] + jnp.log(weight)
            left, right = join_heads(attended)
            o_ref[rows, 256 * j : 256 * j + 128] = left.astype(BF16)
            o_ref[rows, 256 * j + 128 : 256 * j + 256] = right.astype(BF16)
            for h in range(4):
                part = slice(h * BLOCK, (h + 1) * BLOCK)
                keep = low_half if h < 2 else jnp.logical_not(low_half)
                ext_ref[j, h, rows, :] = jnp.where(keep, attended[part], total[part])


def attend_back_body(
    low_ref, high_ref, where_ref, q_ref, kv_ref, starts_ref, go_ref, ext_ref, cos_ref, sin_ref,
    gq_ref, dkv_ref, qs, gs, ds, lse, dqs, sums,
):
    first = (lanes_of(BLOCK) & 63) < 32
    sums[...] = jnp.zeros(sums.shape, F32)
    for qb in range(q_ref.shape[0] // BLOCK):
        rows = slice(qb * BLOCK, (qb + 1) * BLOCK)
        for j in range(PAIRS):
            cols = slice(256 * j, 256 * j + 128), slice(256 * j + 128, 256 * j + 256)
            qs[j] = spread_heads(
                q_ref[rows, cols[0]].astype(F32), q_ref[rows, cols[1]].astype(F32)
            ).astype(BF16)
            grad = spread_heads(
                go_ref[rows, cols[0]].astype(F32), go_ref[rows, cols[1]].astype(F32)
            )
            gs[j] = grad.astype(BF16)
            for h in range(4):
                part = slice(h * BLOCK, (h + 1) * BLOCK)
                ext = ext_ref[j, h, rows, :]
                flat = (BLOCK, BLOCK)
                delta = jnp.sum(grad[part] * ext, axis=-1, keepdims=True)
                total = ext[:, 127:128] if h < 2 else ext[:, 0:1]
                ds[j, part, :] = jnp.broadcast_to(delta, flat)
                lse[j, part, :] = jnp.broadcast_to(total, flat)
        dqs[...] = jnp.zeros(dqs.shape, F32)
        high = high_ref[qb]

        def step(b, carry):
            at = pl.multiple_of(where_ref[b] * BLOCK, BLOCK)
            seen = visible(high, b, starts_ref[rows, :])[None]
            for j in range(PAIRS):
                kcols = slice(128 * j, 128 * j + 128)
                vcols = slice(KVD + 128 * j, KVD + 128 * j + 128)
                key = kv_ref[pl.ds(at, BLOCK), kcols]
                value = kv_ref[pl.ds(at, BLOCK), vcols]
                scores = dot_nt(qs[j], key).reshape(4, BLOCK, BLOCK)
                scores = jnp.where(seen, scores, NEG).reshape(4 * BLOCK, BLOCK)
                weights = jnp.exp(scores - lse[j])
                grad = dot_nt(gs[j], value)
                score_grad = (weights * (grad - ds[j])).astype(BF16)
                dqs[j] += dot_nn(score_grad, key)
                sums[pl.ds(at, BLOCK), kcols] += dot_tn(score_grad, qs[j])
                sums[pl.ds(at, BLOCK), vcols] += dot_tn(weights.astype(BF16), gs[j])
            return carry

        lax.fori_loop(low_ref[qb], high + 1, step, 0)
        cosine, sine = cos_ref[rows, :], sin_ref[rows, :]
        for j in range(PAIRS):
            left, right = join_heads(dqs[j] * (1.0 / HEAD))
            gq_ref[rows, 256 * j : 256 * j + 128] = turn_back(left, cosine, sine, first).astype(BF16)
            gq_ref[rows, 256 * j + 128 : 256 * j + 256] = turn_back(right, cosine, sine, first).astype(
                BF16
            )
    dkv_ref[...] = sums[...].astype(BF16)


def mix_body(count):
    def body(me_ref, x_ref, o_ref, gain_ref, *rest):
        weights, (mixed_ref, act_ref, parts) = rest[:count], rest[count:]
        width = o_ref.shape[1] // count
        for b in range(count):
            parts[b] = o_ref[:, b * width : (b + 1) * width]
        me = me_ref[0]
        total = x_ref[...].astype(F32)
        for s in range(count):
            total = total + dot_nn(parts[me ^ s], weights[s][...])
        mixed_ref[...] = total
        inverse = lax.rsqrt(jnp.mean(total * total, axis=-1, keepdims=True) + EPS)
        act_ref[...] = (total * inverse * gain_ref[...]).astype(BF16)

    return body


def expert_call(blocks, rows, local, served, first, number, last_dims):
    wide, inner = last_dims
    tokens = blocks * rows

    def body(at_ref, *refs):
        acts, grads = refs[:blocks], refs[blocks : 2 * blocks]
        slot_ref, hit_ref, router_ref, wg_ref, wu_ref, wd_ref = refs[2 * blocks : 2 * blocks + 6]
        gg_ref, ug_ref, dg_ref, gate_out, dgate_ref, y_ref, dx_ref = refs[2 * blocks + 6 : 2 * blocks + 13]
        gate_all, xe, gyx, dye = refs[2 * blocks + 13 :]
        e = pl.program_id(0)

        @pl.when(e == 0)
        def _():
            for s in range(blocks):
                part = slice(s * rows, (s + 1) * rows)
                logits = dot_nt(router_ref[...], acts[s][...])
                hit = hit_ref[:, part] > 0
                logits = jnp.where(hit, logits, NEG)
                top = jnp.max(logits, axis=0, keepdims=True)
                raised = jnp.where(hit, jnp.exp(logits - top), 0.0)
                gates = raised / jnp.sum(raised, axis=0, keepdims=True)
                gate_all[:, part] = gates
                if s == 0:
                    gate_out[...] = gates

        slot_row = slot_ref[0]
        gate_row = gate_all[pl.ds(at_ref[1] + e, 1), :]
        slot_id = lax.broadcasted_iota(jnp.int32, (CAP, rows), 0)
        slot_gates = []
        for s in range(blocks):
            part = slice(s * rows, (s + 1) * rows)
            put = slice(s * CAP, (s + 1) * CAP)
            hits = slot_id == slot_row[:, part]
            pick = jnp.where(hits, 1.0, 0.0).astype(BF16)
            gate = jnp.sum(jnp.where(hits, gate_row[:, part], 0.0), axis=1, keepdims=True)
            slot_gates.append(gate)
            xe[put, :] = dot_nn(pick, acts[s][...]).astype(BF16)
            picked = dot_nn(pick, grads[s][...])
            gyx[put, :] = picked.astype(BF16)
            dye[put, :] = (gate * picked).astype(BF16)
        gate_part = dot_nn(xe[...], wg_ref[0])
        up_part = dot_nn(xe[...], wu_ref[0])
        sig = jax.nn.sigmoid(gate_part)
        act = gate_part * sig
        hidden = (act * up_part).astype(BF16)
        out = dot_nn(hidden, wd_ref[0]).astype(BF16).astype(F32)
        slot_dot = jnp.sum(gyx[...].astype(F32) * out, axis=1, keepdims=True)
        for s in range(blocks):
            part = slice(s * rows, (s + 1) * rows)
            put = slice(s * CAP, (s + 1) * CAP)
            hits = slot_id == slot_row[:, part]
            dgate_ref[0, :, part] = jnp.sum(jnp.where(hits, slot_dot[put], 0.0), axis=0, keepdims=True)
            y_ref[0, put, :] = (slot_gates[s] * out[put]).astype(BF16)
        dg_ref[0] = dot_tn(hidden, dye[...]).astype(BF16)
        grad_hidden = dot_nt(dye[...], wd_ref[0])
        grad_gate = (grad_hidden * up_part * sig * (1.0 + gate_part * (1.0 - sig))).astype(BF16)
        grad_up = (grad_hidden * act).astype(BF16)
        gg_ref[0] = dot_tn(xe[...], grad_gate).astype(BF16)
        ug_ref[0] = dot_tn(xe[...], grad_up).astype(BF16)
        dx_ref[0] = (dot_nt(grad_gate, wg_ref[0]) + dot_nt(grad_up, wu_ref[0])).astype(BF16)

    def whole(*shape):
        return pl.BlockSpec(
            shape, lambda e, at: tuple(0 for _ in shape), pipeline_mode=pl.Buffered(1)
        )

    def each(*shape):
        return pl.BlockSpec((1,) + shape, lambda e, at: (e,) + tuple(0 for _ in shape))

    def weight(*shape):
        return pl.BlockSpec((1,) + shape, lambda e, at: (at[0] + e,) + tuple(0 for _ in shape))

    shape = jax.ShapeDtypeStruct
    return pl.pallas_call(
        body,
        cost_estimate=pl.CostEstimate(
            flops=number * blocks * CAP * wide * (18 * inner + 4 * rows),
            transcendentals=0,
            bytes_accessed=number * 12 * wide * inner + 4 * blocks * rows * wide,
        ),
        grid_spec=pltpu.PrefetchScalarGridSpec(
            num_scalar_prefetch=1,
            grid=(number,),
            in_specs=[whole(rows, wide) for _ in range(2 * blocks)]
            + [
                pl.BlockSpec((1, 1, tokens), lambda e, at: (first + e, 0, 0)),
                whole(EXPERTS, tokens),
                whole(EXPERTS, wide),
                weight(wide, inner),
                weight(wide, inner),
                weight(inner, wide),
            ],
            out_specs=[
                each(wide, inner),
                each(wide, inner),
                each(inner, wide),
                pl.BlockSpec((EXPERTS, rows), lambda e, at: (0, 0)),
                each(1, tokens),
                each(blocks * CAP, wide),
                each(blocks * CAP, wide),
            ],
            scratch_shapes=[
                pltpu.VMEM((EXPERTS, tokens), F32),
                pltpu.VMEM((blocks * CAP, wide), BF16),
                pltpu.VMEM((blocks * CAP, wide), BF16),
                pltpu.VMEM((blocks * CAP, wide), BF16),
            ],
        ),
        out_shape=[
            shape((number, wide, inner), BF16),
            shape((number, wide, inner), BF16),
            shape((number, inner, wide), BF16),
            shape((EXPERTS, rows), F32),
            shape((number, 1, tokens), F32),
            shape((number, blocks * CAP, wide), BF16),
            shape((number, blocks * CAP, wide), BF16),
        ],
        compiler_params=pltpu.CompilerParams(
            vmem_limit_bytes=56 << 20, dimension_semantics=("arbitrary",)
        ),
    )


def combine_body(blocks, rows, groups):
    def body(slot_ref, *refs):
        parts, outs = refs[: len(groups)], refs[len(groups) :]
        slot_id = lax.broadcasted_iota(jnp.int32, (CAP, rows), 0)
        for s in range(blocks):
            picks, slots = [], []
            for g, (first, number) in enumerate(groups):
                for e in range(number):
                    hits = slot_id == slot_ref[first + e, :, s * rows : (s + 1) * rows]
                    picks.append(jnp.where(hits, 1.0, 0.0).astype(BF16))
                    slots.append(parts[g][e, s * CAP : (s + 1) * CAP, :])
            outs[s][...] = dot_tn(
                jnp.concatenate(picks, axis=0), jnp.concatenate(slots, axis=0)
            ).astype(BF16)

    return body


def store_pair(held, here, there, places, total):
    rows, cols = here.shape

    def body(at_ref, here_ref, there_ref, *rest):
        out_ref = rest[-1]

        @pl.when(pl.program_id(0) == 0)
        def _():
            out_ref[0] = here_ref[...].astype(F32)

        @pl.when(pl.program_id(0) == 1)
        def _():
            out_ref[0] = there_ref[...].astype(F32)

    more = [] if held is None else [held]
    return pl.pallas_call(
        body,
        grid_spec=pltpu.PrefetchScalarGridSpec(
            num_scalar_prefetch=1,
            grid=(2,),
            in_specs=[pl.BlockSpec((rows, cols), lambda i, at: (0, 0))] * 2
            + [pl.BlockSpec(memory_space=pl.ANY)] * len(more),
            out_specs=pl.BlockSpec((1, rows, cols), lambda i, at: (at[i], 0, 0)),
        ),
        out_shape=jax.ShapeDtypeStruct((total, rows, cols), F32),
        input_output_aliases={3: 0} if more else {},
        compiler_params=pltpu.CompilerParams(
            vmem_limit_bytes=24 << 20, dimension_semantics=("arbitrary",)
        ),
    )(places, here, there, *more)


TO_INNER = [(0, 2), (1, 3), (6, 4), (7, 5)]
ACROSS = [(2, 4), (3, 5), (4, 2), (5, 3)]
TO_OUTER = [(2, 0), (3, 1), (4, 6), (5, 7)]


def tie(value, marks):
    return lax.optimization_barrier((value, marks))[0] if marks else value


def line_step(outer, came, block, part, across, following, sent):
    want_part, want_sent, want_done = block is not None, part is not None, sent is not None
    given = [came] + [a for a in (block, part, across, following, sent) if a is not None]
    outs = want_part + want_sent + want_done

    def body(outer_ref, *refs):
        ins, out = list(refs[: len(given)]), list(refs[len(given) :])
        came_ref = ins.pop(0)
        block_ref = ins.pop(0) if want_part else None
        part_ref, across_ref = (ins.pop(0), ins.pop(0)) if want_sent else (None, None)
        following_ref = ins.pop(0) if following is not None else None
        sent_ref = ins.pop(0) if want_done else None
        part_out = out.pop(0) if want_part else None
        sent_out = out.pop(0) if want_sent else None
        done_out = out.pop(0) if want_done else None

        @pl.when(outer_ref[0] == 0)
        def _():
            if want_part:
                part_out[...] = block_ref[...] + came_ref[...]
            if want_sent:
                sent_out[...] = part_ref[...] + across_ref[...]
            if want_done:
                done_out[...] = sent_ref[...]

        @pl.when(outer_ref[0] == 1)
        def _():
            if following is not None:
                sent_out[...] = following_ref[...]
            if want_done:
                done_out[...] = came_ref[...]

    res = call(body, [outer], given, [(came.shape, BF16)] * outs, mib=24)
    res = list(res)
    return [res.pop(0) if w else None for w in (want_part, want_sent, want_done)]


class LineSums:
    LAG = 3

    def __init__(self, me, beside, base, base_there, total):
        self.outer = ((me < 2) | (me >= 6)).astype(jnp.int32).reshape(1)
        self.beside, self.base, self.base_there, self.total = beside, base, base_there, total
        self.blocks, self.held = [], [None, None, None]
        self.sent, self.parts, self.across = {}, [], []
        self.swaps, self.marks, self.done = [], [], 0

    def feed(self, results):
        for e in range(results[0].shape[0]):
            self.blocks += [results[m][e] for m in range(3)]

    def store(self):
        if self.done < len(self.swaps):
            here, there = self.swaps[self.done]
            e, m = divmod(self.done, 3)
            places = jnp.stack([self.base + e, self.base_there + e])
            self.held[m] = store_pair(self.held[m], here, there, places, self.total)
            self.done += 1

    def step(self, after=()):
        t, count = len(self.marks), len(self.blocks)
        new, old = t < count, t >= self.LAG
        sent = self.sent[t] if old else self.blocks[t]
        kept = [h for h in self.held if h is not None]
        sent, kept, _ = lax.optimization_barrier((sent, kept, list(after)))
        self.held[: len(kept)] = kept
        came = lax.ppermute(sent, "ctx", (TO_INNER if new else []) + (TO_OUTER if old else []))
        self.marks.append(came)
        turn_back = 0 < t <= count
        shape = self.blocks[t % 3].shape
        more = turn_back and t + 2 < count
        part, _, finished = line_step(
            self.outer, came, self.blocks[t] if new else None, None, None, None, sent if old else None
        ) if new or old else (None, None, None)
        if turn_back:
            _, self.sent[t + 2], _ = line_step(
                self.outer, self.across[t - 1], None, self.parts[t - 1], self.across[t - 1],
                self.blocks[t + 2] if more else None, None,
            )
        if new:
            self.parts.append(part)
            self.across.append(lax.ppermute(part, "ctx", ACROSS))
        if len(self.swaps) > 1:
            self.store()
        if old:
            self.swaps.append((finished, lax.ppermute(finished, "ctx", self.beside)))

    def hold(self, value, step):
        return tie(value, self.marks[step : step + 1] + self.across[max(step - 1, 0) : step])

    def finish(self):
        while self.done < len(self.swaps):
            self.store()
        return self.held


def after_body(count):
    def body(
        me_ref, mixed_ref, ga_ref, gy_ref, gain_ref, gates_ref, dgate_ref, router_ref, act_ref, o_ref,
        *rest,
    ):
        weights = rest[:count]
        gy1_ref, go_ref, rgrad_ref, ggrad_ref = rest[count : count + 4]
        wgrads = rest[count + 4 : 2 * count + 4]
        parts, gparts = rest[2 * count + 4 :]
        gates, dgate = gates_ref[...], dgate_ref[...]
        dlogits = gates * (dgate - jnp.sum(gates * dgate, axis=0, keepdims=True))
        dlogits = dlogits.astype(BF16)
        grad = ga_ref[...] + dot_tn(dlogits, router_ref[...])
        rgrad_ref[...] = dot_nn(dlogits, act_ref[...])
        mixed = mixed_ref[...]
        inverse = lax.rsqrt(jnp.mean(mixed * mixed, axis=-1, keepdims=True) + EPS)
        normed = mixed * inverse
        ggrad_ref[...] = jnp.sum(grad * normed, axis=0, keepdims=True)
        gy1 = gy_ref[...] + norm_back(grad, normed, inverse, gain_ref[...])
        gy1_ref[...] = gy1
        low = gy1.astype(BF16)
        me = me_ref[0]
        width = o_ref.shape[1] // count
        for b in range(count):
            parts[b] = o_ref[:, b * width : (b + 1) * width]
        for s in range(count):
            gparts[me ^ s] = dot_nt(low, weights[s][...]).astype(BF16)
            wgrads[s][...] = dot_tn(parts[me ^ s], low).astype(BF16)
        for b in range(count):
            go_ref[:, b * width : (b + 1) * width] = gparts[b]

    return body


def first_body(count):
    def body(me_ref, x_ref, gain_ref, cos_ref, sin_ref, act_ref, gq_ref, dkv_ref, gy1_ref, *rest):
        wq, wkv = rest[:count], rest[count : 2 * count]
        in_ref, ggrad_ref = rest[2 * count : 2 * count + 2]
        qgrads = rest[2 * count + 2 : 3 * count + 2]
        kgrads = rest[3 * count + 2 : 4 * count + 2]
        gkv, gparts = rest[4 * count + 2 :]
        rows = x_ref.shape[0]
        first = (lanes_of(rows) & 63) < 32
        cosine, sine = cos_ref[...], sin_ref[...]
        for j in range(KVD // 128):
            tile = dkv_ref[:, j * 128 : (j + 1) * 128].astype(F32)
            gkv[:, j * 128 : (j + 1) * 128] = turn_back(tile, cosine, sine, first).astype(BF16)
        gkv[:, KVD:] = dkv_ref[:, KVD:].astype(BF16)
        me = me_ref[0]
        gq = gq_ref[...]
        for s in range(count):
            gparts[me ^ s] = dot_nt(gq, wq[s][...]) + dot_nt(gkv[...], wkv[s][...])
            qgrads[s][...] = dot_tn(act_ref[me ^ s], gq).astype(BF16)
            kgrads[s][...] = dot_tn(act_ref[me ^ s], gkv[...]).astype(BF16)
        grad = jnp.concatenate([gparts[b] for b in range(count)], axis=1)
        x = x_ref[...].astype(F32)
        inverse = lax.rsqrt(jnp.mean(x * x, axis=-1, keepdims=True) + EPS)
        normed = x * inverse
        ggrad_ref[...] = jnp.sum(grad * normed, axis=0, keepdims=True)
        in_ref[...] = gy1_ref[...] + norm_back(grad, normed, inverse, gain_ref[...])

    return body


def make(n_dp, n_ctx):
    def on_device(
        layer_input, query_weight, key_weight, value_weight, out_weight, attn_gain, router_weight,
        moe_gain, gate_weight, up_weight, down_weight, expert_ids, fill_order, block_deal,
        seq_lengths, out_grad,
    ):
        rows, wide = layer_input.shape
        local = gate_weight.shape[0]
        width = wide // n_dp
        me_dp = lax.axis_index("dp").astype(jnp.int32)
        me_ctx = lax.axis_index("ctx").astype(jnp.int32)
        me = me_dp.reshape(1)
        near = rows // BLOCK

        pairs = n_ctx == 8 and local % 2 == 0
        served = local // 2 if pairs else local
        beside = xor_pairs(n_ctx, 1)
        column = me_ctx & 1 if pairs else jnp.zeros((), jnp.int32)
        grad_low = out_grad.astype(BF16)
        grad_beside = lax.ppermute(grad_low, "ctx", beside) if pairs else None
        wkv = dp_gather(jnp.concatenate([key_weight, value_weight], axis=1), n_dp)
        small = jnp.concatenate(
            [
                router_weight.T,
                attn_gain[None, :],
                moe_gain[None, :],
                jnp.zeros((14, width), BF16),
            ],
            axis=0,
        )
        small = in_order(dp_gather(small, n_dp), me_dp)
        small = small.transpose(1, 0, 2).reshape(EXPERTS + 16, wide)
        router_t = small[:EXPERTS]
        gain_one = small[EXPERTS : EXPERTS + 1].astype(F32)
        gain_two = small[EXPERTS + 1 : EXPERTS + 2].astype(F32)
        wq = dp_gather(query_weight, n_dp)

        deal, lengths = block_deal[0], seq_lengths[0]
        blocks = deal.shape[0]
        ends = jnp.cumsum(lengths, dtype=jnp.int32)
        mine = lax.dynamic_slice_in_dim(deal, me_ctx * near, near)
        places = (mine[:, None] * BLOCK + jnp.arange(BLOCK, dtype=jnp.int32)[None, :]).reshape(rows, 1)
        starts = jnp.sum(
            jnp.where(places >= ends[None, :], lengths[None, :], 0), axis=1, keepdims=True, dtype=jnp.int32
        )
        relative = (places - starts).astype(F32)
        lane = jnp.arange(128, dtype=jnp.int32)
        inverse = 10000.0 ** (-(lane % 32).astype(F32) * (2.0 / HEAD))
        angles = relative * inverse[None, :]
        cosine = jnp.cos(angles)
        sine = jnp.sin(angles) * jnp.where(lane % 64 < 32, -1.0, 1.0)[None, :]
        block_starts = jnp.sum(
            jnp.where((mine * BLOCK)[:, None] >= ends[None, :], lengths[None, :], 0), axis=1, dtype=jnp.int32
        )
        low_blocks = block_starts // BLOCK
        ring = jnp.array(ring_order(n_ctx)[0], jnp.int32)
        ring_deal = deal.reshape(n_ctx, near)[ring].reshape(blocks)
        held = jnp.arange(blocks, dtype=jnp.int32)
        where_block = jnp.sum(
            jnp.where(ring_deal[None, :] == held[:, None], held[None, :], 0), axis=1, dtype=jnp.int32
        )

        kv_mine, act_one = call(
            kv_body(n_dp),
            [me],
            [tie(layer_input, [grad_beside] if pairs else []), gain_one, cosine, sine] + wkv,
            [((rows, 2 * KVD), BF16), ((n_dp, rows, width), BF16)],
        )
        every_kv = ring_gather(kv_mine, n_ctx)
        (query,) = call(query_body(n_dp), [me], [act_one, cosine, sine] + wq, [((rows, wide), BF16)])
        wo = dp_gather(out_weight, n_dp)

        def reach(block):
            pieces = dp_gather(block, n_dp)
            if pairs:
                pieces = pieces + dp_gather(lax.ppermute(block, "ctx", beside), n_dp)
            return pieces

        table = jnp.concatenate([expert_ids.T, fill_order], axis=0)
        table = jnp.stack(reach(table))
        ids, fill = table[:, :-1], table[:, -1]
        held_blocks = table.shape[0]
        names = jnp.arange(EXPERTS, dtype=jnp.int32)
        hits = jnp.sum((ids[:, :, None, :] == names[None, None, :, None]).astype(F32), axis=1)
        earlier = (fill[:, :, None] < fill[:, None, :]).astype(BF16)
        prior = jnp.einsum(
            "set,stu->seu", hits.astype(BF16), earlier, preferred_element_type=F32
        )
        slot = jnp.where((hits > 0) & (prior < CAP), prior, -1.0).astype(jnp.int32)
        base = column * served
        slot = lax.dynamic_slice_in_dim(slot, me_dp * local + base, served, axis=1)
        slots_t = slot.transpose(1, 0, 2).reshape(served, 1, held_blocks * rows)
        hits_t = hits.transpose(1, 0, 2).reshape(EXPERTS, held_blocks * rows)
        grads_all = dp_gather(grad_low, n_dp)
        if pairs:
            grads_all = grads_all + dp_gather(grad_beside, n_dp)
        query, grads_all, wo = lax.optimization_barrier((query, grads_all, wo))

        attended, extended = call(
            attend_body,
            [low_blocks, mine, where_block],
            [query, every_kv, starts],
            [((rows, wide), BF16), ((PAIRS, 4, rows, 128), F32)],
            [
                pltpu.VMEM((PAIRS, 4 * BLOCK, 128), BF16),
                pltpu.VMEM((PAIRS, 4 * BLOCK, 128), F32),
                pltpu.VMEM((PAIRS, 4 * BLOCK, 128), F32),
                pltpu.VMEM((PAIRS, 4 * BLOCK, 128), F32),
            ],
            flops=rows * blocks * BLOCK * wide * 4,
        )
        mixed, act_two = call(
            mix_body(n_dp),
            [me],
            [layer_input, attended, gain_two] + wo,
            [((rows, wide), F32), ((rows, wide), BF16)],
            [pltpu.VMEM((n_dp, rows, width), BF16)],
        )

        acts_all = reach(act_two)
        groups = [(0, 1), (1, served - 1)] if pairs else [(0, served)]
        results = []
        line = LineSums(me_ctx, beside, base, (1 - column) * served, local) if pairs else None

        def step(*after):
            if pairs:
                line.step(after)

        def hold(value, step):
            return line.hold(value, step) if pairs else value

        for first, number in groups:
            at = jnp.stack([base + first, me_dp * local + base + first])
            results.append(
                expert_call(
                    held_blocks, rows, local, served, first, number, gate_weight.shape[1:]
                )(
                    at, *acts_all, *grads_all, slots_t, hits_t, router_t, gate_weight, up_weight,
                    down_weight,
                )
            )
            if pairs:
                line.feed(results[-1])
            step(*[res[4] for res in results[1:]])
        gates = results[0][3]

        def combine(index, after):
            return call(
                combine_body(held_blocks, rows, groups),
                [],
                [tie(slots_t, after)] + [res[index] for res in results],
                [((rows, wide), BF16)] * held_blocks,
            )

        def settle(parts, between):
            kept = [dp_cores(parts[s : s + n_dp], n_dp) for s in range(0, held_blocks, n_dp)]
            between(kept)
            totals = [dp_rest(k, n_dp) for k in kept]
            between(totals)
            if pairs:
                totals[0] = totals[0] + lax.ppermute(
                    totals[1].astype(BF16), "ctx", beside
                ).astype(F32)
            return totals[0]

        dgates = jnp.concatenate([res[4] for res in results], axis=0)[:, 0]
        back = [dgates[:, s * rows : (s + 1) * rows] for s in range(held_blocks)]
        if pairs:
            other = lax.ppermute(jnp.stack(back[n_dp:]), "ctx", beside)
            own = jnp.stack(back[:n_dp])
            back = jnp.where(
                column == 0,
                jnp.concatenate([own, other], axis=1),
                jnp.concatenate([other, own], axis=1),
            )
        back = [back[0]] + [lax.ppermute(back[s], "dp", xor_pairs(n_dp, s)) for s in range(1, n_dp)]
        dgate_t = in_order(back, me_dp).reshape(EXPERTS, rows)
        g_parts = combine(6, line.marks[:1] if pairs else [])
        grad_act_two = settle(g_parts, lambda values: None)
        step(grad_act_two)
        res = call(
            after_body(n_dp),
            [me],
            [mixed, hold(grad_act_two, 1), out_grad, gain_two, gates, dgate_t, router_t, act_two, attended] + wo,
            [((rows, wide), F32), ((rows, wide), BF16), ((EXPERTS, wide), F32), ((1, wide), F32)]
            + [((width, wide), BF16)] * n_dp,
            [pltpu.VMEM((n_dp, rows, width), BF16), pltpu.VMEM((n_dp, rows, width), BF16)],
        )
        grad_mixed, grad_heads, router_part, gain_two_part = res[:4]
        out_parts = res[4:]
        grad_query, kv_grads = call(
            attend_back_body,
            [low_blocks, mine, where_block],
            [query, every_kv, starts, grad_heads, extended, cosine, sine],
            [((rows, wide), BF16), ((blocks * BLOCK, 2 * KVD), BF16)],
            [
                pltpu.VMEM((PAIRS, 4 * BLOCK, 128), BF16),
                pltpu.VMEM((PAIRS, 4 * BLOCK, 128), BF16),
                pltpu.VMEM((PAIRS, 4 * BLOCK, 128), F32),
                pltpu.VMEM((PAIRS, 4 * BLOCK, 128), F32),
                pltpu.VMEM((PAIRS, 4 * BLOCK, 128), F32),
                pltpu.VMEM((blocks * BLOCK, 2 * KVD), F32),
            ],
            flops=rows * blocks * BLOCK * wide * 10,
        )
        step(grad_query)
        kv_grad = ring_scatter(hold(kv_grads, 2), n_ctx)
        y_parts = combine(5, [grad_query])
        y_total = settle(y_parts, lambda values: None)
        layer_output = mixed + y_total
        dense_out = dp_reduce(out_parts, n_dp).astype(BF16)
        step(layer_output)
        res = call(
            first_body(n_dp),
            [me],
            [layer_input, gain_one, cosine, sine, act_one, grad_query, kv_grad, grad_mixed] + wq + wkv,
            [((rows, wide), F32), ((1, wide), F32)]
            + [((width, wide), BF16)] * n_dp
            + [((width, 2 * KVD), BF16)] * n_dp,
            [pltpu.VMEM((rows, 2 * KVD), BF16), pltpu.VMEM((n_dp, rows, width), F32)],
        )
        input_grad, gain_one_part = res[:2]
        q_parts, kv_parts = res[2 : 2 + n_dp], res[2 + n_dp :]
        step(gain_one_part)

        dense_q = dp_reduce(q_parts, n_dp).astype(BF16)
        dense_kv = dp_reduce(kv_parts, n_dp).astype(BF16)
        dense = jnp.concatenate([dense_out, dense_q, dense_kv], axis=0)
        dense = ring_gather(ring_scatter(dense, n_ctx), n_ctx).astype(F32)
        tiny = jnp.concatenate([router_part, gain_one_part, gain_two_part], axis=0)
        for bit in [1 << b for b in range(n_ctx.bit_length() - 1)]:
            tiny = tiny + lax.ppermute(tiny, "ctx", xor_pairs(n_ctx, bit))
        for bit in [1 << b for b in range(n_dp.bit_length() - 1)]:
            tiny = tiny + lax.ppermute(tiny, "dp", xor_pairs(n_dp, bit))
        tiny = lax.dynamic_slice_in_dim(tiny, me_dp * width, width, axis=1)
        if pairs:
            while len(line.marks) < len(line.blocks) + line.LAG:
                line.step()
            expert_sums = line.finish()
        else:
            expert_sums = [
                ring_gather(ring_scatter(g.reshape(-1, g.shape[2]), n_ctx), n_ctx)
                .reshape(g.shape)
                .astype(F32)
                for g in results[0][:3]
            ]
        return (
            layer_output,
            input_grad,
            dense[width : 2 * width],
            dense[2 * width :, :KVD],
            dense[2 * width :, KVD:],
            dense[:width],
            tiny[EXPERTS],
            tiny[:EXPERTS].T,
            tiny[EXPERTS + 1],
            expert_sums[0],
            expert_sums[1],
            expert_sums[2],
        )

    return on_device


def solution(mesh):
    rows2 = P(("dp", "ctx"), None)
    mat = P("dp", None)
    cube = P("dp", None, None)
    in_specs = (
        rows2, mat, mat, mat, mat, P("dp"), mat, P("dp"), cube, cube, cube, rows2, rows2, mat, mat, rows2,
    )
    out_specs = (rows2, rows2, mat, mat, mat, mat, P("dp"), mat, P("dp"), cube, cube, cube)
    return jax.shard_map(
        make(mesh.shape["dp"], mesh.shape["ctx"]),
        mesh=mesh,
        in_specs=in_specs,
        out_specs=out_specs,
        check_vma=False,
    )
```

```python
import math

import jax
import jax.numpy as jnp
from jax import lax
from jax.experimental import pallas as pl
from jax.experimental.pallas import tpu as pltpu
from jax.sharding import PartitionSpec as P

EXPERTS = 32
BLOCK = 128
CAP = 64
HEAD = 64
KVD = 512
PAIRS = 4
EPS = 1e-06
NEG = -1e30
F32 = jnp.float32
BF16 = jnp.bfloat16


def dot_nn(a, b):
    return lax.dot_general(a, b, (((1,), (0,)), ((), ())), preferred_element_type=F32)


def dot_nt(a, b):
    return lax.dot_general(a, b, (((1,), (1,)), ((), ())), preferred_element_type=F32)


def dot_tn(a, b):
    return lax.dot_general(a, b, (((0,), (0,)), ((), ())), preferred_element_type=F32)


def vmem():
    return pl.BlockSpec(memory_space=pltpu.VMEM)


def smem():
    return pl.BlockSpec(memory_space=pltpu.SMEM)


def cost(flops, arrays, outs):
    moved = sum(a.size * a.dtype.itemsize for a in arrays)
    moved += sum(math.prod(s) * jnp.dtype(d).itemsize for s, d in outs)
    return pl.CostEstimate(flops=flops, transcendentals=0, bytes_accessed=moved)


def call(body, scalars, arrays, outs, scratch=(), mib=48, flops=0):
    return pl.pallas_call(
        body,
        cost_estimate=cost(flops, arrays, outs),
        in_specs=[smem() for _ in scalars] + [vmem() for _ in arrays],
        out_specs=[vmem() for _ in outs],
        out_shape=[jax.ShapeDtypeStruct(s, d) for s, d in outs],
        scratch_shapes=list(scratch),
        compiler_params=pltpu.CompilerParams(vmem_limit_bytes=mib << 20),
    )(*scalars, *arrays)


def xor_pairs(count, step):
    return [(i, i ^ step) for i in range(count)]


def dp_gather(block, count):
    pieces = {0: block}
    for step in range(2, count, 2):
        pieces[step] = lax.ppermute(block, "dp", xor_pairs(count, step))
    for step in range(0, count, 2):
        pieces[step + 1] = lax.ppermute(pieces[step], "dp", xor_pairs(count, 1))
    return [pieces[s] for s in range(count)]


def dp_cores(pieces, count):
    kept = []
    for step in range(0, count, 2):
        other = lax.ppermute(pieces[step + 1], "dp", xor_pairs(count, 1))
        kept.append((pieces[step].astype(F32) + other.astype(F32)).astype(BF16))
    return kept


def dp_rest(kept, count):
    total = kept[0].astype(F32)
    for i in range(1, len(kept)):
        other = lax.ppermute(kept[i], "dp", xor_pairs(count, 2 * i))
        total = total + other.astype(F32)
    return total


def dp_reduce(pieces, count):
    return dp_rest(dp_cores(pieces, count), count)


def in_order(pieces, index):
    stacked = jnp.stack(pieces)
    count = len(pieces)
    bit = 1
    while bit < count:
        swapped = jnp.stack([stacked[j ^ bit] for j in range(count)])
        stacked = jnp.where((index & bit) > 0, swapped, stacked)
        bit *= 2
    return stacked


def ring_order(count):
    return [list(range(0, count, 2)) + list(range(count - 1, 0, -2))]


def ring_gather(block, count):
    return lax.all_gather(block, "ctx", axis=0, tiled=True, axis_index_groups=ring_order(count))


def ring_scatter(block, count):
    return lax.psum_scatter(
        block, "ctx", scatter_dimension=0, tiled=True, axis_index_groups=ring_order(count)
    )


def half_swap(tile, first):
    return jnp.where(first, pltpu.roll(tile, 96, 1), pltpu.roll(tile, 32, 1))


def turn(tile, cosine, sine, first):
    return tile * cosine + half_swap(tile, first) * sine


def turn_back(tile, cosine, sine, first):
    return tile * cosine - half_swap(tile, first) * sine


def lanes_of(rows):
    return lax.broadcasted_iota(jnp.int32, (rows, 128), 1)


def spread_heads(tile_a, tile_b):
    low = lanes_of(tile_a.shape[0]) < HEAD
    return jnp.concatenate(
        [
            jnp.where(low, tile_a, 0.0),
            jnp.where(low, pltpu.roll(tile_a, HEAD, 1), 0.0),
            jnp.where(low, 0.0, pltpu.roll(tile_b, HEAD, 1)),
            jnp.where(low, 0.0, tile_b),
        ],
        axis=0,
    )


def join_heads(stacked):
    rows = stacked.shape[0] // 4
    low = lanes_of(rows) < HEAD
    part = [stacked[h * rows : (h + 1) * rows] for h in range(4)]
    return (
        jnp.where(low, part[0], pltpu.roll(part[1], HEAD, 1)),
        jnp.where(low, pltpu.roll(part[2], HEAD, 1), part[3]),
    )


def norm_back(grad, normed, inverse, gain):
    scaled = grad * gain
    return inverse * (scaled - normed * jnp.mean(scaled * normed, axis=-1, keepdims=True))


def kv_body(count):
    def body(me_ref, x_ref, gain_ref, cos_ref, sin_ref, *rest):
        weights, (kv_ref, act_ref) = rest[:count], rest[count:]
        x = x_ref[...].astype(F32)
        inverse = lax.rsqrt(jnp.mean(x * x, axis=-1, keepdims=True) + EPS)
        act = (x * inverse * gain_ref[...]).astype(BF16)
        width = x.shape[1] // count
        for b in range(count):
            act_ref[b] = act[:, b * width : (b + 1) * width]
        me = me_ref[0]
        total = dot_nn(act_ref[me], weights[0][...])
        for s in range(1, count):
            total = total + dot_nn(act_ref[me ^ s], weights[s][...])
        first = (lanes_of(x.shape[0]) & 63) < 32
        cosine, sine = cos_ref[...], sin_ref[...]
        for j in range(KVD // 128):
            tile = total[:, j * 128 : (j + 1) * 128]
            kv_ref[:, j * 128 : (j + 1) * 128] = turn(tile, cosine, sine, first).astype(BF16)
        kv_ref[:, KVD:] = total[:, KVD:].astype(BF16)

    return body


def query_body(count):
    def body(me_ref, act_ref, cos_ref, sin_ref, *rest):
        weights, q_ref = rest[:count], rest[count]
        me = me_ref[0]
        total = dot_nn(act_ref[me], weights[0][...])
        for s in range(1, count):
            total = total + dot_nn(act_ref[me ^ s], weights[s][...])
        first = (lanes_of(total.shape[0]) & 63) < 32
        cosine, sine = cos_ref[...], sin_ref[...]
        for j in range(total.shape[1] // 128):
            tile = total[:, j * 128 : (j + 1) * 128]
            turned = turn(tile, cosine, sine, first).astype(BF16)
            q_ref[:, j * 128 : (j + 1) * 128] = turned * (1.0 / HEAD)

    return body


def visible(place_block, key_block, starts):
    rows = lax.broadcasted_iota(jnp.int32, (BLOCK, BLOCK), 0) + place_block * BLOCK
    keys = lax.broadcasted_iota(jnp.int32, (BLOCK, BLOCK), 1) + key_block * BLOCK
    return (keys <= rows) & (keys >= starts)


def attend_body(low_ref, high_ref, where_ref, q_ref, kv_ref, starts_ref, o_ref, ext_ref, qs, tops, sums, accs):
    low_half = lanes_of(BLOCK) < HEAD
    for qb in range(q_ref.shape[0] // BLOCK):
        rows = slice(qb * BLOCK, (qb + 1) * BLOCK)
        for j in range(PAIRS):
            qs[j] = spread_heads(
                q_ref[rows, 256 * j : 256 * j + 128].astype(F32),
                q_ref[rows, 256 * j + 128 : 256 * j + 256].astype(F32),
            ).astype(BF16)
        tops[...] = jnp.full(tops.shape, NEG, F32)
        sums[...] = jnp.zeros(sums.shape, F32)
        accs[...] = jnp.zeros(accs.shape, F32)
        low, high = low_ref[qb], high_ref[qb]

        def scores_of(b, at, seen, j):
            key = kv_ref[pl.ds(at, BLOCK), 128 * j : 128 * j + 128]
            scores = dot_nt(qs[j], key).reshape(4, BLOCK, BLOCK)
            return jnp.where(seen, scores, NEG).reshape(4 * BLOCK, BLOCK)

        def find_top(b, carry):
            at = pl.multiple_of(where_ref[b] * BLOCK, BLOCK)
            seen = visible(high, b, starts_ref[rows, :])[None]
            for j in range(PAIRS):
                tops[j] = jnp.maximum(tops[j], scores_of(b, at, seen, j))
            return carry

        lax.fori_loop(low, high + 1, find_top, 0)
        for j in range(PAIRS):
            top = jnp.max(tops[j], axis=-1, keepdims=True)
            tops[j] = jnp.broadcast_to(top, tops.shape[1:])

        def gather_values(b, carry):
            at = pl.multiple_of(where_ref[b] * BLOCK, BLOCK)
            seen = visible(high, b, starts_ref[rows, :])[None]
            for j in range(PAIRS):
                value = kv_ref[pl.ds(at, BLOCK), KVD + 128 * j : KVD + 128 * j + 128]
                weights = jnp.exp(scores_of(b, at, seen, j) - tops[j])
                sums[j] += weights
                accs[j] += dot_nn(weights.astype(BF16), value)
            return carry

        lax.fori_loop(low, high + 1, gather_values, 0)
        for j in range(PAIRS):
            weight = jnp.sum(sums[j], axis=-1, keepdims=True)
            attended = accs[j] / weight
            total = tops[j] + jnp.log(weight)
            left, right = join_heads(attended)
            o_ref[rows, 256 * j : 256 * j + 128] = left.astype(BF16)
            o_ref[rows, 256 * j + 128 : 256 * j + 256] = right.astype(BF16)
            for h in range(4):
                part = slice(h * BLOCK, (h + 1) * BLOCK)
                keep = low_half if h < 2 else jnp.logical_not(low_half)
                ext_ref[j, h, rows, :] = jnp.where(keep, attended[part], total[part])


def attend_back_body(
    low_ref, high_ref, where_ref, q_ref, kv_ref, starts_ref, go_ref, ext_ref, cos_ref, sin_ref,
    gq_ref, dkv_ref, qs, gs, ds, lse, dqs, sums,
):
    first = (lanes_of(BLOCK) & 63) < 32
    sums[...] = jnp.zeros(sums.shape, F32)
    for qb in range(q_ref.shape[0] // BLOCK):
        rows = slice(qb * BLOCK, (qb + 1) * BLOCK)
        for j in range(PAIRS):
            cols = slice(256 * j, 256 * j + 128), slice(256 * j + 128, 256 * j + 256)
            qs[j] = spread_heads(
                q_ref[rows, cols[0]].astype(F32), q_ref[rows, cols[1]].astype(F32)
            ).astype(BF16)
            grad = spread_heads(
                go_ref[rows, cols[0]].astype(F32), go_ref[rows, cols[1]].astype(F32)
            )
            gs[j] = grad.astype(BF16)
            for h in range(4):
                part = slice(h * BLOCK, (h + 1) * BLOCK)
                ext = ext_ref[j, h, rows, :]
                flat = (BLOCK, BLOCK)
                delta = jnp.sum(grad[part] * ext, axis=-1, keepdims=True)
                total = ext[:, 127:128] if h < 2 else ext[:, 0:1]
                ds[j, part, :] = jnp.broadcast_to(delta, flat)
                lse[j, part, :] = jnp.broadcast_to(total, flat)
        dqs[...] = jnp.zeros(dqs.shape, F32)
        high = high_ref[qb]

        def step(b, carry):
            at = pl.multiple_of(where_ref[b] * BLOCK, BLOCK)
            seen = visible(high, b, starts_ref[rows, :])[None]
            for j in range(PAIRS):
                kcols = slice(128 * j, 128 * j + 128)
                vcols = slice(KVD + 128 * j, KVD + 128 * j + 128)
                key = kv_ref[pl.ds(at, BLOCK), kcols]
                value = kv_ref[pl.ds(at, BLOCK), vcols]
                scores = dot_nt(qs[j], key).reshape(4, BLOCK, BLOCK)
                scores = jnp.where(seen, scores, NEG).reshape(4 * BLOCK, BLOCK)
                weights = jnp.exp(scores - lse[j])
                grad = dot_nt(gs[j], value)
                score_grad = (weights * (grad - ds[j])).astype(BF16)
                dqs[j] += dot_nn(score_grad, key)
                sums[pl.ds(at, BLOCK), kcols] += dot_tn(score_grad, qs[j])
                sums[pl.ds(at, BLOCK), vcols] += dot_tn(weights.astype(BF16), gs[j])
            return carry

        lax.fori_loop(low_ref[qb], high + 1, step, 0)
        cosine, sine = cos_ref[rows, :], sin_ref[rows, :]
        for j in range(PAIRS):
            left, right = join_heads(dqs[j] * (1.0 / HEAD))
            gq_ref[rows, 256 * j : 256 * j + 128] = turn_back(left, cosine, sine, first).astype(BF16)
            gq_ref[rows, 256 * j + 128 : 256 * j + 256] = turn_back(right, cosine, sine, first).astype(
                BF16
            )
    dkv_ref[...] = sums[...].astype(BF16)


def mix_body(count):
    def body(me_ref, x_ref, o_ref, gain_ref, *rest):
        weights, (mixed_ref, act_ref, parts) = rest[:count], rest[count:]
        width = o_ref.shape[1] // count
        for b in range(count):
            parts[b] = o_ref[:, b * width : (b + 1) * width]
        me = me_ref[0]
        total = x_ref[...].astype(F32)
        for s in range(count):
            total = total + dot_nn(parts[me ^ s], weights[s][...])
        mixed_ref[...] = total
        inverse = lax.rsqrt(jnp.mean(total * total, axis=-1, keepdims=True) + EPS)
        act_ref[...] = (total * inverse * gain_ref[...]).astype(BF16)

    return body


def expert_call(blocks, rows, local, served, first, number, last_dims):
    wide, inner = last_dims
    tokens = blocks * rows

    def body(at_ref, *refs):
        acts, grads = refs[:blocks], refs[blocks : 2 * blocks]
        slot_ref, hit_ref, router_ref, wg_ref, wu_ref, wd_ref = refs[2 * blocks : 2 * blocks + 6]
        gg_ref, ug_ref, dg_ref, gate_out, dgate_ref, y_ref, dx_ref = refs[2 * blocks + 6 : 2 * blocks + 13]
        gate_all, xe, gyx, dye = refs[2 * blocks + 13 :]
        e = pl.program_id(0)

        @pl.when(e == 0)
        def _():
            for s in range(blocks):
                part = slice(s * rows, (s + 1) * rows)
                logits = dot_nt(router_ref[...], acts[s][...])
                hit = hit_ref[:, part] > 0
                logits = jnp.where(hit, logits, NEG)
                top = jnp.max(logits, axis=0, keepdims=True)
                raised = jnp.where(hit, jnp.exp(logits - top), 0.0)
                gates = raised / jnp.sum(raised, axis=0, keepdims=True)
                gate_all[:, part] = gates
                if s == 0:
                    gate_out[...] = gates

        slot_row = slot_ref[0]
        gate_row = gate_all[pl.ds(at_ref[1] + e, 1), :]
        slot_id = lax.broadcasted_iota(jnp.int32, (CAP, rows), 0)
        slot_gates = []
        for s in range(blocks):
            part = slice(s * rows, (s + 1) * rows)
            put = slice(s * CAP, (s + 1) * CAP)
            hits = slot_id == slot_row[:, part]
            pick = jnp.where(hits, 1.0, 0.0).astype(BF16)
            gate = jnp.sum(jnp.where(hits, gate_row[:, part], 0.0), axis=1, keepdims=True)
            slot_gates.append(gate)
            xe[put, :] = dot_nn(pick, acts[s][...]).astype(BF16)
            picked = dot_nn(pick, grads[s][...])
            gyx[put, :] = picked.astype(BF16)
            dye[put, :] = (gate * picked).astype(BF16)
        gate_part = dot_nn(xe[...], wg_ref[0])
        up_part = dot_nn(xe[...], wu_ref[0])
        sig = jax.nn.sigmoid(gate_part)
        act = gate_part * sig
        hidden = (act * up_part).astype(BF16)
        out = dot_nn(hidden, wd_ref[0]).astype(BF16).astype(F32)
        slot_dot = jnp.sum(gyx[...].astype(F32) * out, axis=1, keepdims=True)
        for s in range(blocks):
            part = slice(s * rows, (s + 1) * rows)
            put = slice(s * CAP, (s + 1) * CAP)
            hits = slot_id == slot_row[:, part]
            dgate_ref[0, :, part] = jnp.sum(jnp.where(hits, slot_dot[put], 0.0), axis=0, keepdims=True)
            y_ref[0, put, :] = (slot_gates[s] * out[put]).astype(BF16)
        dg_ref[0] = dot_tn(hidden, dye[...]).astype(BF16)
        grad_hidden = dot_nt(dye[...], wd_ref[0])
        grad_gate = (grad_hidden * up_part * sig * (1.0 + gate_part * (1.0 - sig))).astype(BF16)
        grad_up = (grad_hidden * act).astype(BF16)
        gg_ref[0] = dot_tn(xe[...], grad_gate).astype(BF16)
        ug_ref[0] = dot_tn(xe[...], grad_up).astype(BF16)
        dx_ref[0] = (dot_nt(grad_gate, wg_ref[0]) + dot_nt(grad_up, wu_ref[0])).astype(BF16)

    def whole(*shape):
        return pl.BlockSpec(
            shape, lambda e, at: tuple(0 for _ in shape), pipeline_mode=pl.Buffered(1)
        )

    def each(*shape):
        return pl.BlockSpec((1,) + shape, lambda e, at: (e,) + tuple(0 for _ in shape))

    def weight(*shape):
        return pl.BlockSpec((1,) + shape, lambda e, at: (at[0] + e,) + tuple(0 for _ in shape))

    shape = jax.ShapeDtypeStruct
    return pl.pallas_call(
        body,
        cost_estimate=pl.CostEstimate(
            flops=number * blocks * CAP * wide * (18 * inner + 4 * rows),
            transcendentals=0,
            bytes_accessed=number * 12 * wide * inner + 4 * blocks * rows * wide,
        ),
        grid_spec=pltpu.PrefetchScalarGridSpec(
            num_scalar_prefetch=1,
            grid=(number,),
            in_specs=[whole(rows, wide) for _ in range(2 * blocks)]
            + [
                pl.BlockSpec((1, 1, tokens), lambda e, at: (first + e, 0, 0)),
                whole(EXPERTS, tokens),
                whole(EXPERTS, wide),
                weight(wide, inner),
                weight(wide, inner),
                weight(inner, wide),
            ],
            out_specs=[
                each(wide, inner),
                each(wide, inner),
                each(inner, wide),
                pl.BlockSpec((EXPERTS, rows), lambda e, at: (0, 0)),
                each(1, tokens),
                each(blocks * CAP, wide),
                each(blocks * CAP, wide),
            ],
            scratch_shapes=[
                pltpu.VMEM((EXPERTS, tokens), F32),
                pltpu.VMEM((blocks * CAP, wide), BF16),
                pltpu.VMEM((blocks * CAP, wide), BF16),
                pltpu.VMEM((blocks * CAP, wide), BF16),
            ],
        ),
        out_shape=[
            shape((number, wide, inner), BF16),
            shape((number, wide, inner), BF16),
            shape((number, inner, wide), BF16),
            shape((EXPERTS, rows), F32),
            shape((number, 1, tokens), F32),
            shape((number, blocks * CAP, wide), BF16),
            shape((number, blocks * CAP, wide), BF16),
        ],
        compiler_params=pltpu.CompilerParams(
            vmem_limit_bytes=56 << 20, dimension_semantics=("arbitrary",)
        ),
    )


def combine_body(blocks, rows, groups):
    def body(slot_ref, *refs):
        parts, outs = refs[: len(groups)], refs[len(groups) :]
        slot_id = lax.broadcasted_iota(jnp.int32, (CAP, rows), 0)
        for s in range(blocks):
            picks, slots = [], []
            for g, (first, number) in enumerate(groups):
                for e in range(number):
                    hits = slot_id == slot_ref[first + e, :, s * rows : (s + 1) * rows]
                    picks.append(jnp.where(hits, 1.0, 0.0).astype(BF16))
                    slots.append(parts[g][e, s * CAP : (s + 1) * CAP, :])
            outs[s][...] = dot_tn(
                jnp.concatenate(picks, axis=0), jnp.concatenate(slots, axis=0)
            ).astype(BF16)

    return body


def store_pair(held, here, there, column, e, served):
    rows, cols = here.shape
    part = rows // 4

    def body(column_ref, here_ref, there_ref, *rest):
        rest[-1][column_ref[0], 0] = here_ref[...].astype(F32)
        rest[-1][1 - column_ref[0], 0] = there_ref[...].astype(F32)

    more = [] if held is None else [held]
    return pl.pallas_call(
        body,
        cost_estimate=pl.CostEstimate(flops=0, transcendentals=0, bytes_accessed=12 * rows * cols),
        grid_spec=pltpu.PrefetchScalarGridSpec(
            num_scalar_prefetch=1,
            grid=(4,),
            in_specs=[pl.BlockSpec((part, cols), lambda i, c: (i, 0))] * 2
            + [pl.BlockSpec(memory_space=pl.ANY)] * len(more),
            out_specs=pl.BlockSpec((2, 1, part, cols), lambda i, c: (0, e, i, 0)),
        ),
        out_shape=jax.ShapeDtypeStruct((2, served, rows, cols), F32),
        input_output_aliases={3: 0} if more else {},
        compiler_params=pltpu.CompilerParams(
            vmem_limit_bytes=24 << 20, dimension_semantics=("arbitrary",)
        ),
    )(column, here, there, *more)


TO_INNER = [(0, 2), (1, 3), (6, 4), (7, 5)]
ACROSS = [(2, 4), (3, 5), (4, 2), (5, 3)]
TO_OUTER = [(2, 0), (3, 1), (4, 6), (5, 7)]


def tie(value, marks):
    return lax.optimization_barrier((value, marks))[0] if marks else value


def line_step(outer, came, block, part, across, following, sent):
    want_part, want_sent, want_done = block is not None, part is not None, sent is not None
    given = [came] + [a for a in (block, part, across, following, sent) if a is not None]
    outs = want_part + want_sent + want_done

    def body(outer_ref, *refs):
        ins, out = list(refs[: len(given)]), list(refs[len(given) :])
        came_ref = ins.pop(0)
        block_ref = ins.pop(0) if want_part else None
        part_ref, across_ref = (ins.pop(0), ins.pop(0)) if want_sent else (None, None)
        following_ref = ins.pop(0) if following is not None else None
        sent_ref = ins.pop(0) if want_done else None
        part_out = out.pop(0) if want_part else None
        sent_out = out.pop(0) if want_sent else None
        done_out = out.pop(0) if want_done else None

        @pl.when(outer_ref[0] == 0)
        def _():
            if want_part:
                part_out[...] = block_ref[...] + came_ref[...]
            if want_sent:
                sent_out[...] = part_ref[...] + across_ref[...]
            if want_done:
                done_out[...] = sent_ref[...]

        @pl.when(outer_ref[0] == 1)
        def _():
            if following is not None:
                sent_out[...] = following_ref[...]
            if want_done:
                done_out[...] = came_ref[...]

    res = call(body, [outer], given, [(came.shape, BF16)] * outs, mib=24)
    res = list(res)
    return [res.pop(0) if w else None for w in (want_part, want_sent, want_done)]


class LineSums:
    LAG = 3

    def __init__(self, me, beside, served):
        self.outer = ((me < 2) | (me >= 6)).astype(jnp.int32).reshape(1)
        self.column = (me & 1).astype(jnp.int32).reshape(1)
        self.beside, self.served = beside, served
        self.blocks, self.held = [], [None, None, None]
        self.sent, self.parts, self.across = {}, [], []
        self.swaps, self.marks, self.done = [], [], 0

    def feed(self, results):
        for e in range(results[0].shape[0]):
            self.blocks += [results[m][e] for m in range(3)]

    def store(self):
        if self.done < len(self.swaps):
            here, there = self.swaps[self.done]
            e, m = divmod(self.done, 3)
            self.held[m] = store_pair(self.held[m], here, there, self.column, e, self.served)
            self.done += 1

    def step(self, after=()):
        t, count = len(self.marks), len(self.blocks)
        new, old = t < count, t >= self.LAG
        sent = self.sent[t] if old else self.blocks[t]
        kept = [h for h in self.held if h is not None]
        sent, kept, _ = lax.optimization_barrier((sent, kept, list(after)))
        self.held[: len(kept)] = kept
        came = lax.ppermute(sent, "ctx", (TO_INNER if new else []) + (TO_OUTER if old else []))
        self.marks.append(came)
        turn_back = 0 < t <= count
        shape = self.blocks[t % 3].shape
        more = turn_back and t + 2 < count
        part, _, finished = line_step(
            self.outer, came, self.blocks[t] if new else None, None, None, None, sent if old else None
        ) if new or old else (None, None, None)
        if turn_back:
            _, self.sent[t + 2], _ = line_step(
                self.outer, self.across[t - 1], None, self.parts[t - 1], self.across[t - 1],
                self.blocks[t + 2] if more else None, None,
            )
        if new:
            self.parts.append(part)
            self.across.append(lax.ppermute(part, "ctx", ACROSS))
        if len(self.swaps) > 1:
            self.store()
        if old:
            self.swaps.append((finished, lax.ppermute(finished, "ctx", self.beside)))

    def hold(self, value, step):
        return tie(value, self.marks[step : step + 1] + self.across[max(step - 1, 0) : step])

    def finish(self):
        while self.done < len(self.swaps):
            self.store()
        return [h.reshape((2 * self.served,) + h.shape[2:]) for h in self.held]


def after_body(count):
    def body(
        me_ref, mixed_ref, ga_ref, gy_ref, gain_ref, gates_ref, dgate_ref, router_ref, act_ref, o_ref,
        *rest,
    ):
        weights = rest[:count]
        gy1_ref, go_ref, rgrad_ref, ggrad_ref = rest[count : count + 4]
        wgrads = rest[count + 4 : 2 * count + 4]
        parts, gparts = rest[2 * count + 4 :]
        gates, dgate = gates_ref[...], dgate_ref[...]
        dlogits = gates * (dgate - jnp.sum(gates * dgate, axis=0, keepdims=True))
        dlogits = dlogits.astype(BF16)
        grad = ga_ref[...] + dot_tn(dlogits, router_ref[...])
        rgrad_ref[...] = dot_nn(dlogits, act_ref[...])
        mixed = mixed_ref[...]
        inverse = lax.rsqrt(jnp.mean(mixed * mixed, axis=-1, keepdims=True) + EPS)
        normed = mixed * inverse
        ggrad_ref[...] = jnp.sum(grad * normed, axis=0, keepdims=True)
        gy1 = gy_ref[...] + norm_back(grad, normed, inverse, gain_ref[...])
        gy1_ref[...] = gy1
        low = gy1.astype(BF16)
        me = me_ref[0]
        width = o_ref.shape[1] // count
        for b in range(count):
            parts[b] = o_ref[:, b * width : (b + 1) * width]
        for s in range(count):
            gparts[me ^ s] = dot_nt(low, weights[s][...]).astype(BF16)
            wgrads[s][...] = dot_tn(parts[me ^ s], low).astype(BF16)
        for b in range(count):
            go_ref[:, b * width : (b + 1) * width] = gparts[b]

    return body


def first_body(count):
    def body(me_ref, x_ref, gain_ref, cos_ref, sin_ref, act_ref, gq_ref, dkv_ref, gy1_ref, *rest):
        wq, wkv = rest[:count], rest[count : 2 * count]
        in_ref, ggrad_ref = rest[2 * count : 2 * count + 2]
        qgrads = rest[2 * count + 2 : 3 * count + 2]
        kgrads = rest[3 * count + 2 : 4 * count + 2]
        gkv, gparts = rest[4 * count + 2 :]
        rows = x_ref.shape[0]
        first = (lanes_of(rows) & 63) < 32
        cosine, sine = cos_ref[...], sin_ref[...]
        for j in range(KVD // 128):
            tile = dkv_ref[:, j * 128 : (j + 1) * 128].astype(F32)
            gkv[:, j * 128 : (j + 1) * 128] = turn_back(tile, cosine, sine, first).astype(BF16)
        gkv[:, KVD:] = dkv_ref[:, KVD:].astype(BF16)
        me = me_ref[0]
        gq = gq_ref[...]
        for s in range(count):
            gparts[me ^ s] = dot_nt(gq, wq[s][...]) + dot_nt(gkv[...], wkv[s][...])
            qgrads[s][...] = dot_tn(act_ref[me ^ s], gq).astype(BF16)
            kgrads[s][...] = dot_tn(act_ref[me ^ s], gkv[...]).astype(BF16)
        grad = jnp.concatenate([gparts[b] for b in range(count)], axis=1)
        x = x_ref[...].astype(F32)
        inverse = lax.rsqrt(jnp.mean(x * x, axis=-1, keepdims=True) + EPS)
        normed = x * inverse
        ggrad_ref[...] = jnp.sum(grad * normed, axis=0, keepdims=True)
        in_ref[...] = gy1_ref[...] + norm_back(grad, normed, inverse, gain_ref[...])

    return body


def make(n_dp, n_ctx):
    def on_device(
        layer_input, query_weight, key_weight, value_weight, out_weight, attn_gain, router_weight,
        moe_gain, gate_weight, up_weight, down_weight, expert_ids, fill_order, block_deal,
        seq_lengths, out_grad,
    ):
        rows, wide = layer_input.shape
        local = gate_weight.shape[0]
        width = wide // n_dp
        me_dp = lax.axis_index("dp").astype(jnp.int32)
        me_ctx = lax.axis_index("ctx").astype(jnp.int32)
        me = me_dp.reshape(1)
        near = rows // BLOCK

        pairs = n_ctx == 8 and local % 2 == 0
        served = local // 2 if pairs else local
        beside = xor_pairs(n_ctx, 1)
        column = me_ctx & 1 if pairs else jnp.zeros((), jnp.int32)
        grad_low = out_grad.astype(BF16)
        grad_beside = lax.ppermute(grad_low, "ctx", beside) if pairs else None
        wkv = dp_gather(jnp.concatenate([key_weight, value_weight], axis=1), n_dp)
        small = jnp.concatenate(
            [
                router_weight.T,
                attn_gain[None, :],
                moe_gain[None, :],
                jnp.zeros((14, width), BF16),
            ],
            axis=0,
        )
        small = in_order(dp_gather(small, n_dp), me_dp)
        small = small.transpose(1, 0, 2).reshape(EXPERTS + 16, wide)
        router_t = small[:EXPERTS]
        gain_one = small[EXPERTS : EXPERTS + 1].astype(F32)
        gain_two = small[EXPERTS + 1 : EXPERTS + 2].astype(F32)
        wq = dp_gather(query_weight, n_dp)

        deal, lengths = block_deal[0], seq_lengths[0]
        blocks = deal.shape[0]
        ends = jnp.cumsum(lengths, dtype=jnp.int32)
        mine = lax.dynamic_slice_in_dim(deal, me_ctx * near, near)
        places = (mine[:, None] * BLOCK + jnp.arange(BLOCK, dtype=jnp.int32)[None, :]).reshape(rows, 1)
        starts = jnp.sum(
            jnp.where(places >= ends[None, :], lengths[None, :], 0), axis=1, keepdims=True, dtype=jnp.int32
        )
        relative = (places - starts).astype(F32)
        lane = jnp.arange(128, dtype=jnp.int32)
        inverse = 10000.0 ** (-(lane % 32).astype(F32) * (2.0 / HEAD))
        angles = relative * inverse[None, :]
        cosine = jnp.cos(angles)
        sine = jnp.sin(angles) * jnp.where(lane % 64 < 32, -1.0, 1.0)[None, :]
        block_starts = jnp.sum(
            jnp.where((mine * BLOCK)[:, None] >= ends[None, :], lengths[None, :], 0), axis=1, dtype=jnp.int32
        )
        low_blocks = block_starts // BLOCK
        ring = jnp.array(ring_order(n_ctx)[0], jnp.int32)
        ring_deal = deal.reshape(n_ctx, near)[ring].reshape(blocks)
        held = jnp.arange(blocks, dtype=jnp.int32)
        where_block = jnp.sum(
            jnp.where(ring_deal[None, :] == held[:, None], held[None, :], 0), axis=1, dtype=jnp.int32
        )

        kv_mine, act_one = call(
            kv_body(n_dp),
            [me],
            [tie(layer_input, [grad_beside] if pairs else []), gain_one, cosine, sine] + wkv,
            [((rows, 2 * KVD), BF16), ((n_dp, rows, width), BF16)],
        )
        every_kv = ring_gather(kv_mine, n_ctx)
        (query,) = call(query_body(n_dp), [me], [act_one, cosine, sine] + wq, [((rows, wide), BF16)])
        wo = dp_gather(out_weight, n_dp)

        def reach(block):
            pieces = dp_gather(block, n_dp)
            if pairs:
                pieces = pieces + dp_gather(lax.ppermute(block, "ctx", beside), n_dp)
            return pieces

        table = jnp.concatenate([expert_ids.T, fill_order], axis=0)
        table = jnp.stack(reach(table))
        ids, fill = table[:, :-1], table[:, -1]
        held_blocks = table.shape[0]
        names = jnp.arange(EXPERTS, dtype=jnp.int32)
        hits = jnp.sum((ids[:, :, None, :] == names[None, None, :, None]).astype(F32), axis=1)
        earlier = (fill[:, :, None] < fill[:, None, :]).astype(BF16)
        prior = jnp.einsum(
            "set,stu->seu", hits.astype(BF16), earlier, preferred_element_type=F32
        )
        slot = jnp.where((hits > 0) & (prior < CAP), prior, -1.0).astype(jnp.int32)
        base = column * served
        slot = lax.dynamic_slice_in_dim(slot, me_dp * local + base, served, axis=1)
        slots_t = slot.transpose(1, 0, 2).reshape(served, 1, held_blocks * rows)
        hits_t = hits.transpose(1, 0, 2).reshape(EXPERTS, held_blocks * rows)
        grads_all = dp_gather(grad_low, n_dp)
        if pairs:
            grads_all = grads_all + dp_gather(grad_beside, n_dp)
        query, grads_all, wo = lax.optimization_barrier((query, grads_all, wo))

        attended, extended = call(
            attend_body,
            [low_blocks, mine, where_block],
            [query, every_kv, starts],
            [((rows, wide), BF16), ((PAIRS, 4, rows, 128), F32)],
            [
                pltpu.VMEM((PAIRS, 4 * BLOCK, 128), BF16),
                pltpu.VMEM((PAIRS, 4 * BLOCK, 128), F32),
                pltpu.VMEM((PAIRS, 4 * BLOCK, 128), F32),
                pltpu.VMEM((PAIRS, 4 * BLOCK, 128), F32),
            ],
            flops=rows * blocks * BLOCK * wide * 4,
        )
        mixed, act_two = call(
            mix_body(n_dp),
            [me],
            [layer_input, attended, gain_two] + wo,
            [((rows, wide), F32), ((rows, wide), BF16)],
            [pltpu.VMEM((n_dp, rows, width), BF16)],
        )

        acts_all = reach(act_two)
        groups = [(0, 1), (1, served - 1)] if pairs else [(0, served)]
        results = []
        line = LineSums(me_ctx, beside, served) if pairs else None

        def step(*after):
            if pairs:
                line.step(after)

        def hold(value, step):
            return line.hold(value, step) if pairs else value

        for first, number in groups:
            at = jnp.stack([base + first, me_dp * local + base + first])
            results.append(
                expert_call(
                    held_blocks, rows, local, served, first, number, gate_weight.shape[1:]
                )(
                    at, *acts_all, *grads_all, slots_t, hits_t, router_t, gate_weight, up_weight,
                    down_weight,
                )
            )
            if pairs:
                line.feed(results[-1])
            step(*[res[4] for res in results[1:]])
        gates = results[0][3]

        def combine(index, after):
            return call(
                combine_body(held_blocks, rows, groups),
                [],
                [tie(slots_t, after)] + [res[index] for res in results],
                [((rows, wide), BF16)] * held_blocks,
            )

        def settle(parts, between):
            kept = [dp_cores(parts[s : s + n_dp], n_dp) for s in range(0, held_blocks, n_dp)]
            between(kept)
            totals = [dp_rest(k, n_dp) for k in kept]
            between(totals)
            if pairs:
                totals[0] = totals[0] + lax.ppermute(
                    totals[1].astype(BF16), "ctx", beside
                ).astype(F32)
            return totals[0]

        dgates = jnp.concatenate([res[4] for res in results], axis=0)[:, 0]
        back = [dgates[:, s * rows : (s + 1) * rows] for s in range(held_blocks)]
        if pairs:
            other = lax.ppermute(jnp.stack(back[n_dp:]), "ctx", beside)
            own = jnp.stack(back[:n_dp])
            back = jnp.where(
                column == 0,
                jnp.concatenate([own, other], axis=1),
                jnp.concatenate([other, own], axis=1),
            )
        back = [back[0]] + [lax.ppermute(back[s], "dp", xor_pairs(n_dp, s)) for s in range(1, n_dp)]
        dgate_t = in_order(back, me_dp).reshape(EXPERTS, rows)
        g_parts = combine(6, line.marks[:1] if pairs else [])
        grad_act_two = settle(g_parts, lambda values: None)
        step(grad_act_two)
        res = call(
            after_body(n_dp),
            [me],
            [mixed, hold(grad_act_two, 1), out_grad, gain_two, gates, dgate_t, router_t, act_two, attended] + wo,
            [((rows, wide), F32), ((rows, wide), BF16), ((EXPERTS, wide), F32), ((1, wide), F32)]
            + [((width, wide), BF16)] * n_dp,
            [pltpu.VMEM((n_dp, rows, width), BF16), pltpu.VMEM((n_dp, rows, width), BF16)],
        )
        grad_mixed, grad_heads, router_part, gain_two_part = res[:4]
        out_parts = res[4:]
        grad_query, kv_grads = call(
            attend_back_body,
            [low_blocks, mine, where_block],
            [query, every_kv, starts, grad_heads, extended, cosine, sine],
            [((rows, wide), BF16), ((blocks * BLOCK, 2 * KVD), BF16)],
            [
                pltpu.VMEM((PAIRS, 4 * BLOCK, 128), BF16),
                pltpu.VMEM((PAIRS, 4 * BLOCK, 128), BF16),
                pltpu.VMEM((PAIRS, 4 * BLOCK, 128), F32),
                pltpu.VMEM((PAIRS, 4 * BLOCK, 128), F32),
                pltpu.VMEM((PAIRS, 4 * BLOCK, 128), F32),
                pltpu.VMEM((blocks * BLOCK, 2 * KVD), F32),
            ],
            flops=rows * blocks * BLOCK * wide * 10,
        )
        step(grad_query)
        kv_grad = ring_scatter(hold(kv_grads, 2), n_ctx)
        y_parts = combine(5, [grad_query])
        y_total = settle(y_parts, lambda values: None)
        layer_output = mixed + y_total
        dense_out = dp_reduce(out_parts, n_dp).astype(BF16)
        step(layer_output)
        res = call(
            first_body(n_dp),
            [me],
            [layer_input, gain_one, cosine, sine, act_one, grad_query, kv_grad, grad_mixed] + wq + wkv,
            [((rows, wide), F32), ((1, wide), F32)]
            + [((width, wide), BF16)] * n_dp
            + [((width, 2 * KVD), BF16)] * n_dp,
            [pltpu.VMEM((rows, 2 * KVD), BF16), pltpu.VMEM((n_dp, rows, width), F32)],
        )
        input_grad, gain_one_part = res[:2]
        q_parts, kv_parts = res[2 : 2 + n_dp], res[2 + n_dp :]
        step(gain_one_part)

        dense_q = dp_reduce(q_parts, n_dp).astype(BF16)
        dense_kv = dp_reduce(kv_parts, n_dp).astype(BF16)
        dense = jnp.concatenate([dense_out, dense_q, dense_kv], axis=0)
        dense = ring_gather(ring_scatter(dense, n_ctx), n_ctx).astype(F32)
        tiny = jnp.concatenate([router_part, gain_one_part, gain_two_part], axis=0)
        for bit in [1 << b for b in range(n_ctx.bit_length() - 1)]:
            tiny = tiny + lax.ppermute(tiny, "ctx", xor_pairs(n_ctx, bit))
        for bit in [1 << b for b in range(n_dp.bit_length() - 1)]:
            tiny = tiny + lax.ppermute(tiny, "dp", xor_pairs(n_dp, bit))
        tiny = lax.dynamic_slice_in_dim(tiny, me_dp * width, width, axis=1)
        if pairs:
            while len(line.marks) < len(line.blocks) + line.LAG:
                line.step()
            expert_sums = line.finish()
        else:
            expert_sums = [
                ring_gather(ring_scatter(g.reshape(-1, g.shape[2]), n_ctx), n_ctx)
                .reshape(g.shape)
                .astype(F32)
                for g in results[0][:3]
            ]
        return (
            layer_output,
            input_grad,
            dense[width : 2 * width],
            dense[2 * width :, :KVD],
            dense[2 * width :, KVD:],
            dense[:width],
            tiny[EXPERTS],
            tiny[:EXPERTS].T,
            tiny[EXPERTS + 1],
            expert_sums[0],
            expert_sums[1],
            expert_sums[2],
        )

    return on_device


def solution(mesh):
    rows2 = P(("dp", "ctx"), None)
    mat = P("dp", None)
    cube = P("dp", None, None)
    in_specs = (
        rows2, mat, mat, mat, mat, P("dp"), mat, P("dp"), cube, cube, cube, rows2, rows2, mat, mat, rows2,
    )
    out_specs = (rows2, rows2, mat, mat, mat, mat, P("dp"), mat, P("dp"), cube, cube, cube)
    return jax.shard_map(
        make(mesh.shape["dp"], mesh.shape["ctx"]),
        mesh=mesh,
        in_specs=in_specs,
        out_specs=out_specs,
        check_vma=False,
    )
```

```python
import math

import jax
import jax.numpy as jnp
from jax import lax
from jax.experimental import pallas as pl
from jax.experimental.pallas import tpu as pltpu
from jax.sharding import PartitionSpec as P

EXPERTS = 32
BLOCK = 128
CAP = 64
HEAD = 64
KVD = 512
PAIRS = 4
EPS = 1e-06
NEG = -1e30
F32 = jnp.float32
BF16 = jnp.bfloat16


def dot_nn(a, b):
    return lax.dot_general(a, b, (((1,), (0,)), ((), ())), preferred_element_type=F32)


def dot_nt(a, b):
    return lax.dot_general(a, b, (((1,), (1,)), ((), ())), preferred_element_type=F32)


def dot_tn(a, b):
    return lax.dot_general(a, b, (((0,), (0,)), ((), ())), preferred_element_type=F32)


def vmem():
    return pl.BlockSpec(memory_space=pltpu.VMEM)


def smem():
    return pl.BlockSpec(memory_space=pltpu.SMEM)


def cost(flops, arrays, outs):
    moved = sum(a.size * a.dtype.itemsize for a in arrays)
    moved += sum(math.prod(s) * jnp.dtype(d).itemsize for s, d in outs)
    return pl.CostEstimate(flops=0, transcendentals=0, bytes_accessed=0)


def call(body, scalars, arrays, outs, scratch=(), mib=48, flops=0):
    return pl.pallas_call(
        body,
        cost_estimate=cost(flops, arrays, outs),
        in_specs=[smem() for _ in scalars] + [vmem() for _ in arrays],
        out_specs=[vmem() for _ in outs],
        out_shape=[jax.ShapeDtypeStruct(s, d) for s, d in outs],
        scratch_shapes=list(scratch),
        compiler_params=pltpu.CompilerParams(vmem_limit_bytes=mib << 20),
    )(*scalars, *arrays)


def xor_pairs(count, step):
    return [(i, i ^ step) for i in range(count)]


def dp_gather(block, count):
    pieces = {0: block}
    for step in range(2, count, 2):
        pieces[step] = lax.ppermute(block, "dp", xor_pairs(count, step))
    for step in range(0, count, 2):
        pieces[step + 1] = lax.ppermute(pieces[step], "dp", xor_pairs(count, 1))
    return [pieces[s] for s in range(count)]


def dp_cores(pieces, count):
    kept = []
    for step in range(0, count, 2):
        other = lax.ppermute(pieces[step + 1], "dp", xor_pairs(count, 1))
        kept.append((pieces[step].astype(F32) + other.astype(F32)).astype(BF16))
    return kept


def dp_rest(kept, count):
    total = kept[0].astype(F32)
    for i in range(1, len(kept)):
        other = lax.ppermute(kept[i], "dp", xor_pairs(count, 2 * i))
        total = total + other.astype(F32)
    return total


def dp_reduce(pieces, count):
    return dp_rest(dp_cores(pieces, count), count)


def in_order(pieces, index):
    stacked = jnp.stack(pieces)
    count = len(pieces)
    bit = 1
    while bit < count:
        swapped = jnp.stack([stacked[j ^ bit] for j in range(count)])
        stacked = jnp.where((index & bit) > 0, swapped, stacked)
        bit *= 2
    return stacked


def ring_order(count):
    return [list(range(0, count, 2)) + list(range(count - 1, 0, -2))]


def ring_gather(block, count):
    return lax.all_gather(block, "ctx", axis=0, tiled=True, axis_index_groups=ring_order(count))


def ring_scatter(block, count):
    return lax.psum_scatter(
        block, "ctx", scatter_dimension=0, tiled=True, axis_index_groups=ring_order(count)
    )


def half_swap(tile, first):
    return jnp.where(first, pltpu.roll(tile, 96, 1), pltpu.roll(tile, 32, 1))


def turn(tile, cosine, sine, first):
    return tile * cosine + half_swap(tile, first) * sine


def turn_back(tile, cosine, sine, first):
    return tile * cosine - half_swap(tile, first) * sine


def lanes_of(rows):
    return lax.broadcasted_iota(jnp.int32, (rows, 128), 1)


def spread_heads(tile_a, tile_b):
    low = lanes_of(tile_a.shape[0]) < HEAD
    return jnp.concatenate(
        [
            jnp.where(low, tile_a, 0.0),
            jnp.where(low, pltpu.roll(tile_a, HEAD, 1), 0.0),
            jnp.where(low, 0.0, pltpu.roll(tile_b, HEAD, 1)),
            jnp.where(low, 0.0, tile_b),
        ],
        axis=0,
    )


def join_heads(stacked):
    rows = stacked.shape[0] // 4
    low = lanes_of(rows) < HEAD
    part = [stacked[h * rows : (h + 1) * rows] for h in range(4)]
    return (
        jnp.where(low, part[0], pltpu.roll(part[1], HEAD, 1)),
        jnp.where(low, pltpu.roll(part[2], HEAD, 1), part[3]),
    )


def norm_back(grad, normed, inverse, gain):
    scaled = grad * gain
    return inverse * (scaled - normed * jnp.mean(scaled * normed, axis=-1, keepdims=True))


def kv_body(count):
    def body(me_ref, x_ref, gain_ref, cos_ref, sin_ref, *rest):
        weights, (kv_ref, act_ref) = rest[:count], rest[count:]
        x = x_ref[...].astype(F32)
        inverse = lax.rsqrt(jnp.mean(x * x, axis=-1, keepdims=True) + EPS)
        act = (x * inverse * gain_ref[...]).astype(BF16)
        width = x.shape[1] // count
        for b in range(count):
            act_ref[b] = act[:, b * width : (b + 1) * width]
        me = me_ref[0]
        total = dot_nn(act_ref[me], weights[0][...])
        for s in range(1, count):
            total = total + dot_nn(act_ref[me ^ s], weights[s][...])
        first = (lanes_of(x.shape[0]) & 63) < 32
        cosine, sine = cos_ref[...], sin_ref[...]
        for j in range(KVD // 128):
            tile = total[:, j * 128 : (j + 1) * 128]
            kv_ref[:, j * 128 : (j + 1) * 128] = turn(tile, cosine, sine, first).astype(BF16)
        kv_ref[:, KVD:] = total[:, KVD:].astype(BF16)

    return body


def query_body(count):
    def body(me_ref, act_ref, cos_ref, sin_ref, *rest):
        weights, q_ref = rest[:count], rest[count]
        me = me_ref[0]
        total = dot_nn(act_ref[me], weights[0][...])
        for s in range(1, count):
            total = total + dot_nn(act_ref[me ^ s], weights[s][...])
        first = (lanes_of(total.shape[0]) & 63) < 32
        cosine, sine = cos_ref[...], sin_ref[...]
        for j in range(total.shape[1] // 128):
            tile = total[:, j * 128 : (j + 1) * 128]
            turned = turn(tile, cosine, sine, first).astype(BF16)
            q_ref[:, j * 128 : (j + 1) * 128] = turned * (1.0 / HEAD)

    return body


def visible(place_block, key_block, starts):
    rows = lax.broadcasted_iota(jnp.int32, (BLOCK, BLOCK), 0) + place_block * BLOCK
    keys = lax.broadcasted_iota(jnp.int32, (BLOCK, BLOCK), 1) + key_block * BLOCK
    return (keys <= rows) & (keys >= starts)


def attend_body(low_ref, high_ref, where_ref, q_ref, kv_ref, starts_ref, o_ref, ext_ref, qs, tops, sums, accs):
    low_half = lanes_of(BLOCK) < HEAD
    for qb in range(q_ref.shape[0] // BLOCK):
        rows = slice(qb * BLOCK, (qb + 1) * BLOCK)
        for j in range(PAIRS):
            qs[j] = spread_heads(
                q_ref[rows, 256 * j : 256 * j + 128].astype(F32),
                q_ref[rows, 256 * j + 128 : 256 * j + 256].astype(F32),
            ).astype(BF16)
        tops[...] = jnp.full(tops.shape, NEG, F32)
        sums[...] = jnp.zeros(sums.shape, F32)
        accs[...] = jnp.zeros(accs.shape, F32)
        low, high = low_ref[qb], high_ref[qb]

        def scores_of(b, at, seen, j):
            key = kv_ref[pl.ds(at, BLOCK), 128 * j : 128 * j + 128]
            scores = dot_nt(qs[j], key).reshape(4, BLOCK, BLOCK)
            return jnp.where(seen, scores, NEG).reshape(4 * BLOCK, BLOCK)

        def find_top(b, carry):
            at = pl.multiple_of(where_ref[b] * BLOCK, BLOCK)
            seen = visible(high, b, starts_ref[rows, :])[None]
            for j in range(PAIRS):
                tops[j] = jnp.maximum(tops[j], scores_of(b, at, seen, j))
            return carry

        lax.fori_loop(low, high + 1, find_top, 0)
        for j in range(PAIRS):
            top = jnp.max(tops[j], axis=-1, keepdims=True)
            tops[j] = jnp.broadcast_to(top, tops.shape[1:])

        def gather_values(b, carry):
            at = pl.multiple_of(where_ref[b] * BLOCK, BLOCK)
            seen = visible(high, b, starts_ref[rows, :])[None]
            for j in range(PAIRS):
                value = kv_ref[pl.ds(at, BLOCK), KVD + 128 * j : KVD + 128 * j + 128]
                weights = jnp.exp(scores_of(b, at, seen, j) - tops[j])
                sums[j] += weights
                accs[j] += dot_nn(weights.astype(BF16), value)
            return carry

        lax.fori_loop(low, high + 1, gather_values, 0)
        for j in range(PAIRS):
            weight = jnp.sum(sums[j], axis=-1, keepdims=True)
            attended = accs[j] / weight
            total = tops[j] + jnp.log(weight)
            left, right = join_heads(attended)
            o_ref[rows, 256 * j : 256 * j + 128] = left.astype(BF16)
            o_ref[rows, 256 * j + 128 : 256 * j + 256] = right.astype(BF16)
            for h in range(4):
                part = slice(h * BLOCK, (h + 1) * BLOCK)
                keep = low_half if h < 2 else jnp.logical_not(low_half)
                ext_ref[j, h, rows, :] = jnp.where(keep, attended[part], total[part])


def attend_back_body(
    low_ref, high_ref, where_ref, q_ref, kv_ref, starts_ref, go_ref, ext_ref, cos_ref, sin_ref,
    gq_ref, dkv_ref, qs, gs, ds, lse, dqs, sums,
):
    first = (lanes_of(BLOCK) & 63) < 32
    sums[...] = jnp.zeros(sums.shape, F32)
    for qb in range(q_ref.shape[0] // BLOCK):
        rows = slice(qb * BLOCK, (qb + 1) * BLOCK)
        for j in range(PAIRS):
            cols = slice(256 * j, 256 * j + 128), slice(256 * j + 128, 256 * j + 256)
            qs[j] = spread_heads(
                q_ref[rows, cols[0]].astype(F32), q_ref[rows, cols[1]].astype(F32)
            ).astype(BF16)
            grad = spread_heads(
                go_ref[rows, cols[0]].astype(F32), go_ref[rows, cols[1]].astype(F32)
            )
            gs[j] = grad.astype(BF16)
            for h in range(4):
                part = slice(h * BLOCK, (h + 1) * BLOCK)
                ext = ext_ref[j, h, rows, :]
                flat = (BLOCK, BLOCK)
                delta = jnp.sum(grad[part] * ext, axis=-1, keepdims=True)
                total = ext[:, 127:128] if h < 2 else ext[:, 0:1]
                ds[j, part, :] = jnp.broadcast_to(delta, flat)
                lse[j, part, :] = jnp.broadcast_to(total, flat)
        dqs[...] = jnp.zeros(dqs.shape, F32)
        high = high_ref[qb]

        def step(b, carry):
            at = pl.multiple_of(where_ref[b] * BLOCK, BLOCK)
            seen = visible(high, b, starts_ref[rows, :])[None]
            for j in range(PAIRS):
                kcols = slice(128 * j, 128 * j + 128)
                vcols = slice(KVD + 128 * j, KVD + 128 * j + 128)
                key = kv_ref[pl.ds(at, BLOCK), kcols]
                value = kv_ref[pl.ds(at, BLOCK), vcols]
                scores = dot_nt(qs[j], key).reshape(4, BLOCK, BLOCK)
                scores = jnp.where(seen, scores, NEG).reshape(4 * BLOCK, BLOCK)
                weights = jnp.exp(scores - lse[j])
                grad = dot_nt(gs[j], value)
                score_grad = (weights * (grad - ds[j])).astype(BF16)
                dqs[j] += dot_nn(score_grad, key)
                sums[pl.ds(at, BLOCK), kcols] += dot_tn(score_grad, qs[j])
                sums[pl.ds(at, BLOCK), vcols] += dot_tn(weights.astype(BF16), gs[j])
            return carry

        lax.fori_loop(low_ref[qb], high + 1, step, 0)
        cosine, sine = cos_ref[rows, :], sin_ref[rows, :]
        for j in range(PAIRS):
            left, right = join_heads(dqs[j] * (1.0 / HEAD))
            gq_ref[rows, 256 * j : 256 * j + 128] = turn_back(left, cosine, sine, first).astype(BF16)
            gq_ref[rows, 256 * j + 128 : 256 * j + 256] = turn_back(right, cosine, sine, first).astype(
                BF16
            )
    dkv_ref[...] = sums[...].astype(BF16)


def mix_body(count):
    def body(me_ref, x_ref, o_ref, gain_ref, *rest):
        weights, (mixed_ref, act_ref, parts) = rest[:count], rest[count:]
        width = o_ref.shape[1] // count
        for b in range(count):
            parts[b] = o_ref[:, b * width : (b + 1) * width]
        me = me_ref[0]
        total = x_ref[...].astype(F32)
        for s in range(count):
            total = total + dot_nn(parts[me ^ s], weights[s][...])
        mixed_ref[...] = total
        inverse = lax.rsqrt(jnp.mean(total * total, axis=-1, keepdims=True) + EPS)
        act_ref[...] = (total * inverse * gain_ref[...]).astype(BF16)

    return body


def expert_call(blocks, rows, local, served, first, number, last_dims):
    wide, inner = last_dims
    tokens = blocks * rows

    def body(at_ref, *refs):
        acts, grads = refs[:blocks], refs[blocks : 2 * blocks]
        slot_ref, hit_ref, router_ref, wg_ref, wu_ref, wd_ref = refs[2 * blocks : 2 * blocks + 6]
        gg_ref, ug_ref, dg_ref, gate_out, dgate_ref, y_ref, dx_ref = refs[2 * blocks + 6 : 2 * blocks + 13]
        gate_all, xe, gyx, dye = refs[2 * blocks + 13 :]
        e = pl.program_id(0)

        @pl.when(e == 0)
        def _():
            for s in range(blocks):
                part = slice(s * rows, (s + 1) * rows)
                logits = dot_nt(router_ref[...], acts[s][...])
                hit = hit_ref[:, part] > 0
                logits = jnp.where(hit, logits, NEG)
                top = jnp.max(logits, axis=0, keepdims=True)
                raised = jnp.where(hit, jnp.exp(logits - top), 0.0)
                gates = raised / jnp.sum(raised, axis=0, keepdims=True)
                gate_all[:, part] = gates
                if s == 0:
                    gate_out[...] = gates

        slot_row = slot_ref[0]
        gate_row = gate_all[pl.ds(at_ref[1] + e, 1), :]
        slot_id = lax.broadcasted_iota(jnp.int32, (CAP, rows), 0)
        slot_gates = []
        for s in range(blocks):
            part = slice(s * rows, (s + 1) * rows)
            put = slice(s * CAP, (s + 1) * CAP)
            hits = slot_id == slot_row[:, part]
            pick = jnp.where(hits, 1.0, 0.0).astype(BF16)
            gate = jnp.sum(jnp.where(hits, gate_row[:, part], 0.0), axis=1, keepdims=True)
            slot_gates.append(gate)
            xe[put, :] = dot_nn(pick, acts[s][...]).astype(BF16)
            picked = dot_nn(pick, grads[s][...])
            gyx[put, :] = picked.astype(BF16)
            dye[put, :] = (gate * picked).astype(BF16)
        gate_part = dot_nn(xe[...], wg_ref[0])
        up_part = dot_nn(xe[...], wu_ref[0])
        sig = jax.nn.sigmoid(gate_part)
        act = gate_part * sig
        hidden = (act * up_part).astype(BF16)
        out = dot_nn(hidden, wd_ref[0]).astype(BF16).astype(F32)
        slot_dot = jnp.sum(gyx[...].astype(F32) * out, axis=1, keepdims=True)
        for s in range(blocks):
            part = slice(s * rows, (s + 1) * rows)
            put = slice(s * CAP, (s + 1) * CAP)
            hits = slot_id == slot_row[:, part]
            dgate_ref[0, :, part] = jnp.sum(jnp.where(hits, slot_dot[put], 0.0), axis=0, keepdims=True)
            y_ref[0, put, :] = (slot_gates[s] * out[put]).astype(BF16)
        dg_ref[0] = dot_tn(hidden, dye[...]).astype(BF16)
        grad_hidden = dot_nt(dye[...], wd_ref[0])
        grad_gate = (grad_hidden * up_part * sig * (1.0 + gate_part * (1.0 - sig))).astype(BF16)
        grad_up = (grad_hidden * act).astype(BF16)
        gg_ref[0] = dot_tn(xe[...], grad_gate).astype(BF16)
        ug_ref[0] = dot_tn(xe[...], grad_up).astype(BF16)
        dx_ref[0] = (dot_nt(grad_gate, wg_ref[0]) + dot_nt(grad_up, wu_ref[0])).astype(BF16)

    def whole(*shape):
        return pl.BlockSpec(
            shape, lambda e, at: tuple(0 for _ in shape), pipeline_mode=pl.Buffered(1)
        )

    def each(*shape):
        return pl.BlockSpec((1,) + shape, lambda e, at: (e,) + tuple(0 for _ in shape))

    def weight(*shape):
        return pl.BlockSpec((1,) + shape, lambda e, at: (at[0] + e,) + tuple(0 for _ in shape))

    shape = jax.ShapeDtypeStruct
    return pl.pallas_call(
        body,
        cost_estimate=pl.CostEstimate(
            flops=number * blocks * CAP * wide * (18 * inner + 4 * rows),
            transcendentals=0,
            bytes_accessed=number * 12 * wide * inner + 4 * blocks * rows * wide,
        ),
        grid_spec=pltpu.PrefetchScalarGridSpec(
            num_scalar_prefetch=1,
            grid=(number,),
            in_specs=[whole(rows, wide) for _ in range(2 * blocks)]
            + [
                pl.BlockSpec((1, 1, tokens), lambda e, at: (first + e, 0, 0)),
                whole(EXPERTS, tokens),
                whole(EXPERTS, wide),
                weight(wide, inner),
                weight(wide, inner),
                weight(inner, wide),
            ],
            out_specs=[
                each(wide, inner),
                each(wide, inner),
                each(inner, wide),
                pl.BlockSpec((EXPERTS, rows), lambda e, at: (0, 0)),
                each(1, tokens),
                each(blocks * CAP, wide),
                each(blocks * CAP, wide),
            ],
            scratch_shapes=[
                pltpu.VMEM((EXPERTS, tokens), F32),
                pltpu.VMEM((blocks * CAP, wide), BF16),
                pltpu.VMEM((blocks * CAP, wide), BF16),
                pltpu.VMEM((blocks * CAP, wide), BF16),
            ],
        ),
        out_shape=[
            shape((number, wide, inner), BF16),
            shape((number, wide, inner), BF16),
            shape((number, inner, wide), BF16),
            shape((EXPERTS, rows), F32),
            shape((number, 1, tokens), F32),
            shape((number, blocks * CAP, wide), BF16),
            shape((number, blocks * CAP, wide), BF16),
        ],
        compiler_params=pltpu.CompilerParams(
            vmem_limit_bytes=56 << 20, dimension_semantics=("arbitrary",)
        ),
    )


def combine_body(blocks, rows, groups):
    def body(slot_ref, *refs):
        parts, outs = refs[: len(groups)], refs[len(groups) :]
        slot_id = lax.broadcasted_iota(jnp.int32, (CAP, rows), 0)
        for s in range(blocks):
            picks, slots = [], []
            for g, (first, number) in enumerate(groups):
                for e in range(number):
                    hits = slot_id == slot_ref[first + e, :, s * rows : (s + 1) * rows]
                    picks.append(jnp.where(hits, 1.0, 0.0).astype(BF16))
                    slots.append(parts[g][e, s * CAP : (s + 1) * CAP, :])
            outs[s][...] = dot_tn(
                jnp.concatenate(picks, axis=0), jnp.concatenate(slots, axis=0)
            ).astype(BF16)

    return body


def store_pair(held, here, there, column, e, served):
    rows, cols = here.shape
    part = rows // 4

    def body(column_ref, here_ref, there_ref, *rest):
        rest[-1][column_ref[0], 0] = here_ref[...].astype(F32)
        rest[-1][1 - column_ref[0], 0] = there_ref[...].astype(F32)

    more = [] if held is None else [held]
    return pl.pallas_call(
        body,
        cost_estimate=pl.CostEstimate(flops=0, transcendentals=0, bytes_accessed=12 * rows * cols),
        grid_spec=pltpu.PrefetchScalarGridSpec(
            num_scalar_prefetch=1,
            grid=(4,),
            in_specs=[pl.BlockSpec((part, cols), lambda i, c: (i, 0))] * 2
            + [pl.BlockSpec(memory_space=pl.ANY)] * len(more),
            out_specs=pl.BlockSpec((2, 1, part, cols), lambda i, c: (0, e, i, 0)),
        ),
        out_shape=jax.ShapeDtypeStruct((2, served, rows, cols), F32),
        input_output_aliases={3: 0} if more else {},
        compiler_params=pltpu.CompilerParams(
            vmem_limit_bytes=24 << 20, dimension_semantics=("arbitrary",)
        ),
    )(column, here, there, *more)


TO_INNER = [(0, 2), (1, 3), (6, 4), (7, 5)]
ACROSS = [(2, 4), (3, 5), (4, 2), (5, 3)]
TO_OUTER = [(2, 0), (3, 1), (4, 6), (5, 7)]


def tie(value, marks):
    return lax.optimization_barrier((value, marks))[0] if marks else value


def line_step(outer, came, block, part, across, following, sent):
    want_part, want_sent, want_done = block is not None, part is not None, sent is not None
    given = [came] + [a for a in (block, part, across, following, sent) if a is not None]
    outs = want_part + want_sent + want_done

    def body(outer_ref, *refs):
        ins, out = list(refs[: len(given)]), list(refs[len(given) :])
        came_ref = ins.pop(0)
        block_ref = ins.pop(0) if want_part else None
        part_ref, across_ref = (ins.pop(0), ins.pop(0)) if want_sent else (None, None)
        following_ref = ins.pop(0) if following is not None else None
        sent_ref = ins.pop(0) if want_done else None
        part_out = out.pop(0) if want_part else None
        sent_out = out.pop(0) if want_sent else None
        done_out = out.pop(0) if want_done else None

        @pl.when(outer_ref[0] == 0)
        def _():
            if want_part:
                part_out[...] = block_ref[...] + came_ref[...]
            if want_sent:
                sent_out[...] = part_ref[...] + across_ref[...]
            if want_done:
                done_out[...] = sent_ref[...]

        @pl.when(outer_ref[0] == 1)
        def _():
            if following is not None:
                sent_out[...] = following_ref[...]
            if want_done:
                done_out[...] = came_ref[...]

    res = call(body, [outer], given, [(came.shape, BF16)] * outs, mib=24)
    res = list(res)
    return [res.pop(0) if w else None for w in (want_part, want_sent, want_done)]


class LineSums:
    LAG = 3

    def __init__(self, me, beside, served):
        self.outer = ((me < 2) | (me >= 6)).astype(jnp.int32).reshape(1)
        self.column = (me & 1).astype(jnp.int32).reshape(1)
        self.beside, self.served = beside, served
        self.blocks, self.held = [], [None, None, None]
        self.sent, self.parts, self.across = {}, [], []
        self.swaps, self.marks, self.done = [], [], 0

    def feed(self, results):
        for e in range(results[0].shape[0]):
            self.blocks += [results[m][e] for m in range(3)]

    def store(self):
        if self.done < len(self.swaps):
            here, there = self.swaps[self.done]
            e, m = divmod(self.done, 3)
            self.held[m] = store_pair(self.held[m], here, there, self.column, e, self.served)
            self.done += 1

    def step(self, after=()):
        t, count = len(self.marks), len(self.blocks)
        new, old = t < count, t >= self.LAG
        sent = self.sent[t] if old else self.blocks[t]
        kept = [h for h in self.held if h is not None]
        sent, kept, _ = lax.optimization_barrier((sent, kept, list(after)))
        self.held[: len(kept)] = kept
        came = lax.ppermute(sent, "ctx", (TO_INNER if new else []) + (TO_OUTER if old else []))
        self.marks.append(came)
        turn_back = 0 < t <= count
        shape = self.blocks[t % 3].shape
        more = turn_back and t + 2 < count
        part, _, finished = line_step(
            self.outer, came, self.blocks[t] if new else None, None, None, None, sent if old else None
        ) if new or old else (None, None, None)
        if turn_back:
            _, self.sent[t + 2], _ = line_step(
                self.outer, self.across[t - 1], None, self.parts[t - 1], self.across[t - 1],
                self.blocks[t + 2] if more else None, None,
            )
        if new:
            self.parts.append(part)
            self.across.append(lax.ppermute(part, "ctx", ACROSS))
        if len(self.swaps) > 1:
            self.store()
        if old:
            self.swaps.append((finished, lax.ppermute(finished, "ctx", self.beside)))

    def hold(self, value, step):
        return tie(value, self.marks[step : step + 1] + self.across[max(step - 1, 0) : step])

    def finish(self):
        while self.done < len(self.swaps):
            self.store()
        return [h.reshape((2 * self.served,) + h.shape[2:]) for h in self.held]


def after_body(count):
    def body(
        me_ref, mixed_ref, ga_ref, gy_ref, gain_ref, gates_ref, dgate_ref, router_ref, act_ref, o_ref,
        *rest,
    ):
        weights = rest[:count]
        gy1_ref, go_ref, rgrad_ref, ggrad_ref = rest[count : count + 4]
        wgrads = rest[count + 4 : 2 * count + 4]
        parts, gparts = rest[2 * count + 4 :]
        gates, dgate = gates_ref[...], dgate_ref[...]
        dlogits = gates * (dgate - jnp.sum(gates * dgate, axis=0, keepdims=True))
        dlogits = dlogits.astype(BF16)
        grad = ga_ref[...] + dot_tn(dlogits, router_ref[...])
        rgrad_ref[...] = dot_nn(dlogits, act_ref[...])
        mixed = mixed_ref[...]
        inverse = lax.rsqrt(jnp.mean(mixed * mixed, axis=-1, keepdims=True) + EPS)
        normed = mixed * inverse
        ggrad_ref[...] = jnp.sum(grad * normed, axis=0, keepdims=True)
        gy1 = gy_ref[...] + norm_back(grad, normed, inverse, gain_ref[...])
        gy1_ref[...] = gy1
        low = gy1.astype(BF16)
        me = me_ref[0]
        width = o_ref.shape[1] // count
        for b in range(count):
            parts[b] = o_ref[:, b * width : (b + 1) * width]
        for s in range(count):
            gparts[me ^ s] = dot_nt(low, weights[s][...]).astype(BF16)
            wgrads[s][...] = dot_tn(parts[me ^ s], low).astype(BF16)
        for b in range(count):
            go_ref[:, b * width : (b + 1) * width] = gparts[b]

    return body


def first_body(count):
    def body(me_ref, x_ref, gain_ref, cos_ref, sin_ref, act_ref, gq_ref, dkv_ref, gy1_ref, *rest):
        wq, wkv = rest[:count], rest[count : 2 * count]
        in_ref, ggrad_ref = rest[2 * count : 2 * count + 2]
        qgrads = rest[2 * count + 2 : 3 * count + 2]
        kgrads = rest[3 * count + 2 : 4 * count + 2]
        gkv, gparts = rest[4 * count + 2 :]
        rows = x_ref.shape[0]
        first = (lanes_of(rows) & 63) < 32
        cosine, sine = cos_ref[...], sin_ref[...]
        for j in range(KVD // 128):
            tile = dkv_ref[:, j * 128 : (j + 1) * 128].astype(F32)
            gkv[:, j * 128 : (j + 1) * 128] = turn_back(tile, cosine, sine, first).astype(BF16)
        gkv[:, KVD:] = dkv_ref[:, KVD:].astype(BF16)
        me = me_ref[0]
        gq = gq_ref[...]
        for s in range(count):
            gparts[me ^ s] = dot_nt(gq, wq[s][...]) + dot_nt(gkv[...], wkv[s][...])
            qgrads[s][...] = dot_tn(act_ref[me ^ s], gq).astype(BF16)
            kgrads[s][...] = dot_tn(act_ref[me ^ s], gkv[...]).astype(BF16)
        grad = jnp.concatenate([gparts[b] for b in range(count)], axis=1)
        x = x_ref[...].astype(F32)
        inverse = lax.rsqrt(jnp.mean(x * x, axis=-1, keepdims=True) + EPS)
        normed = x * inverse
        ggrad_ref[...] = jnp.sum(grad * normed, axis=0, keepdims=True)
        in_ref[...] = gy1_ref[...] + norm_back(grad, normed, inverse, gain_ref[...])

    return body


def make(n_dp, n_ctx):
    def on_device(
        layer_input, query_weight, key_weight, value_weight, out_weight, attn_gain, router_weight,
        moe_gain, gate_weight, up_weight, down_weight, expert_ids, fill_order, block_deal,
        seq_lengths, out_grad,
    ):
        rows, wide = layer_input.shape
        local = gate_weight.shape[0]
        width = wide // n_dp
        me_dp = lax.axis_index("dp").astype(jnp.int32)
        me_ctx = lax.axis_index("ctx").astype(jnp.int32)
        me = me_dp.reshape(1)
        near = rows // BLOCK

        pairs = n_ctx == 8 and local % 2 == 0
        served = local // 2 if pairs else local
        beside = xor_pairs(n_ctx, 1)
        column = me_ctx & 1 if pairs else jnp.zeros((), jnp.int32)
        grad_low = out_grad.astype(BF16)
        grad_beside = lax.ppermute(grad_low, "ctx", beside) if pairs else None
        wkv = dp_gather(jnp.concatenate([key_weight, value_weight], axis=1), n_dp)
        small = jnp.concatenate(
            [
                router_weight.T,
                attn_gain[None, :],
                moe_gain[None, :],
                jnp.zeros((14, width), BF16),
            ],
            axis=0,
        )
        small = in_order(dp_gather(small, n_dp), me_dp)
        small = small.transpose(1, 0, 2).reshape(EXPERTS + 16, wide)
        router_t = small[:EXPERTS]
        gain_one = small[EXPERTS : EXPERTS + 1].astype(F32)
        gain_two = small[EXPERTS + 1 : EXPERTS + 2].astype(F32)
        wq = dp_gather(query_weight, n_dp)

        deal, lengths = block_deal[0], seq_lengths[0]
        blocks = deal.shape[0]
        ends = jnp.cumsum(lengths, dtype=jnp.int32)
        mine = lax.dynamic_slice_in_dim(deal, me_ctx * near, near)
        places = (mine[:, None] * BLOCK + jnp.arange(BLOCK, dtype=jnp.int32)[None, :]).reshape(rows, 1)
        starts = jnp.sum(
            jnp.where(places >= ends[None, :], lengths[None, :], 0), axis=1, keepdims=True, dtype=jnp.int32
        )
        relative = (places - starts).astype(F32)
        lane = jnp.arange(128, dtype=jnp.int32)
        inverse = 10000.0 ** (-(lane % 32).astype(F32) * (2.0 / HEAD))
        angles = relative * inverse[None, :]
        cosine = jnp.cos(angles)
        sine = jnp.sin(angles) * jnp.where(lane % 64 < 32, -1.0, 1.0)[None, :]
        block_starts = jnp.sum(
            jnp.where((mine * BLOCK)[:, None] >= ends[None, :], lengths[None, :], 0), axis=1, dtype=jnp.int32
        )
        low_blocks = block_starts // BLOCK
        ring = jnp.array(ring_order(n_ctx)[0], jnp.int32)
        ring_deal = deal.reshape(n_ctx, near)[ring].reshape(blocks)
        held = jnp.arange(blocks, dtype=jnp.int32)
        where_block = jnp.sum(
            jnp.where(ring_deal[None, :] == held[:, None], held[None, :], 0), axis=1, dtype=jnp.int32
        )

        kv_mine, act_one = call(
            kv_body(n_dp),
            [me],
            [tie(layer_input, [grad_beside] if pairs else []), gain_one, cosine, sine] + wkv,
            [((rows, 2 * KVD), BF16), ((n_dp, rows, width), BF16)],
        )
        every_kv = ring_gather(kv_mine, n_ctx)
        (query,) = call(query_body(n_dp), [me], [act_one, cosine, sine] + wq, [((rows, wide), BF16)])
        wo = dp_gather(out_weight, n_dp)

        def reach(block):
            pieces = dp_gather(block, n_dp)
            if pairs:
                pieces = pieces + dp_gather(lax.ppermute(block, "ctx", beside), n_dp)
            return pieces

        table = jnp.concatenate([expert_ids.T, fill_order], axis=0)
        table = jnp.stack(reach(table))
        ids, fill = table[:, :-1], table[:, -1]
        held_blocks = table.shape[0]
        names = jnp.arange(EXPERTS, dtype=jnp.int32)
        hits = jnp.sum((ids[:, :, None, :] == names[None, None, :, None]).astype(F32), axis=1)
        earlier = (fill[:, :, None] < fill[:, None, :]).astype(BF16)
        prior = jnp.einsum(
            "set,stu->seu", hits.astype(BF16), earlier, preferred_element_type=F32
        )
        slot = jnp.where((hits > 0) & (prior < CAP), prior, -1.0).astype(jnp.int32)
        base = column * served
        slot = lax.dynamic_slice_in_dim(slot, me_dp * local + base, served, axis=1)
        slots_t = slot.transpose(1, 0, 2).reshape(served, 1, held_blocks * rows)
        hits_t = hits.transpose(1, 0, 2).reshape(EXPERTS, held_blocks * rows)
        grads_all = dp_gather(grad_low, n_dp)
        if pairs:
            grads_all = grads_all + dp_gather(grad_beside, n_dp)
        query, grads_all, wo = lax.optimization_barrier((query, grads_all, wo))

        attended, extended = call(
            attend_body,
            [low_blocks, mine, where_block],
            [query, every_kv, starts],
            [((rows, wide), BF16), ((PAIRS, 4, rows, 128), F32)],
            [
                pltpu.VMEM((PAIRS, 4 * BLOCK, 128), BF16),
                pltpu.VMEM((PAIRS, 4 * BLOCK, 128), F32),
                pltpu.VMEM((PAIRS, 4 * BLOCK, 128), F32),
                pltpu.VMEM((PAIRS, 4 * BLOCK, 128), F32),
            ],
            flops=rows * blocks * BLOCK * wide * 4,
        )
        mixed, act_two = call(
            mix_body(n_dp),
            [me],
            [layer_input, attended, gain_two] + wo,
            [((rows, wide), F32), ((rows, wide), BF16)],
            [pltpu.VMEM((n_dp, rows, width), BF16)],
        )

        acts_all = reach(act_two)
        groups = [(0, 1), (1, served - 1)] if pairs else [(0, served)]
        results = []
        line = LineSums(me_ctx, beside, served) if pairs else None

        def step(*after):
            if pairs:
                line.step(after)

        def hold(value, step):
            return line.hold(value, step) if pairs else value

        for first, number in groups:
            at = jnp.stack([base + first, me_dp * local + base + first])
            results.append(
                expert_call(
                    held_blocks, rows, local, served, first, number, gate_weight.shape[1:]
                )(
                    at, *acts_all, *grads_all, slots_t, hits_t, router_t, gate_weight, up_weight,
                    down_weight,
                )
            )
            if pairs:
                line.feed(results[-1])
            step(*[res[4] for res in results[1:]])
        gates = results[0][3]

        def combine(index, after):
            return call(
                combine_body(held_blocks, rows, groups),
                [],
                [tie(slots_t, after)] + [res[index] for res in results],
                [((rows, wide), BF16)] * held_blocks,
            )

        def settle(parts, between):
            kept = [dp_cores(parts[s : s + n_dp], n_dp) for s in range(0, held_blocks, n_dp)]
            between(kept)
            totals = [dp_rest(k, n_dp) for k in kept]
            between(totals)
            if pairs:
                totals[0] = totals[0] + lax.ppermute(
                    totals[1].astype(BF16), "ctx", beside
                ).astype(F32)
            return totals[0]

        dgates = jnp.concatenate([res[4] for res in results], axis=0)[:, 0]
        back = [dgates[:, s * rows : (s + 1) * rows] for s in range(held_blocks)]
        if pairs:
            other = lax.ppermute(jnp.stack(back[n_dp:]), "ctx", beside)
            own = jnp.stack(back[:n_dp])
            back = jnp.where(
                column == 0,
                jnp.concatenate([own, other], axis=1),
                jnp.concatenate([other, own], axis=1),
            )
        back = [back[0]] + [lax.ppermute(back[s], "dp", xor_pairs(n_dp, s)) for s in range(1, n_dp)]
        dgate_t = in_order(back, me_dp).reshape(EXPERTS, rows)
        g_parts = combine(6, line.marks[:1] if pairs else [])
        grad_act_two = settle(g_parts, lambda values: None)
        step(grad_act_two)
        res = call(
            after_body(n_dp),
            [me],
            [mixed, hold(grad_act_two, 1), out_grad, gain_two, gates, dgate_t, router_t, act_two, attended] + wo,
            [((rows, wide), F32), ((rows, wide), BF16), ((EXPERTS, wide), F32), ((1, wide), F32)]
            + [((width, wide), BF16)] * n_dp,
            [pltpu.VMEM((n_dp, rows, width), BF16), pltpu.VMEM((n_dp, rows, width), BF16)],
        )
        grad_mixed, grad_heads, router_part, gain_two_part = res[:4]
        out_parts = res[4:]
        grad_query, kv_grads = call(
            attend_back_body,
            [low_blocks, mine, where_block],
            [query, every_kv, starts, grad_heads, extended, cosine, sine],
            [((rows, wide), BF16), ((blocks * BLOCK, 2 * KVD), BF16)],
            [
                pltpu.VMEM((PAIRS, 4 * BLOCK, 128), BF16),
                pltpu.VMEM((PAIRS, 4 * BLOCK, 128), BF16),
                pltpu.VMEM((PAIRS, 4 * BLOCK, 128), F32),
                pltpu.VMEM((PAIRS, 4 * BLOCK, 128), F32),
                pltpu.VMEM((PAIRS, 4 * BLOCK, 128), F32),
                pltpu.VMEM((blocks * BLOCK, 2 * KVD), F32),
            ],
            flops=rows * blocks * BLOCK * wide * 10,
        )
        step(grad_query)
        kv_grad = ring_scatter(hold(kv_grads, 2), n_ctx)
        y_parts = combine(5, [grad_query])
        y_total = settle(y_parts, lambda values: None)
        dense_out = dp_reduce(out_parts, n_dp).astype(BF16)
        layer_output = mixed + y_total
        step(layer_output)
        res = call(
            first_body(n_dp),
            [me],
            [layer_input, gain_one, cosine, sine, act_one, grad_query, kv_grad, grad_mixed] + wq + wkv,
            [((rows, wide), F32), ((1, wide), F32)]
            + [((width, wide), BF16)] * n_dp
            + [((width, 2 * KVD), BF16)] * n_dp,
            [pltpu.VMEM((rows, 2 * KVD), BF16), pltpu.VMEM((n_dp, rows, width), F32)],
        )
        input_grad, gain_one_part = res[:2]
        q_parts, kv_parts = res[2 : 2 + n_dp], res[2 + n_dp :]
        step(gain_one_part)

        dense_q = dp_reduce(q_parts, n_dp).astype(BF16)
        dense_kv = dp_reduce(kv_parts, n_dp).astype(BF16)
        dense = jnp.concatenate([dense_out, dense_q, dense_kv], axis=0)
        dense = ring_gather(ring_scatter(dense, n_ctx), n_ctx).astype(F32)
        tiny = jnp.concatenate([router_part, gain_one_part, gain_two_part], axis=0)
        for bit in [1 << b for b in range(n_dp.bit_length() - 1)]:
            tiny = tiny + lax.ppermute(tiny, "dp", xor_pairs(n_dp, bit))
        tiny = lax.dynamic_slice_in_dim(tiny, me_dp * width, width, axis=1)
        for bit in [1 << b for b in range(n_ctx.bit_length() - 1)]:
            tiny = tiny + lax.ppermute(tiny, "ctx", xor_pairs(n_ctx, bit))
        if pairs:
            while len(line.marks) < len(line.blocks) + line.LAG:
                line.step()
            expert_sums = line.finish()
        else:
            expert_sums = [
                ring_gather(ring_scatter(g.reshape(-1, g.shape[2]), n_ctx), n_ctx)
                .reshape(g.shape)
                .astype(F32)
                for g in results[0][:3]
            ]
        return (
            layer_output,
            input_grad,
            dense[width : 2 * width],
            dense[2 * width :, :KVD],
            dense[2 * width :, KVD:],
            dense[:width],
            tiny[EXPERTS],
            tiny[:EXPERTS].T,
            tiny[EXPERTS + 1],
            expert_sums[0],
            expert_sums[1],
            expert_sums[2],
        )

    return on_device


def solution(mesh):
    rows2 = P(("dp", "ctx"), None)
    mat = P("dp", None)
    cube = P("dp", None, None)
    in_specs = (
        rows2, mat, mat, mat, mat, P("dp"), mat, P("dp"), cube, cube, cube, rows2, rows2, mat, mat, rows2,
    )
    out_specs = (rows2, rows2, mat, mat, mat, mat, P("dp"), mat, P("dp"), cube, cube, cube)
    return jax.shard_map(
        make(mesh.shape["dp"], mesh.shape["ctx"]),
        mesh=mesh,
        in_specs=in_specs,
        out_specs=out_specs,
        check_vma=False,
    )
```
